32 devices in a mesh: dp: 4 (over x, core), rows: 8 (over z, y).
Axes of the slice: x: 2, y: 2, z: 4, core: 2. Of those that a mesh axis runs over, the one named last changes fastest.
Arguments:
- images: bfloat16 [8, 64, 64, 768], P('dp', 'rows'), may hold values from -6 to 6
- norm1_gain: float32 [768], replicated, may hold values from 0.1 to 1.9
- norm1_bias: float32 [768], replicated, may hold values from -2 to 2
- qkv_weight: bfloat16 [768, 2304], P('dp', 'rows'), may hold values from -0.21875 to 0.21875
- qkv_bias: float32 [2304], replicated, may hold values from -2 to 2
- height_table: bfloat16 [27, 64], replicated, may hold values from -1 to 1
- width_table: bfloat16 [27, 64], replicated, may hold values from -1 to 1
- proj_weight: bfloat16 [768, 768], P('dp', 'rows'), may hold values from -0.875 to 0.875
- proj_bias: float32 [768], replicated, may hold values from -2 to 2
- norm2_gain: float32 [768], replicated, may hold values from 0.1 to 1.9
- norm2_bias: float32 [768], replicated, may hold values from -2 to 2
- expand_weight: bfloat16 [768, 3072], P('dp', 'rows'), may hold values from -0.21875 to 0.21875
- expand_bias: float32 [3072], replicated, may hold values from -2 to 2
- contract_weight: bfloat16 [3072, 768], P('dp', 'rows'), may hold values from -0.109375 to 0.109375
- contract_bias: float32 [768], replicated, may hold values from -2 to 2
- adapter_index: int32 [8, 1], P('dp'), may hold values from 0 to 7
- qkv_down: bfloat16 [8, 16, 768], P('dp', None, 'rows'), may hold values from -0.21875 to 0.21875
- qkv_up: bfloat16 [8, 16, 2304], P('dp', None, 'rows'), may hold values from -0.75 to 0.75
- proj_down: bfloat16 [8, 16, 768], P('dp', None, 'rows'), may hold values from -0.21875 to 0.21875
- proj_up: bfloat16 [8, 16, 768], P('dp', None, 'rows'), may hold values from -1.5 to 1.5
- expand_down: bfloat16 [8, 16, 768], P('dp', None, 'rows'), may hold values from -0.21875 to 0.21875
- expand_up: bfloat16 [8, 16, 3072], P('dp', None, 'rows'), may hold values from -0.75 to 0.75
- contract_down: bfloat16 [8, 16, 3072], P('dp', None, 'rows'), may hold values from -0.109375 to 0.109375
- contract_up: bfloat16 [8, 16, 768], P('dp', None, 'rows'), may hold values from -0.75 to 0.75
- cotangent: bfloat16 [8, 64, 64, 768], P('dp', 'rows'), may hold values from -6 to 6
Outputs:
- block_out: bfloat16 [8, 64, 64, 768], P('dp', 'rows')
- input_grad: float32 [8, 64, 64, 768], P('dp', 'rows')
- qkv_down_grad: float32 [8, 16, 768], P('dp', None, 'rows')
- qkv_up_grad: float32 [8, 16, 2304], P('dp', None, 'rows')
- proj_down_grad: float32 [8, 16, 768], P('dp', None, 'rows')
- proj_up_grad: float32 [8, 16, 768], P('dp', None, 'rows')
- expand_down_grad: float32 [8, 16, 768], P('dp', None, 'rows')
- expand_up_grad: float32 [8, 16, 3072], P('dp', None, 'rows')
- contract_down_grad: float32 [8, 16, 3072], P('dp', None, 'rows')
- contract_up_grad: float32 [8, 16, 768], P('dp', None, 'rows')
The draws below stay inside these ranges and needn't reach their ends.
Inputs may be any that keep to these rules, and one draw needn't show every extreme that they name: `adapter_index`: each image's adapter, one of 8.
All inputs are finite; a program needn't handle non-finite values.
Results may differ from the reference program's by a relative error of at most 0.018.
Values may be sent and summed in bfloat16 or wider, within the bound.
No kernel may reach another device: no remote copies, remote signals or barrier semaphores. Data moves between devices by JAX's collectives and lax.ppermute only.
A program may use at most 384 MiB of HBM per device.

```python
import jax
import jax.numpy as jnp
from jax import lax

D = 768
HEADS = 12
HEAD_DIM = 64
FF = 3072
WIN = 14
SIDE = 64
RANK = 16
ADAPTERS = 8
IMAGES = 8
GRID = 5
PADDED = 70
RELS = 27


def with_ends(result, key, low, top_value):
    longest = result.shape.index(max(result.shape))
    spots = []
    for shift in (0, 1):
        where = [jax.random.randint(jax.random.fold_in(key, axis), (), 0, length) for axis, length in enumerate(result.shape)]
        where[longest] = (where[longest] + shift) % result.shape[longest]
        spots.append(tuple(where))
    return result.at[spots[0]].set(low).at[spots[1]].set(top_value)


def spiked(entries, rng, source, target, parts, factor):
    owner, partner = [(jnp.arange(entries.shape[axis_at]) // (entries.shape[axis_at] // parts)).reshape([-1 if axis == axis_at else 1 for axis in range(entries.ndim)]) for axis_at in (source, target)]
    chosen = jax.random.permutation(rng, parts)[partner]
    strong = (owner == chosen) | (owner == (partner + parts // 2) % parts)
    return jnp.where(strong, factor * entries, entries)


def steps_of(rng, dims, pieces, smallest, largest):
    gain = 1.0
    for dim, parts in pieces:
        draws = jax.random.uniform(jax.random.fold_in(jax.random.fold_in(rng, 6), dim), (parts,), jnp.float32, smallest / len(pieces), largest / len(pieces))
        gain = gain * jnp.repeat(jnp.exp(draws), dims[dim] // parts).reshape((-1,) + (1,) * (len(dims) - 1 - dim))
    return gain


def gaussian(own_key, shape, scale, reach, cuts=(), kind=jnp.bfloat16):
    result = scale * jax.random.normal(own_key, shape, jnp.float32)
    if cuts:
        result = result * steps_of(own_key, shape, cuts, -0.22, 0.18)
    return jnp.clip(result, -reach, reach).astype(kind)


def noise_with(key, shape, scale, most, shards, heavy, kind=jnp.bfloat16):
    entries = scale * jax.random.normal(key, shape, jnp.float32)
    if shards:
        entries = entries * steps_of(key, shape, shards, -0.22, 0.18)
    return jnp.clip(spiked(entries, jax.random.fold_in(key, 3), *heavy), -most, most).astype(kind)


def setup_inputs(seed: int = 0) -> dict:
    arg_keys = jax.random.split(jax.random.key(seed), 26)
    return {
        "images": gaussian(arg_keys[0], (IMAGES, SIDE, SIDE, D), 1.0, 6.0, ((0, 4), (1, 8))),
        "norm1_gain": jnp.clip(1.0 + 0.18 * jax.random.normal(arg_keys[1], (D,), jnp.float32), 0.1, 1.9),
        "norm1_bias": gaussian(arg_keys[2], (D,), 0.3, 2.0, (), jnp.float32),
        "qkv_weight": gaussian(arg_keys[3], (D, 3 * D), D ** -0.5, 0.21875, ((0, 4), (1, 8))),
        "qkv_bias": gaussian(arg_keys[4], (3 * D,), 0.3, 2.0, (), jnp.float32),
        "height_table": gaussian(arg_keys[5], (RELS, HEAD_DIM), 0.15, 1.0),
        "width_table": gaussian(arg_keys[6], (RELS, HEAD_DIM), 0.15, 1.0),
        "proj_weight": gaussian(arg_keys[7], (D, D), (D // 16) ** -0.5, 0.875, ((0, 4), (1, 8))),
        "proj_bias": gaussian(arg_keys[8], (D,), 0.3, 2.0, (), jnp.float32),
        "norm2_gain": jnp.clip(1.0 + 0.18 * jax.random.normal(arg_keys[9], (D,), jnp.float32), 0.1, 1.9),
        "norm2_bias": gaussian(arg_keys[10], (D,), 0.3, 2.0, (), jnp.float32),
        "expand_weight": gaussian(arg_keys[11], (D, FF), D ** -0.5, 0.21875, ((0, 4), (1, 8))),
        "expand_bias": gaussian(arg_keys[12], (FF,), 0.3, 2.0, (), jnp.float32),
        "contract_weight": gaussian(arg_keys[13], (FF, D), FF ** -0.5, 0.109375, ((0, 4), (1, 8))),
        "contract_bias": gaussian(arg_keys[14], (D,), 0.3, 2.0, (), jnp.float32),
        "adapter_index": with_ends(jax.random.randint(arg_keys[15], (IMAGES, 1), 0, ADAPTERS), jax.random.fold_in(arg_keys[15], 1), 0, ADAPTERS - 1).astype(jnp.int32),
        "qkv_down": gaussian(arg_keys[16], (ADAPTERS, RANK, D), D ** -0.5, 0.21875, ((0, 4), (2, 8))),
        "qkv_up": gaussian(arg_keys[17], (ADAPTERS, RANK, 3 * D), (4 * RANK) ** -0.5, 0.75, ((0, 4), (2, 8))),
        "proj_down": gaussian(arg_keys[18], (ADAPTERS, RANK, D), D ** -0.5, 0.21875, ((0, 4), (2, 8))),
        "proj_up": gaussian(arg_keys[19], (ADAPTERS, RANK, D), RANK ** -0.5, 1.5, ((0, 4), (2, 8))),
        "expand_down": gaussian(arg_keys[20], (ADAPTERS, RANK, D), D ** -0.5, 0.21875, ((0, 4), (2, 8))),
        "expand_up": gaussian(arg_keys[21], (ADAPTERS, RANK, FF), (4 * RANK) ** -0.5, 0.75, ((0, 4), (2, 8))),
        "contract_down": gaussian(arg_keys[22], (ADAPTERS, RANK, FF), FF ** -0.5, 0.109375, ((0, 4), (2, 8))),
        "contract_up": gaussian(arg_keys[23], (ADAPTERS, RANK, D), (4 * RANK) ** -0.5, 0.75, ((0, 4), (2, 8))),
        "cotangent": noise_with(arg_keys[24], (IMAGES, SIDE, SIDE, D), 1.0, 6.0, ((0, 4), (1, 8)), (1, 3, 8, 2.0)),
    }


@jax.custom_vjp
def low(v):
    return lax.optimization_barrier(v.astype(jnp.bfloat16)).astype(jnp.float32)

@jax.custom_vjp
def low_back(v):
    return v

def low_keep(v):
    return (low(v), None)

def low_pass(kept, grad):
    return (grad,)

def back_keep(v):
    return (v, None)

def back_low(kept, grad):
    return (low(grad),)
low.defvjp(low_keep, low_pass)
low_back.defvjp(back_keep, back_low)
EPSILON = 1e-06
HIGHEST_PRECISION = lax.Precision.HIGHEST

def product(first_operand, second_operand):
    return jnp.dot(first_operand, second_operand, precision=HIGHEST_PRECISION)

def layer_norm(values, norm_gain, norm_bias):
    average = lax.optimization_barrier(jnp.mean(values, axis=-1, keepdims=True))
    centred = values - average
    variance = lax.optimization_barrier(jnp.mean(centred * centred, axis=-1, keepdims=True))
    return centred * lax.rsqrt(variance + EPSILON) * norm_gain + norm_bias

def adapter(inputs, down_matrix, up_matrix):
    inner_rank = low(low_back(product(inputs, down_matrix.T)))
    return product(inner_rank, up_matrix)

def relative_table(table):
    offsets = jnp.arange(WIN)[:, None] - jnp.arange(WIN)[None, :] + WIN - 1
    return table[offsets]

def window_attention(normed, qkv_weight, qkv_bias, height_table, width_table, down_matrix, up_matrix):
    window_total = GRID * GRID
    padded = jnp.pad(normed, ((0, PADDED - SIDE), (0, PADDED - SIDE), (0, 0)))
    windows = padded.reshape(GRID, WIN, GRID, WIN, D).transpose(0, 2, 1, 3, 4).reshape(window_total, WIN * WIN, D)
    mixed = product(windows, qkv_weight) + qkv_bias + adapter(windows, down_matrix, up_matrix)
    mixed = low(low_back(mixed))
    split_up = mixed.reshape(window_total, WIN * WIN, 3, HEADS, HEAD_DIM)
    queries = split_up[:, :, 0]
    keys_all = split_up[:, :, 1]
    values_all = split_up[:, :, 2]
    scale_factor = HEAD_DIM ** (-0.5)
    scores = jnp.einsum('bqhc,bkhc->bhqk', queries, keys_all, precision=HIGHEST_PRECISION) * scale_factor
    shaped = queries.reshape(window_total, WIN, WIN, HEADS, HEAD_DIM)
    along_height = jnp.einsum('bxyhc,xkc->bhxyk', shaped, relative_table(height_table), precision=HIGHEST_PRECISION)
    along_width = jnp.einsum('bxyhc,ykc->bhxyk', shaped, relative_table(width_table), precision=HIGHEST_PRECISION)
    scores = scores.reshape(window_total, HEADS, WIN, WIN, WIN, WIN) + along_height[..., :, None] + along_width[..., None, :]
    scores = low_back(scores.reshape(window_total, HEADS, WIN * WIN, WIN * WIN))
    soft_low = low(jax.nn.softmax(scores, axis=-1))
    attended = jnp.einsum('bhqk,bkhc->bqhc', soft_low, values_all, precision=HIGHEST_PRECISION)
    attended = low(low_back(attended.reshape(window_total, WIN * WIN, D)))
    attended = attended.reshape(GRID, GRID, WIN, WIN, D).transpose(0, 2, 1, 3, 4).reshape(PADDED, PADDED, D)
    return attended[:SIDE, :SIDE]

def block_forward(picture, weights, chosen):
    norm1_gain, norm1_bias, qkv_weight, qkv_bias, height_table, width_table, proj_weight, proj_bias, norm2_gain, norm2_bias, expand_weight, expand_bias, contract_weight, contract_bias = weights
    normed = low(low_back(layer_norm(picture, norm1_gain, norm1_bias)))
    attended = window_attention(normed, qkv_weight, qkv_bias, height_table, width_table, chosen[0], chosen[1])
    branch = low_back(product(attended, proj_weight) + proj_bias + adapter(attended, chosen[2], chosen[3]))
    middle = picture + branch
    second = low(layer_norm(middle, norm2_gain, norm2_bias))
    hidden = low_back(product(second, expand_weight) + expand_bias + adapter(second, chosen[4], chosen[5]))
    active = low(jax.nn.gelu(hidden, approximate=False))
    return middle + product(active, contract_weight) + contract_bias + adapter(active, chosen[6], chosen[7])

def selected_forward(picture, weights, selector, adapters_in):
    chosen = tuple((jnp.einsum('e,erc->rc', selector, matrix, precision=HIGHEST_PRECISION) for matrix in adapters_in))
    return block_forward(picture, weights, chosen)

def reference(images, norm1_gain, norm1_bias, qkv_weight, qkv_bias, height_table, width_table, proj_weight, proj_bias, norm2_gain, norm2_bias, expand_weight, expand_bias, contract_weight, contract_bias, adapter_index, qkv_down, qkv_up, proj_down, proj_up, expand_down, expand_up, contract_down, contract_up, cotangent):
    weights = tuple((matrix.astype(jnp.float32) for matrix in (norm1_gain, norm1_bias, qkv_weight, qkv_bias, height_table, width_table, proj_weight, proj_bias, norm2_gain, norm2_bias, expand_weight, expand_bias, contract_weight, contract_bias)))
    adapters = tuple((matrix.astype(jnp.float32) for matrix in (qkv_down, qkv_up, proj_down, proj_up, expand_down, expand_up, contract_down, contract_up)))

    def per_image(totals, inputs):
        picture, index_row, cotangent_image = inputs
        selector = (jnp.arange(ADAPTERS, dtype=jnp.int32) == index_row[0]).astype(jnp.float32)
        outputs, pullback = jax.vjp(lambda picture_in, adapters_in: selected_forward(picture_in, weights, selector, adapters_in), picture, adapters)
        picture_grad, adapters_grad = pullback(cotangent_image)
        totals = tuple((running + portion for running, portion in zip(totals, adapters_grad)))
        return (totals, (outputs.astype(jnp.bfloat16), picture_grad))
    initial = tuple((jnp.zeros(matrix.shape, jnp.float32) for matrix in adapters))
    totals, stacked = lax.scan(per_image, initial, (images.astype(jnp.float32), adapter_index, cotangent.astype(jnp.float32)))
    return (stacked[0], stacked[1], totals[0], totals[1], totals[2], totals[3], totals[4], totals[5], totals[6], totals[7])
```

```python
import itertools

import jax
import jax.numpy as jnp
import numpy as np
from jax import lax
from jax.experimental import pallas as pl
from jax.experimental.pallas import tpu as pltpu
from jax.sharding import PartitionSpec as P

HEAD_DIM = 64
WIN = 14
PITCH = 16
ADAPTERS = 8
RANK = 16
GRID = 5
D = 768
FF = 3072
HEADS = 12
PAIRS = HEADS // 2
TOK = WIN * PITCH
KEYS = 256
EPSILON = 1e-06
SQRT_HALF = 0.7071067811865476
INV_SQRT_TAU = 0.3989422804014327
SHIFT = 1024
SHORT = 8
CUT = SHORT * PITCH
BF = jnp.bfloat16
F32 = jnp.float32
VMEM_LIMIT = 60 * 1024 * 1024


def choose_owner(ranks, row_count, images):
    side_rows = ranks * row_count
    total = GRID * GRID * images
    weight = np.array(
        [0.77 if side_rows - (w // (GRID * images)) * WIN <= SHORT else 1.0 for w in range(total)]
    )

    def owner_of(cuts):
        return np.repeat(np.arange(ranks), np.diff([0] + list(cuts) + [total]))

    def cost_of(cuts):
        if min(np.diff([0] + list(cuts) + [total])) < 0:
            return 1e9
        owner = owner_of(cuts)
        load = np.bincount(owner, weights=weight, minlength=ranks).max()
        return 12.0 * load + color_edges(owner, ranks, row_count, images)[0]

    def filled(limit):
        cuts, load = [], 0.0
        for window in range(total):
            if load + weight[window] > limit + 1e-9:
                cuts.append(window)
                load = 0.0
            load += weight[window]
        return cuts + [total] * (ranks - 1 - len(cuts))

    limits = sorted({weight[a:b].sum() for a in range(total) for b in range(a + 1, total + 1)})
    least = next(limit for limit in limits if len(filled(limit)) == ranks - 1)
    reach = np.cumsum(weight) / weight.sum() * ranks
    even = [int(np.searchsorted(reach, r - 0.5)) for r in range(1, ranks)]
    found = (1e10, None)
    for cuts in (filled(least), even):
        best = cost_of(cuts)
        for _ in range(12):
            moved = False
            for place in range(ranks - 1):
                for width in (1, 2, 3):
                    for step in (-1, 1):
                        trial = list(cuts)
                        for extra in range(width):
                            if place + extra < ranks - 1:
                                trial[place + extra] += step
                        cost = cost_of(trial)
                        if cost < best - 1e-9:
                            best, cuts, moved = cost, trial, True
            if not moved:
                break
        if best < found[0] - 1e-9:
            found = (best, list(cuts))
    return owner_of(found[1])


def color_edges(owner, ranks, row_count, images):
    edges = {}
    local = [[] for _ in range(ranks)]
    for rank in range(ranks):
        for img in range(images):
            for k in range(row_count):
                row = rank * row_count + k
                for col in range(GRID):
                    window = (row // WIN) * images * GRID + img * GRID + col
                    unit = (img, k, col, window, row % WIN)
                    if owner[window] == rank:
                        local[rank].append(unit)
                    else:
                        edges.setdefault((rank, int(owner[window])), []).append(unit)
    colors = []
    for (src, dst), units in sorted(edges.items(), key=lambda e: (-len(e[1]), e[0])):
        for color in colors:
            if src not in color["src"] and dst not in color["dst"]:
                break
        else:
            color = {"src": set(), "dst": set(), "pairs": [], "units": []}
            colors.append(color)
        color["src"].add(src)
        color["dst"].add(dst)
        color["pairs"].append((src, dst))
        color["units"].append(units)
    sizes = [max(len(u) for u in c["units"]) for c in colors]
    cost = 0.4 * sum(sizes) + 3.0 * len(sizes)
    return cost, local, colors, sizes


def make_plan(ranks, row_count, images):
    total = GRID * GRID * images
    owner = choose_owner(ranks, row_count, images)
    _, local, colors, sizes = color_edges(owner, ranks, row_count, images)
    kinds = [ranks * row_count - w // (images * GRID) * WIN <= SHORT for w in range(total)]
    heights = [SHORT if short else WIN for short in kinds]
    most = int(np.bincount(owner, weights=heights, minlength=ranks).max())
    full_most = int(np.bincount(owner, weights=~np.array(kinds), minlength=ranks).max())
    short_most = int(np.bincount(owner, weights=np.array(kinds), minlength=ranks).max())
    skip = (len(colors) + 1) * SHIFT
    rows_code = np.full((ranks, images, row_count, GRID), skip, np.int32)
    win_code = np.full((ranks, most), skip, np.int32)
    first = np.searchsorted(owner, np.arange(ranks))

    def put(rank, unit, code, dst):
        img, k, col, window, place = unit
        rows_code[rank, img, k, col] = code
        win_code[dst, sum(heights[first[dst] : window]) + place] = code

    for rank in range(ranks):
        for number, unit in enumerate(local[rank]):
            put(rank, unit, number, rank)
    for which, color in enumerate(colors):
        for (src, dst), units in zip(color["pairs"], color["units"]):
            for number, unit in enumerate(units):
                put(src, unit, (which + 1) * SHIFT + number, dst)
    slot_info = np.zeros((ranks, 3), np.int32)
    for rank in range(ranks):
        mine = [kinds[w] for w in np.flatnonzero(owner == rank)]
        slot_info[rank] = (mine.count(False), mine.count(True),
                           sum(SHORT if short else WIN for short in mine))
    return {
        "rows": rows_code.reshape(ranks, -1),
        "wins": win_code,
        "info": slot_info,
        "units": most,
        "full": full_most,
        "short": short_most,
        "local": max(max(len(u) for u in local), 1),
        "sizes": sizes,
        "pairs": [c["pairs"] for c in colors],
    }


def place_matrix(side):
    out = np.zeros((GRID * PITCH, side), np.float32)
    for token in range(side):
        out[token // WIN * PITCH + token % WIN, token] = 1.0
    return out


def key_marks():
    fwd = np.zeros((2 * KEYS, 128), np.float32)
    bwd = np.zeros((2 * KEYS, 128), np.float32)
    for head in range(2):
        for key in range(KEYS):
            row = head * KEYS + key
            u, w = divmod(key, PITCH)
            if key >= TOK or w >= WIN:
                fwd[row, 14] = -1e30
                continue
            base = 64 * head
            for lane in (base + u, base + 32 + w):
                fwd[row, lane] = 1.0
            bwd[row, base + 13 - u] = 1.0
            bwd[row, base + 32 + 13 - w] = 1.0
    return fwd, bwd


def pair_tables(height_table, width_table):
    rev = jnp.pad(jnp.stack((height_table[::-1], width_table[::-1])), ((0, 0), (2, 3), (0, 0)))
    half = rev.reshape(64, HEAD_DIM).T
    zero = jnp.zeros_like(half)
    fwd = jnp.concatenate(
        (jnp.concatenate((half, zero), 1), jnp.concatenate((zero, half), 1)), 0
    )
    straight = jnp.pad(jnp.stack((height_table, width_table)), ((0, 0), (0, 5), (0, 0)))
    back = straight.reshape(64, HEAD_DIM)
    blank = jnp.zeros_like(back)
    bwd = jnp.concatenate(
        (jnp.concatenate((back, blank), 1), jnp.concatenate((blank, back), 1)), 0
    )
    return fwd, bwd


def nn(a, b):
    return lax.dot_general(a, b, (((1,), (0,)), ((), ())), preferred_element_type=F32)


def nt(a, b):
    return lax.dot_general(a, b, (((1,), (1,)), ((), ())), preferred_element_type=F32)


def tn(a, b):
    return lax.dot_general(a, b, (((0,), (0,)), ((), ())), preferred_element_type=F32)


def start_in(codes, count, bufs, dst, sem):
    def body(u, carry):
        code = codes[u]
        which = code // SHIFT
        index = code % SHIFT
        for number, buf in enumerate(bufs):
            @pl.when(which == number)
            def _():
                pltpu.make_async_copy(buf.at[index], dst.at[u], sem).start()
        return carry

    lax.fori_loop(0, count, body, 0)


def start_out(codes, first, count, src, bufs, spare, sem):
    def body(u, carry):
        code = codes[u]
        which = code // SHIFT
        index = code % SHIFT
        for number, buf in enumerate(bufs):
            @pl.when(which == number)
            def _():
                pltpu.make_async_copy(src.at[u], buf.at[index], sem).start()

        if spare is not None:
            @pl.when(which >= len(bufs))
            def _():
                pltpu.make_async_copy(src.at[u], bufs[0].at[spare + u], sem).start()
        return carry

    lax.fori_loop(first, first + count, body, 0)


def wait_all(whole, sem):
    pltpu.make_async_copy(whole, whole, sem).wait()


def norm_parts(values):
    average = jnp.mean(values, axis=-1, keepdims=True)
    centred = values - average
    variance = jnp.mean(centred * centred, axis=-1, keepdims=True)
    inverse = lax.rsqrt(variance + EPSILON)
    return centred * inverse, inverse


def norm_back(upstream, standard, inverse, gain):
    scaled = upstream * gain
    first_term = jnp.mean(scaled, axis=-1, keepdims=True)
    second_term = jnp.mean(scaled * standard, axis=-1, keepdims=True)
    return inverse * (scaled - first_term - standard * second_term)


def any_specs(count):
    return [pl.BlockSpec(memory_space=pl.ANY)] * count


def full_spec(shape):
    return pl.BlockSpec(shape, lambda *_: (0,) * len(shape))


def unit_shapes(plan):
    counts = [plan["local"] + plan["units"]] + plan["sizes"]
    return [jax.ShapeDtypeStruct((n, PITCH, D), BF) for n in counts]


def after(value, *others):
    return lax.optimization_barrier((value, *others))[0]


def exchange(bufs, plan, back):
    moved = [bufs[0]]
    for buf, pairs in zip(bufs[1:], plan["pairs"]):
        pairs = [(b, a) for a, b in pairs] if back else list(pairs)
        moved.append(lax.ppermute(buf, "rows", pairs))
    return moved


def cost(flops, moved, special=0):
    return pl.CostEstimate(flops=int(flops), bytes_accessed=int(moved), transcendentals=int(special))


def params():
    return pltpu.CompilerParams(vmem_limit_bytes=VMEM_LIMIT)


def rows_plan(images, row_count, rows_block, number):
    side = images.shape[1]
    steps = row_count // rows_block
    spec = pl.BlockSpec((rows_block, side, D), lambda i, *_: (number * steps + i, 0, 0))
    return side, steps, spec


def first_norm(images, number, row_count, gain, bias, place, codes, plan, rows_block):
    side, steps, rows_spec = rows_plan(images, row_count, rows_block, number)
    per_step = rows_block * GRID
    outs = unit_shapes(plan)

    def kernel(codes_ref, x_ref, g_ref, b_ref, p_ref, *rest):
        bufs, scratch, sems = rest[: len(outs)], rest[len(outs)], rest[len(outs) + 1]
        step = pl.program_id(0)
        values = x_ref[...].reshape(rows_block * side, D).astype(F32)
        standard, _ = norm_parts(values)
        normed = (standard * g_ref[...] + b_ref[...]).astype(BF)
        for r in range(rows_block):
            spread = nn(p_ref[...], normed[r * side : (r + 1) * side])
            scratch[pl.ds(step * per_step + r * GRID, GRID)] = spread.astype(BF).reshape(
                GRID, PITCH, D
            )
        start_out(codes_ref, step * per_step, per_step, scratch, bufs, None, sems.at[0])

        @pl.when(step == steps - 1)
        def _():
            wait_all(scratch, sems.at[0])

    return pl.pallas_call(
        kernel,
        out_shape=outs,
        grid_spec=pltpu.PrefetchScalarGridSpec(
            num_scalar_prefetch=1,
            grid=(steps,),
            in_specs=[rows_spec, full_spec((1, D)), full_spec((1, D)), full_spec(place.shape)],
            out_specs=any_specs(len(outs)),
            scratch_shapes=[
                pltpu.VMEM((row_count * GRID, PITCH, D), BF),
                pltpu.SemaphoreType.DMA((1,)),
            ],
        ),
        cost_estimate=cost(1e9, 8e6),
        compiler_params=params(),
        name="first_norm",
    )(codes, images, gain, bias, place)


def image_spec(shape, number):
    return pl.BlockSpec((1,) + shape[1:], lambda *_: (number,) + (0,) * (len(shape) - 1))


def saved_shapes(plan):
    rows = plan["units"] * PITCH
    return [
        jax.ShapeDtypeStruct((rows, D), BF),
        jax.ShapeDtypeStruct((rows, 3 * D), BF),
        jax.ShapeDtypeStruct((rows, RANK), BF),
        jax.ShapeDtypeStruct((PAIRS, rows, 2 * KEYS), BF),
        jax.ShapeDtypeStruct((rows, D), F32),
        jax.ShapeDtypeStruct((rows, D), BF),
    ]


def each_slot(info_ref, plan, body):
    n_full = info_ref[0]
    if plan["full"]:
        def full(slot, carry):
            body(pl.multiple_of(slot * TOK, 32), TOK, slot)
            return carry

        lax.fori_loop(0, n_full, full, 0)
    if plan["short"]:
        def short(slot, carry):
            body(pl.multiple_of(n_full * TOK + slot * CUT, 32), CUT, n_full + slot)
            return carry

        lax.fori_loop(0, info_ref[1], short, 0)


def key_value(mixed_ref, bias_low, at, rows, j):
    out = []
    for part in (1, 2):
        cols = slice(part * D + 128 * j, part * D + 128 * j + 128)
        own = mixed_ref[pl.ds(at, rows), cols]
        if rows < TOK:
            rest = jnp.broadcast_to(bias_low[:, cols], (TOK - rows, 128))
            own = jnp.concatenate((own, rest), 0)
        out.append(own)
    return out[0] * jnp.asarray(HEAD_DIM ** -0.5, BF), out[1]


def fill_heads(ref, value, low_half):
    nil = jnp.zeros_like(value)
    ref[0:TOK, 0:128] = jnp.where(low_half, value, nil)
    ref[KEYS : KEYS + TOK, 0:128] = jnp.where(low_half, nil, value)


def attention_forward(units, zero, weight, qkv_bias, down, up, number, table, marks, codes, info,
                      plan):
    outs = unit_shapes(plan)
    n_buf = len(outs)
    n_units = plan["units"]
    n_rows = n_units * PITCH
    n_slots = plan["full"] + plan["short"]

    def kernel(codes_ref, info_ref, *refs):
        in_bufs = refs[: n_buf + 1]
        w_src, bias_ref, down_ref, up_ref, table_ref, marks_ref = refs[n_buf + 1 : n_buf + 7]
        refs = refs[n_buf + 7 :]
        out_bufs = refs[:n_buf]
        win_out, mixed_out, inner_out, prob_out, inv_out, att_out = refs[n_buf : n_buf + 6]
        (x_in, x_out, w_vmem, keys, vals, mixed_ref, inner_ref, prob_ref, inv_ref, in_sems,
         out_sems, w_sems, save_sems, prob_sems) = refs[n_buf + 6 :]
        used = info_ref[2]
        fetches = []
        for part in range(3):
            rows = slice(part * D, (part + 1) * D)
            fetches.append(pltpu.make_async_copy(w_src.at[rows], w_vmem.at[rows], w_sems.at[part]))
            fetches[-1].start()
        start_in(codes_ref, n_units, in_bufs, x_in, in_sems.at[0])
        bias_low = bias_ref[...].astype(BF)
        lane = lax.broadcasted_iota(jnp.int32, (KEYS, 128), 1)
        for twin in range(2):
            keys[twin, :, 0:128] = jnp.zeros((2 * KEYS, 128), BF)
            keys[twin, :, 128:256] = marks_ref[...]
            vals[twin, :, 0:128] = jnp.zeros((2 * KEYS, 128), BF)
            vals[twin, 0:KEYS, 128:256] = (lane < 64).astype(BF)
            vals[twin, KEYS:, 128:256] = (lane >= 64).astype(BF)

        wait_all(x_in, in_sems.at[0])
        x = x_in[...].reshape(n_rows, D)
        saves = [pltpu.make_async_copy(x_in, win_out, save_sems.at[0])]
        inner = nt(x, down_ref[0]).astype(BF)
        inner_ref[...] = inner
        for part in range(3):
            cols = slice(part * D, (part + 1) * D)
            fetches[part].wait()
            mixed = nt(x, w_vmem[cols]) + bias_ref[:, cols] + nn(inner, up_ref[0, :, cols])
            mixed_ref[:, cols] = mixed.astype(BF)
        saves.append(pltpu.make_async_copy(mixed_ref, mixed_out, save_sems.at[1]))
        saves.append(pltpu.make_async_copy(inner_ref, inner_out, save_sems.at[2]))
        for save in saves:
            save.start()
        small = lax.broadcasted_iota(jnp.int32, (PITCH, 128), 1)
        low_half = lax.broadcasted_iota(jnp.int32, (TOK, 128), 1) < 64

        def attend(at, rows, slot):
            for j in range(PAIRS):
                twin = j % 2
                key, value = key_value(mixed_ref, bias_low, at, rows, j)
                fill_heads(keys.at[twin], key, low_half)
                fill_heads(vals.at[twin], value, low_half)
                cols = slice(128 * j, 128 * j + 128)
                q = mixed_ref[pl.ds(at, rows), cols]
                rel = nn(q, table_ref[...])
                pieces = []
                for x_at in range(rows // PITCH):
                    slab = rel[PITCH * x_at : PITCH * x_at + PITCH]
                    tall = pltpu.roll(slab, 113 + x_at, 1)
                    wide = pltpu.roll(slab, 113, 1, stride=1, stride_axis=0)
                    both = jnp.where(small % 64 < 32, tall, wide)
                    pieces.append(jnp.where(small == 14, 1.0, both).astype(BF))
                query = jnp.concatenate((q, jnp.concatenate(pieces, 0)), 1)
                scores = nt(query, keys[twin])
                probs = []
                for head in range(2):
                    part = scores[:, KEYS * head : KEYS * head + KEYS]
                    top = jnp.max(part, axis=-1, keepdims=True)
                    probs.append(jnp.exp(part - top).astype(BF))
                prob = jnp.concatenate(probs, 1)
                prob_ref[j, pl.ds(at, rows)] = prob
                summed = nn(prob, vals[twin])
                inverse = 1.0 / summed[:, 128:256]
                inv_ref[pl.ds(at, rows), cols] = inverse
                att = (summed[:, 0:128] * inverse).astype(BF)
                x_out[pl.ds(at // PITCH, rows // PITCH), :, cols] = att.reshape(
                    rows // PITCH, PITCH, 128
                )
            span = pl.ds(at, rows)
            pltpu.make_async_copy(prob_ref.at[:, span], prob_out.at[:, span],
                                  prob_sems.at[slot, 0]).start()
            pltpu.make_async_copy(inv_ref.at[span], inv_out.at[span], prob_sems.at[slot, 1]).start()
            start_out(codes_ref, at // PITCH, rows // PITCH, x_out, out_bufs, None, out_sems.at[0])

        each_slot(info_ref, plan, attend)
        start_out(codes_ref, used, n_units - used, x_out, out_bufs, plan["local"], out_sems.at[0])
        save = pltpu.make_async_copy(x_out, att_out, save_sems.at[3])
        save.start()

        def finish(at, rows, slot):
            span = pl.ds(at, rows)
            pltpu.make_async_copy(prob_ref.at[:, span], prob_out.at[:, span],
                                  prob_sems.at[slot, 0]).wait()
            pltpu.make_async_copy(inv_ref.at[span], inv_out.at[span], prob_sems.at[slot, 1]).wait()

        wait_all(x_out, out_sems.at[0])
        each_slot(info_ref, plan, finish)
        for one in saves + [save]:
            one.wait()

    saved = saved_shapes(plan)
    boxed = jax.ShapeDtypeStruct((n_units, PITCH, D), BF)
    results = pl.pallas_call(
        kernel,
        out_shape=outs + [boxed] + saved[1:5] + [boxed],
        grid_spec=pltpu.PrefetchScalarGridSpec(
            num_scalar_prefetch=2,
            grid=(1,),
            in_specs=any_specs(n_buf + 2)
            + [
                full_spec((1, 3 * D)),
                image_spec(down.shape, number),
                image_spec(up.shape, number),
                full_spec(table.shape),
                full_spec(marks.shape),
            ],
            out_specs=any_specs(n_buf + 6),
            scratch_shapes=[
                pltpu.VMEM((n_units, PITCH, D), BF),
                pltpu.VMEM((n_units, PITCH, D), BF),
                pltpu.VMEM((3 * D, D), BF),
                pltpu.VMEM((2, 2 * KEYS, 256), BF),
                pltpu.VMEM((2, 2 * KEYS, 256), BF),
                pltpu.VMEM((n_rows, 3 * D), BF),
                pltpu.VMEM((n_rows, RANK), BF),
                pltpu.VMEM((PAIRS, n_rows, 2 * KEYS), BF),
                pltpu.VMEM((n_rows, D), F32),
                pltpu.SemaphoreType.DMA((1,)),
                pltpu.SemaphoreType.DMA((1,)),
                pltpu.SemaphoreType.DMA((3,)),
                pltpu.SemaphoreType.DMA((4,)),
                pltpu.SemaphoreType.DMA((n_slots, 2)),
            ],
        ),
        cost_estimate=cost(10e9, 20e6, 4e6),
        compiler_params=params(),
        name="attention_forward",
    )(codes, info, *units, zero, weight, qkv_bias, down, up, table, marks)
    return results[:n_buf], results[n_buf:]


FF_KINDS = ("pd", "pu", "ed", "eu", "cd", "cu")
HALVES = (("eu", "pd", "pu", "ed", "cu"), ("cd",))
FF_WIDTHS = {"pd": D, "pu": D, "ed": D, "eu": FF, "cd": FF, "cu": D}


def stage_pieces(ranks):
    for h, kinds in enumerate(HALVES):
        at = 0
        for kind in kinds:
            wide = FF_WIDTHS[kind] // ranks
            yield h, at, wide, kind
            at += wide


def feed_forward(units, images, cotangent, number, row_count, weight_src, proj_copies,
                 expand_copies, contract_copies, vectors, adapter_src, adapter_index,
                 adapter_copies, place, codes, plan, rows_block, ranks, previous):
    side, steps, rows_spec = rows_plan(images, row_count, rows_block, number)
    per_step = rows_block * GRID
    tokens = rows_block * side
    outs = unit_shapes(plan)
    n_buf = len(outs)
    copies = [proj_copies, expand_copies, contract_copies]
    chunk = 512
    chunks = FF // chunk
    n_src = len(weight_src)
    stage_width = 2 * FF // ranks
    n_prev = len(previous)
    term_width = 3 * FF // ranks

    def kernel(codes_ref, pick_ref, *refs):
        in_bufs, refs = refs[:n_buf], refs[n_buf:]
        img_ref, cot_ref, refs = refs[0], refs[1], refs[2:]
        w_src, refs = refs[:n_src], refs[n_src:]
        (bp, g2, b2, be, bc), refs = refs[:5], refs[5:]
        a_src, place_ref, placet_ref, refs = refs[0:2], refs[2], refs[3], refs[4 + n_prev :]
        out_bufs, refs = refs[:n_buf], refs[n_buf:]
        block_ref, mid_ref, terms_ref, refs = refs[0], refs[1], refs[2], refs[3:]
        (pd, pu, ed, eu, cd, cu), refs = refs[:6], refs[6:]
        (d_pd, d_pu, d_ed, d_eu, d_cd, d_cu), refs = refs[:6], refs[6:]
        u_in, u_out, wp, we, wc, stage_a, stage_b, in_sems, out_sems, w_sems, s_sems = refs
        adapters = dict(zip(FF_KINDS, (pd, pu, ed, eu, cd, cu)))
        grads = dict(zip(FF_KINDS, (d_pd, d_pu, d_ed, d_eu, d_cd, d_cu)))
        step = pl.program_id(0)
        targets = [wp, we, wc]

        def weights(which):
            for src, dst in copies[which]:
                pltpu.make_async_copy(
                    w_src[which].at[src], targets[which].at[dst], w_sems.at[which]
                ).start()

        @pl.when(step == 0)
        def _():
            stages = (stage_a, stage_b)
            for half, src, dst in adapter_copies(pick_ref[number]):
                pltpu.make_async_copy(a_src[half].at[src], stages[half].at[dst],
                                      s_sems.at[half]).start()
            start_in(codes_ref, row_count * GRID, in_bufs, u_in, in_sems.at[0])
            for which in range(3):
                weights(which)
            for grad in grads.values():
                grad[...] = jnp.zeros_like(grad)
            wait_all(stage_a, s_sems.at[0])
            wait_all(stage_b, s_sems.at[1])
            for h, at, wide, kind in stage_pieces(ranks):
                for r in range(ranks):
                    adapters[kind][:, wide * r : wide * r + wide] = stages[h][
                        r, :, at : at + wide
                    ]
            wait_all(wp, w_sems.at[0])
            wait_all(u_in, in_sems.at[0])

        rows = []
        for r in range(rows_block):
            spread = u_in[pl.ds(step * per_step + r * GRID, GRID)].reshape(GRID * PITCH, D)
            rows.append(nn(placet_ref[...], spread).astype(BF))
        att = jnp.concatenate(rows, 0)
        cot = cot_ref[...].reshape(tokens, D)
        p_inner = nt(att, pd[...]).astype(BF)
        middle = (
            img_ref[...].reshape(tokens, D).astype(F32)
            + nt(att, wp[...])
            + bp[...]
            + nn(p_inner, pu[...])
        )
        standard, inverse = norm_parts(middle)
        second = (standard * g2[...] + b2[...]).astype(BF)
        e_inner = nt(second, ed[...]).astype(BF)
        c_mid = nt(cot, cu[...]).astype(BF)
        result = middle + bc[...]
        c_inner = jnp.zeros((tokens, RANK), F32)
        e_mid = jnp.zeros((tokens, RANK), F32)
        second_grad = jnp.zeros((tokens, D), F32)

        @pl.when(step == 0)
        def _():
            wait_all(we, w_sems.at[1])
            wait_all(wc, w_sems.at[2])

        for n in range(chunks):
            cols = slice(n * chunk, (n + 1) * chunk)
            hidden = nn(second, we[:, cols]) + be[:, cols] + nn(e_inner, eu[:, cols])
            cdf = 0.5 * (1.0 + lax.erf(hidden * SQRT_HALF))
            slope = cdf + hidden * jnp.exp(-0.5 * hidden * hidden) * INV_SQRT_TAU
            active = (hidden * cdf).astype(BF)
            a_grad = nn(cot, wc[:, cols]) + nn(c_mid, cd[:, cols])
            h_grad = (a_grad * slope).astype(BF)
            result = result + nt(active, wc[:, cols])
            c_inner = c_inner + nt(active, cd[:, cols])
            second_grad = second_grad + nt(h_grad, we[:, cols])
            e_mid = e_mid + nt(h_grad, eu[:, cols])
            d_cd[:, cols] += tn(c_mid, active)
            d_eu[:, cols] += tn(e_inner, h_grad)
        c_inner = c_inner.astype(BF)
        e_mid = e_mid.astype(BF)
        result = result + nn(c_inner, cu[...])
        block_ref[...] = result.astype(BF).reshape(rows_block, side, D)
        d_cu[...] += tn(c_inner, cot)
        d_ed[...] += tn(e_mid, second)
        second_grad = second_grad + nn(e_mid, ed[...])
        middle_grad = cot.astype(F32) + norm_back(second_grad, standard, inverse, g2[...])
        mid_ref[...] = middle_grad.reshape(rows_block, side, D)
        branch = middle_grad.astype(BF)
        p_mid = nt(branch, pu[...]).astype(BF)
        d_pu[...] += tn(p_inner, branch)
        d_pd[...] += tn(p_mid, att)
        att_grad = (nn(branch, wp[...]) + nn(p_mid, pd[...])).astype(BF)
        for r in range(rows_block):
            spread = nn(place_ref[...], att_grad[r * side : (r + 1) * side])
            u_out[pl.ds(step * per_step + r * GRID, GRID)] = spread.astype(BF).reshape(
                GRID, PITCH, D
            )
        start_out(codes_ref, step * per_step, per_step, u_out, out_bufs, None, out_sems.at[0])

        @pl.when(step == steps - 1)
        def _():
            at = 0
            for kind in FF_KINDS:
                wide = FF_WIDTHS[kind] // ranks
                for r in range(ranks):
                    terms_ref[r, :, at : at + wide] = grads[kind][
                        :, wide * r : wide * r + wide
                    ].astype(BF)
                at += wide
            if at < term_width:
                terms_ref[:, :, at:] = jnp.zeros((ranks, RANK, term_width - at), BF)
            wait_all(u_out, out_sems.at[0])

    results = pl.pallas_call(
        kernel,
        out_shape=outs
        + [
            jax.ShapeDtypeStruct(images.shape, BF),
            jax.ShapeDtypeStruct((row_count, side, D), F32),
            jax.ShapeDtypeStruct((ranks, RANK, term_width), BF),
        ],
        grid_spec=pltpu.PrefetchScalarGridSpec(
            num_scalar_prefetch=2,
            grid=(steps,),
            in_specs=any_specs(n_buf)
            + [rows_spec, rows_spec]
            + any_specs(n_src)
            + [full_spec(v.shape) for v in vectors]
            + any_specs(2)
            + [full_spec(place.shape), full_spec(place.shape[::-1])]
            + any_specs(n_prev),
            out_specs=any_specs(n_buf)
            + [
                rows_spec,
                pl.BlockSpec((rows_block, side, D), lambda i, *_: (i, 0, 0)),
                full_spec((ranks, RANK, term_width)),
            ],
            scratch_shapes=[pltpu.VMEM((RANK, FF_WIDTHS[k]), BF) for k in FF_KINDS]
            + [pltpu.VMEM((RANK, FF_WIDTHS[k]), F32) for k in FF_KINDS]
            + [
                pltpu.VMEM((row_count * GRID, PITCH, D), BF),
                pltpu.VMEM((row_count * GRID, PITCH, D), BF),
                pltpu.VMEM((D, D), BF),
                pltpu.VMEM((D, FF), BF),
                pltpu.VMEM((D, FF), BF),
                pltpu.VMEM((ranks, RANK, stage_width), BF),
                pltpu.VMEM((ranks, RANK, FF // ranks), BF),
                pltpu.SemaphoreType.DMA((1,)),
                pltpu.SemaphoreType.DMA((1,)),
                pltpu.SemaphoreType.DMA((3,)),
                pltpu.SemaphoreType.DMA((2,)),
            ],
        ),
        input_output_aliases={2 + n_buf + 2 + n_src + 5 + 4: n_buf} if n_prev else {},
        cost_estimate=cost(18e9, 20e6, 4e6),
        compiler_params=params(),
        name="feed_forward",
    )(codes, adapter_index, *units, images, cotangent, *weight_src, *vectors, *adapter_src, place,
      place.T, *previous)
    return results[:n_buf], results[n_buf], results[n_buf + 1], results[n_buf + 2]


def attention_backward(units, zero, weight, saved, qkv_bias, down, up, number, table, marks, codes,
                       info, plan, ranks):
    outs = unit_shapes(plan)
    n_buf = len(outs)
    n_units = plan["units"]
    n_rows = n_units * PITCH
    n_slots = plan["full"] + plan["short"]
    term_width = 4 * D // ranks

    def kernel(codes_ref, info_ref, *refs):
        in_bufs, refs = refs[: n_buf + 1], refs[n_buf + 1 :]
        w_src, refs = refs[0], refs[1:]
        (win_src, mixed_src, inner_src, prob_src, inv_src, att_src), refs = refs[:6], refs[6:]
        bias_ref, down_ref, up_ref, table_ref, marks_ref = refs[:5]
        refs = refs[5:]
        out_bufs, refs = refs[:n_buf], refs[n_buf:]
        terms_ref, refs = refs[0], refs[1:]
        (g_in, x_out, w_vmem, keys, vals, grads, win_ref, mixed_ref, inner_ref, prob_ref, inv_ref,
         att_ref, in_sems, out_sems, load_sems, prob_sems) = refs
        used = info_ref[2]
        start_in(codes_ref, n_units, in_bufs, g_in, in_sems.at[0])
        loads = [
            pltpu.make_async_copy(src, dst, load_sems.at[n])
            for n, (src, dst) in enumerate(
                ((mixed_src, mixed_ref), (att_src, att_ref), (inner_src, inner_ref),
                 (win_src, win_ref), (w_src, w_vmem)))
        ]

        def slot_loads(at, rows, slot):
            span = pl.ds(at, rows)
            return (
                pltpu.make_async_copy(prob_src.at[:, span], prob_ref.at[:, span],
                                      prob_sems.at[slot, 0]),
                pltpu.make_async_copy(inv_src.at[span], inv_ref.at[span], prob_sems.at[slot, 1]),
            )

        def begin(at, rows, slot):
            for copy in slot_loads(at, rows, slot):
                copy.start()

        for load in loads[:2]:
            load.start()
        each_slot(info_ref, plan, begin)
        for load in loads[2:]:
            load.start()
        bias_low = bias_ref[...].astype(BF)
        for twin in range(2):
            keys[twin, :, 0:128] = jnp.zeros((2 * KEYS, 128), BF)
            keys[twin, :, 128:256] = marks_ref[...]
            vals[twin] = jnp.zeros((2 * KEYS, 128), BF)

        def clear(unit, carry):
            grads[pl.ds(pl.multiple_of(unit * PITCH, PITCH), PITCH)] = jnp.zeros((PITCH, 3 * D), BF)
            return carry

        lax.fori_loop(used, n_units, clear, 0)
        loads[0].wait()
        loads[1].wait()
        wait_all(g_in, in_sems.at[0])
        small = lax.broadcasted_iota(jnp.int32, (PITCH, 128), 1)
        low_half = lax.broadcasted_iota(jnp.int32, (TOK, 128), 1) < 64

        def attend(at, rows, slot):
            for copy in slot_loads(at, rows, slot):
                copy.wait()
            span = pl.ds(at, rows)
            half = low_half[:rows]
            for j in range(PAIRS):
                twin = j % 2
                cols = slice(128 * j, 128 * j + 128)
                key, value = key_value(mixed_ref, bias_low, at, rows, j)
                fill_heads(keys.at[twin], key, low_half)
                fill_heads(vals.at[twin], value, low_half)
                q = mixed_ref[span, cols]
                units_at = pl.ds(at // PITCH, rows // PITCH)
                grad = g_in[units_at, :, cols].reshape(rows, 128).astype(F32) * inv_ref[span, cols]
                grad_low = grad.astype(BF)
                weighed = grad * att_ref[units_at, :, cols].reshape(rows, 128).astype(F32)
                total = jnp.sum(weighed, axis=-1, keepdims=True)
                dot_a = jnp.sum(jnp.where(half, weighed, 0.0), axis=-1, keepdims=True)
                dots = (dot_a, total - dot_a)
                soft = nt(grad_low, vals[twin])
                pieces = []
                for head in range(2):
                    lanes = slice(KEYS * head, KEYS * head + KEYS)
                    prob = prob_ref[j, span, lanes].astype(F32)
                    pieces.append((prob * (soft[:, lanes] - dots[head])).astype(BF))
                both = nn(jnp.concatenate(pieces, 1), keys[twin])
                rel = both[:, 128:256]
                unrolled = []
                for x_at in range(rows // PITCH):
                    slab = rel[PITCH * x_at : PITCH * x_at + PITCH]
                    tall = pltpu.roll(slab, x_at, 1) if x_at else slab
                    wide = pltpu.roll(slab, 0, 1, stride=1, stride_axis=0)
                    unrolled.append(jnp.where(small % 64 < 32, tall, wide).astype(BF))
                q_grad = both[:, 0:128] + nn(jnp.concatenate(unrolled, 0), table_ref[...])
                grads[span, cols] = q_grad.astype(BF)
                q_t = q.T
                g_t = grad_low.T
                k_parts = []
                v_parts = []
                for head in range(2):
                    lanes = slice(KEYS * head, KEYS * head + KEYS)
                    own = slice(64 * head, 64 * head + 64)
                    k_parts.append(nn(q_t[own], pieces[head]))
                    v_parts.append(nn(g_t[own], prob_ref[j, span, lanes]))
                k_grad = jnp.concatenate(k_parts, 0).T[:rows] * HEAD_DIM ** -0.5
                v_grad = jnp.concatenate(v_parts, 0).T[:rows]
                grads[span, D + 128 * j : D + 128 * j + 128] = k_grad.astype(BF)
                grads[span, 2 * D + 128 * j : 2 * D + 128 * j + 128] = v_grad.astype(BF)

        each_slot(info_ref, plan, attend)
        for load in loads[2:]:
            load.wait()
        mixed_grad = grads[...]
        mid = nt(mixed_grad, up_ref[0]).astype(BF)
        normed = nn(mixed_grad, w_vmem[...]) + nn(mid, down_ref[0])
        x_out[...] = normed.astype(BF).reshape(n_units, PITCH, D)
        start_out(codes_ref, 0, n_units, x_out, out_bufs, plan["local"], out_sems.at[0])
        d_up = tn(inner_ref[...], mixed_grad).astype(BF)
        d_down = tn(mid, win_ref[...].reshape(n_rows, D)).astype(BF)
        at = 0
        for value, wide in ((d_down, D // ranks), (d_up, 3 * D // ranks)):
            for r in range(ranks):
                terms_ref[r, :, at : at + wide] = value[:, wide * r : wide * r + wide]
            at += wide
        wait_all(x_out, out_sems.at[0])

    results = pl.pallas_call(
        kernel,
        out_shape=outs + [jax.ShapeDtypeStruct((ranks, RANK, term_width), BF)],
        grid_spec=pltpu.PrefetchScalarGridSpec(
            num_scalar_prefetch=2,
            grid=(1,),
            in_specs=any_specs(n_buf + 8)
            + [full_spec((1, 3 * D)), image_spec(down.shape, number), image_spec(up.shape, number),
               full_spec(table.shape), full_spec(marks.shape)],
            out_specs=any_specs(n_buf) + [full_spec((ranks, RANK, term_width))],
            scratch_shapes=[
                pltpu.VMEM((n_units, PITCH, D), BF),
                pltpu.VMEM((n_units, PITCH, D), BF),
                pltpu.VMEM((3 * D, D), BF),
                pltpu.VMEM((2, 2 * KEYS, 256), BF),
                pltpu.VMEM((2, 2 * KEYS, 128), BF),
                pltpu.VMEM((n_rows, 3 * D), BF),
                pltpu.VMEM((n_units, PITCH, D), BF),
                pltpu.VMEM((n_rows, 3 * D), BF),
                pltpu.VMEM((n_rows, RANK), BF),
                pltpu.VMEM((PAIRS, n_rows, 2 * KEYS), BF),
                pltpu.VMEM((n_rows, D), F32),
                pltpu.VMEM((n_units, PITCH, D), BF),
                pltpu.SemaphoreType.DMA((1,)),
                pltpu.SemaphoreType.DMA((1,)),
                pltpu.SemaphoreType.DMA((5,)),
                pltpu.SemaphoreType.DMA((n_slots, 2)),
            ],
        ),
        cost_estimate=cost(12e9, 20e6, 4e6),
        compiler_params=params(),
        name="attention_backward",
    )(codes, info, *units, zero, weight, *saved, qkv_bias, down, up, table, marks)
    return results[:n_buf], results[n_buf]


def first_norm_back(units, images, middle_grad, number, row_count, gain, place_t, codes, plan,
                    rows_block, previous):
    side, steps, rows_spec = rows_plan(images, row_count, rows_block, number)
    per_step = rows_block * GRID
    n_buf = len(units)
    n_prev = len(previous)

    def kernel(codes_ref, *refs):
        in_bufs, refs = refs[:n_buf], refs[n_buf:]
        x_ref, m_ref, g_ref, p_ref, refs = refs[0], refs[1], refs[2], refs[3], refs[4 + n_prev :]
        out_ref, u_in, sems = refs
        step = pl.program_id(0)

        @pl.when(step == 0)
        def _():
            start_in(codes_ref, row_count * GRID, in_bufs, u_in, sems.at[0])

        values = x_ref[...].reshape(rows_block * side, D).astype(F32)
        standard, inverse = norm_parts(values)

        @pl.when(step == 0)
        def _():
            wait_all(u_in, sems.at[0])

        rows = []
        for r in range(rows_block):
            spread = u_in[pl.ds(step * per_step + r * GRID, GRID)].reshape(GRID * PITCH, D)
            rows.append(nn(p_ref[...], spread))
        upstream = jnp.concatenate(rows, 0)
        back = norm_back(upstream, standard, inverse, g_ref[...])
        out_ref[...] = m_ref[...] + back.reshape(rows_block, side, D)

    return pl.pallas_call(
        kernel,
        out_shape=jax.ShapeDtypeStruct(images.shape, F32),
        grid_spec=pltpu.PrefetchScalarGridSpec(
            num_scalar_prefetch=1,
            grid=(steps,),
            in_specs=any_specs(n_buf)
            + [
                rows_spec,
                pl.BlockSpec((rows_block, side, D), lambda i, *_: (i, 0, 0)),
                full_spec((1, D)),
                full_spec(place_t.shape),
            ]
            + any_specs(n_prev),
            out_specs=rows_spec,
            scratch_shapes=[
                pltpu.VMEM((row_count * GRID, PITCH, D), BF),
                pltpu.SemaphoreType.DMA((1,)),
            ],
        ),
        input_output_aliases={1 + n_buf + 4: 0} if n_prev else {},
        cost_estimate=cost(1e9, 8e6),
        compiler_params=params(),
        name="first_norm_back",
    )(codes, *units, images, middle_grad, gain, place_t, *previous)


KINDS = ("qd", "qu", "pd", "pu", "ed", "eu", "cd", "cu")
WIDTHS = {"qd": D, "qu": 3 * D, "pd": D, "pu": D, "ed": D, "eu": FF, "cd": FF, "cu": D}


def packed_form(groups, ranks):
    return groups == 4 and ranks == 8


def shift_z(value, step):
    return lax.ppermute(value, "rows", [(r, (r + 2 * step) % 8) for r in range(8)])


def flip_y(value):
    return lax.ppermute(value, "rows", [(r, r ^ 1) for r in range(8)])


def flip_x(value):
    return lax.ppermute(value, "dp", [(d, d ^ 2) for d in range(4)])


def flip_core(value):
    return lax.ppermute(value, "dp", [(d, d ^ 1) for d in range(4)])


NQ, NP = 144, 48
MOVES = ((0, 0, 0), (0, 0, 1), (0, 1, 0), (0, 1, 1), (1, 0, 0), (1, 0, 1), (1, 1, 0), (1, 1, 1),
         (0, 0, 2), (0, 0, 3), (1, 0, 2), (1, 0, 3), (0, 1, 2), (0, 1, 3), (1, 1, 2), (1, 1, 3))


def piece_table():
    table = np.zeros((4, 8, 32), np.int32)
    for d in range(4):
        for r in range(8):
            for number, (kx, ky, kz) in enumerate(MOVES):
                for kc in range(2):
                    source_d = (d ^ (2 * kx)) ^ kc
                    source_r = ((r // 2 - kz) % 4) * 2 + ((r % 2) ^ ky)
                    table[d, r, source_r * 4 + source_d] = 16 * kc + number
    return table


def pack(qkv, proj, expand, contract, adapters):
    core = (lax.axis_index("dp") % 2).reshape(1)
    rows = qkv.shape[0]
    ne, nc = expand.shape[0] // 2, contract.shape[1]
    n_ad = len(adapters)
    lists = KINDS

    def kernel(core_ref, q_ref, p_ref, e_ref, c_ref, *refs):
        ads = dict(zip(lists, refs[:n_ad]))
        second, own, other, extra = refs[n_ad:]

        def turned(value):
            wide = value.shape[1]
            eye = (
                lax.broadcasted_iota(jnp.int32, (wide, wide), 0)
                == lax.broadcasted_iota(jnp.int32, (wide, wide), 1)
            )
            return nt(eye.astype(F32).astype(BF), value).astype(BF)

        q_t = turned(q_ref[...])
        p_t = turned(p_ref[...])
        for half, chosen in ((0, 0), (1, 1)):
            @pl.when(core_ref[0] == chosen)
            def _():
                own[0:NQ] = q_t[half * NQ : half * NQ + NQ]
                own[NQ:] = p_t[half * NP : half * NP + NP]
                other[0:NQ] = q_t[(1 - half) * NQ : (1 - half) * NQ + NQ]
                other[NQ:] = p_t[(1 - half) * NP : (1 - half) * NP + NP]

        second[0:ne, 0 : expand.shape[1]] = e_ref[0:ne]
        second[0:ne, expand.shape[1] :] = e_ref[ne:]
        second[ne : ne + nc] = turned(c_ref[...])
        base = ne + nc
        for i in range(2):
            rows_i = slice(base + i * RANK, base + i * RANK + RANK)
            at = 0
            for kind in HALVES[0]:
                wide = ads[kind].shape[2]
                second[rows_i, at : at + wide] = ads[kind][i]
                at += wide
            wide = ads["cd"].shape[2]
            second[base + 2 * RANK :, i * wide : i * wide + wide] = ads["cd"][i]
            at = ads["qu"].shape[2]
            extra[i * RANK : i * RANK + RANK, 0:at] = ads["qu"][i]
            extra[i * RANK : i * RANK + RANK, at:] = ads["qd"][i]

    shapes = [(ne + nc + 3 * RANK, D), (NQ + NP, rows), (NQ + NP, rows), (2 * RANK, 384)]
    return pl.pallas_call(
        kernel,
        out_shape=[jax.ShapeDtypeStruct(shape, BF) for shape in shapes],
        grid_spec=pltpu.PrefetchScalarGridSpec(
            num_scalar_prefetch=1,
            grid=(1,),
            in_specs=[full_spec(v.shape) for v in (qkv, proj, expand, contract) + adapters],
            out_specs=[full_spec(shape) for shape in shapes],
        ),
        cost_estimate=cost(1e8, 2e6),
        compiler_params=params(),
        name="pack",
    )(core, qkv, proj, expand, contract, *adapters)


def gather_first(own, other, extra, norms):
    core = lax.axis_index("dp") % 2
    other = flip_core(other)
    joined = jnp.where(
        core == 0, jnp.concatenate((own, other), 1), jnp.concatenate((other, own), 1)
    )
    piece = jnp.concatenate((joined, extra), 0)
    piece = after(piece, norms[0])
    line = jnp.stack([piece] + [shift_z(piece, k) for k in (1, 2, 3)])
    line = after(line, norms[-1])
    left, right = line[:2], line[2:]
    left = jnp.concatenate((left, flip_y(left)))
    right = jnp.concatenate((right, flip_x(right)))
    left, right = lax.optimization_barrier((left, right))
    pieces = jnp.concatenate((left, flip_x(left), right, flip_y(right)))
    return (left, right), pieces, flip_core(pieces), line


def assemble(pieces, others, table, adapter_index, image_count):
    def kernel(table_ref, pick_ref, a_ref, b_ref, wq, wp, down_ref, up_ref, stage, w_sems, s_sems):
        def fetch(block, src_rows, dst, sem):
            code = table_ref[block]
            index = code % 16

            @pl.when(code < 16)
            def _():
                pltpu.make_async_copy(a_ref.at[index, src_rows], dst, sem).start()

            @pl.when(code >= 16)
            def _():
                pltpu.make_async_copy(b_ref.at[index, src_rows], dst, sem).start()

        for n in range(image_count):
            chosen = pick_ref[n]
            rows = pl.ds(pl.multiple_of(NQ + NP + RANK * (chosen % 2), 16), RANK)
            for r in range(8):
                fetch(r * 4 + chosen // 2, rows, stage.at[n, r], s_sems.at[0])
        for r in range(8):
            for d in range(4):
                x, c = divmod(d, 2)
                lanes = slice(384 * x, 384 * x + 384)
                top = 2 * NQ * r + NQ * c
                fetch(r * 4 + d, slice(0, NQ), wq.at[top : top + NQ, lanes], w_sems.at[0])
                top = 2 * NP * r + NP * c
                fetch(r * 4 + d, slice(NQ, NQ + NP), wp.at[top : top + NP, lanes], w_sems.at[1])
        wait_all(stage, s_sems.at[0])
        for n in range(image_count):
            for r in range(8):
                up_ref[n, :, 288 * r : 288 * r + 288] = stage[n, r, :, 0:288]
                down_ref[n, :, 96 * r : 96 * r + 96] = stage[n, r, :, 288:384]
        wait_all(wq, w_sems.at[0])
        wait_all(wp, w_sems.at[1])

    return pl.pallas_call(
        kernel,
        out_shape=[
            jax.ShapeDtypeStruct((3 * D, D), BF),
            jax.ShapeDtypeStruct((D, D), BF),
            jax.ShapeDtypeStruct((image_count, RANK, D), BF),
            jax.ShapeDtypeStruct((image_count, RANK, 3 * D), BF),
        ],
        grid_spec=pltpu.PrefetchScalarGridSpec(
            num_scalar_prefetch=2,
            grid=(1,),
            in_specs=any_specs(2),
            out_specs=[
                full_spec((3 * D, D)),
                full_spec((D, D)),
                full_spec((image_count, RANK, D)),
                full_spec((image_count, RANK, 3 * D)),
            ],
            scratch_shapes=[
                pltpu.VMEM((image_count, 8, RANK, 384), BF),
                pltpu.SemaphoreType.DMA((2,)),
                pltpu.SemaphoreType.DMA((1,)),
            ],
        ),
        cost_estimate=cost(1e6, 10e6),
        compiler_params=params(),
        name="assemble",
    )(table, adapter_index, pieces, others)


def second_copies(groups, ranks):
    ne, nc = FF // (groups * ranks), D // ranks
    wide = FF // ranks
    expand, contract = [], []
    for r in range(ranks):
        for d in range(groups):
            b = r * groups + d
            for h in range(2):
                top = d * 2 * ne + h * ne
                expand.append(
                    (
                        (b, slice(0, ne), slice(h * wide, h * wide + wide)),
                        (slice(top, top + ne), slice(r * wide, r * wide + wide)),
                    )
                )
            contract.append(
                ((b, slice(ne, ne + nc)), (slice(nc * r, nc * r + nc), slice(D * d, D * d + D)))
            )
    return expand, contract, ne + nc


def second_adapters(base, groups, ranks):
    per_group = ADAPTERS // groups
    wide = FF // ranks

    def copies(chosen):
        found = []
        for r in range(ranks):
            block = r * groups + chosen // per_group
            own = chosen % per_group
            rows = pl.ds(pl.multiple_of(base + own * RANK, RANK), RANK)
            found.append((0, (block, rows), (r,)))
            rows = slice(base + 2 * RANK, base + 3 * RANK)
            found.append((1, (block, rows, pl.ds(pl.multiple_of(own * wide, 128), wide)), (r,)))
        return found

    return copies


def plain_stage(chosen, ranks):
    images = chosen[0].shape[0]
    lists = dict(zip(FF_KINDS, chosen))
    halves = []
    for kinds in HALVES:
        parts = [lists[k].reshape(images, RANK, ranks, -1).transpose(0, 2, 1, 3) for k in kinds]
        halves.append(jnp.concatenate(parts, 3))
    return [[half[n] for half in halves] for n in range(images)]


def gather_plain(weights, adapters, adapter_index):
    full = []
    for m in weights:
        m = lax.all_gather(m, "dp", axis=0, tiled=True)
        full.append(lax.all_gather(m, "rows", axis=1, tiled=True))
    qkv, proj, expand, contract = full
    chosen = []
    for m in adapters:
        m = lax.all_gather(m, "dp", axis=0, tiled=True)
        m = jnp.take(m, adapter_index[:, 0], axis=0)
        chosen.append(lax.all_gather(m, "rows", axis=2, tiled=True))
    return [qkv.T, proj.T, expand, contract.T], chosen


def rows_sum(packed):
    moved = lax.all_to_all(packed, "rows", split_axis=0, concat_axis=0, tiled=True)
    return jnp.sum(moved.astype(F32), axis=0)


def adapters_sum(sums, widths, adapter_index, groups):
    per_group = ADAPTERS // groups
    local = sums
    hit = (adapter_index[None, :] == jnp.arange(ADAPTERS)[:, None]).astype(F32)
    spread = jnp.sum(hit[:, :, None, None] * local[None], axis=1).astype(BF)
    spread = spread.reshape(groups, per_group, RANK, -1)
    moved = lax.all_to_all(spread, "dp", split_axis=0, concat_axis=0, tiled=True)
    total = jnp.sum(moved.astype(F32), axis=0)
    outs = []
    at = 0
    for wide in widths:
        outs.append(total[:, :, at : at + wide])
        at += wide
    return outs


def per_device(
    images, norm1_gain, norm1_bias, qkv_weight, qkv_bias, height_table, width_table, proj_weight,
    proj_bias, norm2_gain, norm2_bias, expand_weight, expand_bias, contract_weight, contract_bias,
    adapter_index, qkv_down, qkv_up, proj_down, proj_up, expand_down, expand_up, contract_down,
    contract_up, cotangent,
):
    image_count, row_count, side, _ = images.shape
    ranks = lax.axis_size("rows")
    groups = lax.axis_size("dp")
    rank = lax.axis_index("rows")
    plan = make_plan(ranks, row_count, 1)
    packed = packed_form(groups, ranks)
    pieces_at = piece_table() if packed else np.zeros((groups, ranks, 1), np.int32)
    tables = [np.broadcast_to(plan[k][None], (groups,) + plan[k].shape)
              for k in ("rows", "wins", "info")] + [pieces_at]
    ends = np.cumsum([0] + [t.shape[2] for t in tables])
    mine = jnp.asarray(np.concatenate(tables, 2))[lax.axis_index("dp"), rank]
    rows_code, win_code, info, piece_code = [mine[a:b] for a, b in zip(ends[:-1], ends[1:])]
    rows_block = 4 if row_count % 4 == 0 else row_count
    place = jnp.asarray(place_matrix(side), BF)
    marks_fwd, marks_bwd = [jnp.asarray(m, BF) for m in key_marks()]
    table_fwd, table_bwd = pair_tables(height_table, width_table)
    zero = jnp.zeros((1, PITCH, D), BF)
    row_vector = lambda v: v.reshape(1, -1)
    picked = adapter_index[:, 0]
    flat_images = images.reshape(image_count * row_count, side, D)
    flat_cotangent = cotangent.reshape(image_count * row_count, side, D)

    adapters = (qkv_down, qkv_up, proj_down, proj_up, expand_down, expand_up, contract_down,
                contract_up)
    whole = [((slice(None),), (slice(None),))]
    gain_one, bias_one = row_vector(norm1_gain), row_vector(norm1_bias)
    split = range(image_count)
    if packed:
        second, own, other, extra = pack(qkv_weight, proj_weight, expand_weight, contract_weight,
                                         adapters)
        gain_one = after(gain_one, own)
    sent = [first_norm(flat_images, n, row_count, gain_one, bias_one, place, rows_code, plan,
                       rows_block) for n in split]
    if packed:
        ready, pieces, others, line = gather_first(own, other, extra, [v[0] for v in sent])
        second = lax.all_gather(after(second, line), ("rows", "dp"), axis=0, tiled=False)
        units = [exchange([after(v, *ready) for v in sent[n]], plan, False) for n in split]
        others = after(others, *units[0])
        qkv_full, proj_full, down_one, up_one = assemble(pieces, others, piece_code, picked,
                                                         image_count)
        expand_copies, contract_copies, base = second_copies(groups, ranks)
        adapter_copies = second_adapters(base, groups, ranks)
        ff_src = [proj_full, second, second]
        adapter_src = [[second, second]] * image_count
    else:
        units = [exchange(sent[n], plan, False) for n in split]
        weights = (qkv_weight, proj_weight, expand_weight, contract_weight)
        full, chosen = gather_plain(weights, adapters, adapter_index)
        expand_copies = contract_copies = whole
        qkv_full = full[0]
        down_one, up_one = chosen[:2]
        ff_src = full[1:]
        everything = (slice(None),)
        adapter_copies = lambda index: [(h, everything, everything) for h in range(2)]
        adapter_src = plain_stage(chosen[2:], ranks)
    vectors = [row_vector(v) for v in (proj_bias, norm2_gain, norm2_bias, expand_bias,
                                       contract_bias)]
    forward = [attention_forward(units[n], zero, qkv_full, row_vector(qkv_bias), down_one, up_one,
                                 n, table_fwd, marks_fwd, win_code, info, plan) for n in split]
    units = [exchange(forward[n][0], plan, True) for n in split]
    ff = []
    for n in split:
        ff.append(feed_forward(units[n], flat_images, flat_cotangent, n, row_count, ff_src, whole,
                               expand_copies, contract_copies, vectors, adapter_src[n], picked,
                               adapter_copies, place, rows_code, plan, rows_block, ranks,
                               [f[1] for f in ff[-1:]]))
    units = [exchange(ff[n][0], plan, False) for n in split]
    backward = [attention_backward(units[n], zero, qkv_full, forward[n][1],
                                   row_vector(qkv_bias), down_one, up_one, n,
                                   table_bwd, marks_bwd, win_code, info, plan, ranks)
                for n in split]
    units = [exchange(backward[n][0], plan, True) for n in split]
    ff_terms = jnp.concatenate([f[3] for f in ff], 1)
    early_sums = after(rows_sum(ff_terms), backward[0][1]).reshape(image_count, RANK, -1)
    early = adapters_sum(early_sums, [FF_WIDTHS[k] // ranks for k in FF_KINDS], picked, groups)
    gain_one = after(gain_one, early[0])
    back = []
    for n in split:
        back.append(first_norm_back(units[n], flat_images, ff[n][2], n, row_count, gain_one,
                                    place.T, rows_code, plan, rows_block, back[-1:]))
    late_terms = jnp.concatenate([b[1] for b in backward], 1)
    late_terms = after(late_terms, back[0])
    late_sums = rows_sum(late_terms).reshape(image_count, RANK, -1)
    late = adapters_sum(late_sums, [D // ranks, 3 * D // ranks], picked, groups)
    return (ff[-1][1].reshape(images.shape), back[-1].reshape(images.shape), *late, *early)


def solution(mesh):
    whole = P()
    both = P("dp", "rows")
    adapter = P("dp", None, "rows")
    image = P("dp", "rows", None, None)
    placed = (image, whole, whole, both, whole, whole, whole, both, whole, whole, whole, both,
              whole, both, whole, P("dp", None), *([adapter] * 8), image)
    return jax.shard_map(
        per_device,
        mesh=mesh,
        in_specs=placed,
        out_specs=(image, image, *([adapter] * 8)),
        check_vma=False,
    )
```

```python
import itertools

import jax
import jax.numpy as jnp
import numpy as np
from jax import lax
from jax.experimental import pallas as pl
from jax.experimental.pallas import tpu as pltpu
from jax.sharding import PartitionSpec as P

HEAD_DIM = 64
WIN = 14
PITCH = 16
ADAPTERS = 8
RANK = 16
GRID = 5
D = 768
FF = 3072
HEADS = 12
PAIRS = HEADS // 2
TOK = WIN * PITCH
KEYS = 256
EPSILON = 1e-06
SQRT_HALF = 0.7071067811865476
INV_SQRT_TAU = 0.3989422804014327
SHIFT = 1024
SHORT = 8
CUT = SHORT * PITCH
BF = jnp.bfloat16
F32 = jnp.float32
VMEM_LIMIT = 60 * 1024 * 1024


def choose_owner(ranks, row_count, images):
    side_rows = ranks * row_count
    total = GRID * GRID * images
    weight = np.array(
        [0.77 if side_rows - (w // (GRID * images)) * WIN <= SHORT else 1.0 for w in range(total)]
    )

    def owner_of(cuts):
        return np.repeat(np.arange(ranks), np.diff([0] + list(cuts) + [total]))

    def cost_of(cuts):
        if min(np.diff([0] + list(cuts) + [total])) < 0:
            return 1e9
        owner = owner_of(cuts)
        load = np.bincount(owner, weights=weight, minlength=ranks).max()
        return 12.0 * load + color_edges(owner, ranks, row_count, images)[0]

    def filled(limit):
        cuts, load = [], 0.0
        for window in range(total):
            if load + weight[window] > limit + 1e-9:
                cuts.append(window)
                load = 0.0
            load += weight[window]
        return cuts + [total] * (ranks - 1 - len(cuts))

    limits = sorted({weight[a:b].sum() for a in range(total) for b in range(a + 1, total + 1)})
    least = next(limit for limit in limits if len(filled(limit)) == ranks - 1)
    reach = np.cumsum(weight) / weight.sum() * ranks
    even = [int(np.searchsorted(reach, r - 0.5)) for r in range(1, ranks)]
    found = (1e10, None)
    for cuts in (filled(least), even):
        best = cost_of(cuts)
        for _ in range(12):
            moved = False
            for place in range(ranks - 1):
                for width in (1, 2, 3):
                    for step in (-1, 1):
                        trial = list(cuts)
                        for extra in range(width):
                            if place + extra < ranks - 1:
                                trial[place + extra] += step
                        cost = cost_of(trial)
                        if cost < best - 1e-9:
                            best, cuts, moved = cost, trial, True
            if not moved:
                break
        if best < found[0] - 1e-9:
            found = (best, list(cuts))
    return owner_of(found[1])


def color_edges(owner, ranks, row_count, images):
    edges = {}
    local = [[] for _ in range(ranks)]
    for rank in range(ranks):
        for img in range(images):
            for k in range(row_count):
                row = rank * row_count + k
                for col in range(GRID):
                    window = (row // WIN) * images * GRID + img * GRID + col
                    unit = (img, k, col, window, row % WIN)
                    if owner[window] == rank:
                        local[rank].append(unit)
                    else:
                        edges.setdefault((rank, int(owner[window])), []).append(unit)
    colors = []
    for (src, dst), units in sorted(edges.items(), key=lambda e: (-len(e[1]), e[0])):
        for color in colors:
            if src not in color["src"] and dst not in color["dst"]:
                break
        else:
            color = {"src": set(), "dst": set(), "pairs": [], "units": []}
            colors.append(color)
        color["src"].add(src)
        color["dst"].add(dst)
        color["pairs"].append((src, dst))
        color["units"].append(units)
    sizes = [max(len(u) for u in c["units"]) for c in colors]
    cost = 0.4 * sum(sizes) + 3.0 * len(sizes)
    return cost, local, colors, sizes


def make_plan(ranks, row_count, images):
    total = GRID * GRID * images
    owner = choose_owner(ranks, row_count, images)
    _, local, colors, sizes = color_edges(owner, ranks, row_count, images)
    kinds = [ranks * row_count - w // (images * GRID) * WIN <= SHORT for w in range(total)]
    heights = [SHORT if short else WIN for short in kinds]
    most = int(np.bincount(owner, weights=heights, minlength=ranks).max())
    full_most = int(np.bincount(owner, weights=~np.array(kinds), minlength=ranks).max())
    short_most = int(np.bincount(owner, weights=np.array(kinds), minlength=ranks).max())
    skip = (len(colors) + 1) * SHIFT
    rows_code = np.full((ranks, images, row_count, GRID), skip, np.int32)
    win_code = np.full((ranks, most), skip, np.int32)
    first = np.searchsorted(owner, np.arange(ranks))

    def put(rank, unit, code, dst):
        img, k, col, window, place = unit
        rows_code[rank, img, k, col] = code
        win_code[dst, sum(heights[first[dst] : window]) + place] = code

    for rank in range(ranks):
        for number, unit in enumerate(local[rank]):
            put(rank, unit, number, rank)
    for which, color in enumerate(colors):
        for (src, dst), units in zip(color["pairs"], color["units"]):
            for number, unit in enumerate(units):
                put(src, unit, (which + 1) * SHIFT + number, dst)
    slot_info = np.zeros((ranks, 3), np.int32)
    for rank in range(ranks):
        mine = [kinds[w] for w in np.flatnonzero(owner == rank)]
        slot_info[rank] = (mine.count(False), mine.count(True),
                           sum(SHORT if short else WIN for short in mine))
    return {
        "rows": rows_code.reshape(ranks, -1),
        "wins": win_code,
        "info": slot_info,
        "units": most,
        "full": full_most,
        "short": short_most,
        "local": max(max(len(u) for u in local), 1),
        "sizes": sizes,
        "pairs": [c["pairs"] for c in colors],
    }


def place_matrix(side):
    out = np.zeros((GRID * PITCH, side), np.float32)
    for token in range(side):
        out[token // WIN * PITCH + token % WIN, token] = 1.0
    return out


def key_marks():
    fwd = np.zeros((2 * KEYS, 128), np.float32)
    bwd = np.zeros((2 * KEYS, 128), np.float32)
    for head in range(2):
        for key in range(KEYS):
            row = head * KEYS + key
            u, w = divmod(key, PITCH)
            if key >= TOK or w >= WIN:
                fwd[row, 14] = -1e30
                continue
            base = 64 * head
            for lane in (base + u, base + 32 + w):
                fwd[row, lane] = 1.0
            bwd[row, base + 13 - u] = 1.0
            bwd[row, base + 32 + 13 - w] = 1.0
    return fwd, bwd


def pair_tables(height_table, width_table):
    rev = jnp.pad(jnp.stack((height_table[::-1], width_table[::-1])), ((0, 0), (2, 3), (0, 0)))
    half = rev.reshape(64, HEAD_DIM).T
    zero = jnp.zeros_like(half)
    fwd = jnp.concatenate(
        (jnp.concatenate((half, zero), 1), jnp.concatenate((zero, half), 1)), 0
    )
    straight = jnp.pad(jnp.stack((height_table, width_table)), ((0, 0), (0, 5), (0, 0)))
    back = straight.reshape(64, HEAD_DIM)
    blank = jnp.zeros_like(back)
    bwd = jnp.concatenate(
        (jnp.concatenate((back, blank), 1), jnp.concatenate((blank, back), 1)), 0
    )
    return fwd, bwd


def nn(a, b):
    return lax.dot_general(a, b, (((1,), (0,)), ((), ())), preferred_element_type=F32)


def nt(a, b):
    return lax.dot_general(a, b, (((1,), (1,)), ((), ())), preferred_element_type=F32)


def tn(a, b):
    return lax.dot_general(a, b, (((0,), (0,)), ((), ())), preferred_element_type=F32)


def start_in(codes, count, bufs, dst, sem):
    def body(u, carry):
        code = codes[u]
        which = code // SHIFT
        index = code % SHIFT
        for number, buf in enumerate(bufs):
            @pl.when(which == number)
            def _():
                pltpu.make_async_copy(buf.at[index], dst.at[u], sem).start()
        return carry

    lax.fori_loop(0, count, body, 0)


def start_out(codes, first, count, src, bufs, spare, sem):
    def body(u, carry):
        code = codes[u]
        which = code // SHIFT
        index = code % SHIFT
        for number, buf in enumerate(bufs):
            @pl.when(which == number)
            def _():
                pltpu.make_async_copy(src.at[u], buf.at[index], sem).start()

        if spare is not None:
            @pl.when(which >= len(bufs))
            def _():
                pltpu.make_async_copy(src.at[u], bufs[0].at[spare + u], sem).start()
        return carry

    lax.fori_loop(first, first + count, body, 0)


def wait_all(whole, sem):
    pltpu.make_async_copy(whole, whole, sem).wait()


def norm_parts(values):
    average = jnp.mean(values, axis=-1, keepdims=True)
    centred = values - average
    variance = jnp.mean(centred * centred, axis=-1, keepdims=True)
    inverse = lax.rsqrt(variance + EPSILON)
    return centred * inverse, inverse


def norm_back(upstream, standard, inverse, gain):
    scaled = upstream * gain
    first_term = jnp.mean(scaled, axis=-1, keepdims=True)
    second_term = jnp.mean(scaled * standard, axis=-1, keepdims=True)
    return inverse * (scaled - first_term - standard * second_term)


def any_specs(count):
    return [pl.BlockSpec(memory_space=pl.ANY)] * count


def full_spec(shape):
    return pl.BlockSpec(shape, lambda *_: (0,) * len(shape))


def unit_shapes(plan):
    counts = [plan["local"] + plan["units"]] + plan["sizes"]
    return [jax.ShapeDtypeStruct((n, PITCH, D), BF) for n in counts]


def after(value, *others):
    return lax.optimization_barrier((value, *others))[0]


def exchange(bufs, plan, back):
    moved = [bufs[0]]
    for buf, pairs in zip(bufs[1:], plan["pairs"]):
        pairs = [(b, a) for a, b in pairs] if back else list(pairs)
        moved.append(lax.ppermute(buf, "rows", pairs))
    return moved


def cost(flops, moved, special=0):
    return pl.CostEstimate(flops=int(flops), bytes_accessed=int(moved), transcendentals=int(special))


def params():
    return pltpu.CompilerParams(vmem_limit_bytes=VMEM_LIMIT)


def rows_plan(images, row_count, rows_block, number):
    side = images.shape[1]
    steps = row_count // rows_block
    spec = pl.BlockSpec((rows_block, side, D), lambda i, *_: (number * steps + i, 0, 0))
    return side, steps, spec


def first_norm(images, number, row_count, gain, bias, place, codes, plan, rows_block):
    side, steps, rows_spec = rows_plan(images, row_count, rows_block, number)
    per_step = rows_block * GRID
    outs = unit_shapes(plan)

    def kernel(codes_ref, x_ref, g_ref, b_ref, p_ref, *rest):
        bufs, scratch, sems = rest[: len(outs)], rest[len(outs)], rest[len(outs) + 1]
        step = pl.program_id(0)
        values = x_ref[...].reshape(rows_block * side, D).astype(F32)
        standard, _ = norm_parts(values)
        normed = (standard * g_ref[...] + b_ref[...]).astype(BF)
        for r in range(rows_block):
            spread = nn(p_ref[...], normed[r * side : (r + 1) * side])
            scratch[pl.ds(step * per_step + r * GRID, GRID)] = spread.astype(BF).reshape(
                GRID, PITCH, D
            )
        start_out(codes_ref, step * per_step, per_step, scratch, bufs, None, sems.at[0])

        @pl.when(step == steps - 1)
        def _():
            wait_all(scratch, sems.at[0])

    return pl.pallas_call(
        kernel,
        out_shape=outs,
        grid_spec=pltpu.PrefetchScalarGridSpec(
            num_scalar_prefetch=1,
            grid=(steps,),
            in_specs=[rows_spec, full_spec((1, D)), full_spec((1, D)), full_spec(place.shape)],
            out_specs=any_specs(len(outs)),
            scratch_shapes=[
                pltpu.VMEM((row_count * GRID, PITCH, D), BF),
                pltpu.SemaphoreType.DMA((1,)),
            ],
        ),
        cost_estimate=cost(1e9, 8e6),
        compiler_params=params(),
        name="first_norm",
    )(codes, images, gain, bias, place)


def image_spec(shape, number):
    return pl.BlockSpec((1,) + shape[1:], lambda *_: (number,) + (0,) * (len(shape) - 1))


def saved_shapes(plan):
    rows = plan["units"] * PITCH
    return [
        jax.ShapeDtypeStruct((rows, D), BF),
        jax.ShapeDtypeStruct((rows, 3 * D), BF),
        jax.ShapeDtypeStruct((rows, RANK), BF),
        jax.ShapeDtypeStruct((PAIRS, rows, 2 * KEYS), BF),
        jax.ShapeDtypeStruct((rows, D), F32),
        jax.ShapeDtypeStruct((rows, D), BF),
    ]


def each_slot(info_ref, plan, body):
    n_full = info_ref[0]
    if plan["full"]:
        def full(slot, carry):
            body(pl.multiple_of(slot * TOK, 32), TOK, slot)
            return carry

        lax.fori_loop(0, n_full, full, 0)
    if plan["short"]:
        def short(slot, carry):
            body(pl.multiple_of(n_full * TOK + slot * CUT, 32), CUT, n_full + slot)
            return carry

        lax.fori_loop(0, info_ref[1], short, 0)


def key_value(mixed_ref, bias_low, at, rows, j):
    out = []
    for part in (1, 2):
        cols = slice(part * D + 128 * j, part * D + 128 * j + 128)
        own = mixed_ref[pl.ds(at, rows), cols]
        if rows < TOK:
            rest = jnp.broadcast_to(bias_low[:, cols], (TOK - rows, 128))
            own = jnp.concatenate((own, rest), 0)
        out.append(own)
    return out[0] * jnp.asarray(HEAD_DIM ** -0.5, BF), out[1]


def fill_heads(ref, value, low_half):
    nil = jnp.zeros_like(value)
    ref[0:TOK, 0:128] = jnp.where(low_half, value, nil)
    ref[KEYS : KEYS + TOK, 0:128] = jnp.where(low_half, nil, value)


def attention_forward(units, zero, weight, qkv_bias, down, up, number, table, marks, codes, info,
                      plan):
    outs = unit_shapes(plan)
    n_buf = len(outs)
    n_units = plan["units"]
    n_rows = n_units * PITCH
    n_slots = plan["full"] + plan["short"]

    def kernel(codes_ref, info_ref, *refs):
        in_bufs = refs[: n_buf + 1]
        w_src, bias_ref, down_ref, up_ref, table_ref, marks_ref = refs[n_buf + 1 : n_buf + 7]
        refs = refs[n_buf + 7 :]
        out_bufs = refs[:n_buf]
        win_out, mixed_out, inner_out, prob_out, inv_out, att_out = refs[n_buf : n_buf + 6]
        (x_in, x_out, w_vmem, keys, vals, mixed_ref, inner_ref, prob_ref, inv_ref, in_sems,
         out_sems, w_sems, save_sems, prob_sems) = refs[n_buf + 6 :]
        used = info_ref[2]
        fetches = []
        for part in range(3):
            rows = slice(part * D, (part + 1) * D)
            fetches.append(pltpu.make_async_copy(w_src.at[rows], w_vmem.at[rows], w_sems.at[part]))
            fetches[-1].start()
        start_in(codes_ref, n_units, in_bufs, x_in, in_sems.at[0])
        bias_low = bias_ref[...].astype(BF)
        lane = lax.broadcasted_iota(jnp.int32, (KEYS, 128), 1)
        for twin in range(2):
            keys[twin, :, 0:128] = jnp.zeros((2 * KEYS, 128), BF)
            keys[twin, :, 128:256] = marks_ref[...]
            vals[twin, :, 0:128] = jnp.zeros((2 * KEYS, 128), BF)
            vals[twin, 0:KEYS, 128:256] = (lane < 64).astype(BF)
            vals[twin, KEYS:, 128:256] = (lane >= 64).astype(BF)

        wait_all(x_in, in_sems.at[0])
        x = x_in[...].reshape(n_rows, D)
        saves = [pltpu.make_async_copy(x_in, win_out, save_sems.at[0])]
        inner = nt(x, down_ref[0]).astype(BF)
        inner_ref[...] = inner
        for part in range(3):
            cols = slice(part * D, (part + 1) * D)
            fetches[part].wait()
            mixed = nt(x, w_vmem[cols]) + bias_ref[:, cols] + nn(inner, up_ref[0, :, cols])
            mixed_ref[:, cols] = mixed.astype(BF)
        saves.append(pltpu.make_async_copy(mixed_ref, mixed_out, save_sems.at[1]))
        saves.append(pltpu.make_async_copy(inner_ref, inner_out, save_sems.at[2]))
        for save in saves:
            save.start()
        small = lax.broadcasted_iota(jnp.int32, (PITCH, 128), 1)
        low_half = lax.broadcasted_iota(jnp.int32, (TOK, 128), 1) < 64

        def attend(at, rows, slot):
            for j in range(PAIRS):
                twin = j % 2
                key, value = key_value(mixed_ref, bias_low, at, rows, j)
                fill_heads(keys.at[twin], key, low_half)
                fill_heads(vals.at[twin], value, low_half)
                cols = slice(128 * j, 128 * j + 128)
                q = mixed_ref[pl.ds(at, rows), cols]
                rel = nn(q, table_ref[...])
                pieces = []
                for x_at in range(rows // PITCH):
                    slab = rel[PITCH * x_at : PITCH * x_at + PITCH]
                    tall = pltpu.roll(slab, 113 + x_at, 1)
                    wide = pltpu.roll(slab, 113, 1, stride=1, stride_axis=0)
                    both = jnp.where(small % 64 < 32, tall, wide)
                    pieces.append(jnp.where(small == 14, 1.0, both).astype(BF))
                query = jnp.concatenate((q, jnp.concatenate(pieces, 0)), 1)
                scores = nt(query, keys[twin])
                probs = []
                for head in range(2):
                    part = scores[:, KEYS * head : KEYS * head + KEYS]
                    top = jnp.max(part, axis=-1, keepdims=True)
                    probs.append(jnp.exp(part - top).astype(BF))
                prob = jnp.concatenate(probs, 1)
                prob_ref[j, pl.ds(at, rows)] = prob
                summed = nn(prob, vals[twin])
                inverse = 1.0 / summed[:, 128:256]
                inv_ref[pl.ds(at, rows), cols] = inverse
                att = (summed[:, 0:128] * inverse).astype(BF)
                x_out[pl.ds(at // PITCH, rows // PITCH), :, cols] = att.reshape(
                    rows // PITCH, PITCH, 128
                )
            span = pl.ds(at, rows)
            pltpu.make_async_copy(prob_ref.at[:, span], prob_out.at[:, span],
                                  prob_sems.at[slot, 0]).start()
            pltpu.make_async_copy(inv_ref.at[span], inv_out.at[span], prob_sems.at[slot, 1]).start()
            start_out(codes_ref, at // PITCH, rows // PITCH, x_out, out_bufs, None, out_sems.at[0])

        each_slot(info_ref, plan, attend)
        start_out(codes_ref, used, n_units - used, x_out, out_bufs, plan["local"], out_sems.at[0])
        save = pltpu.make_async_copy(x_out, att_out, save_sems.at[3])
        save.start()

        def finish(at, rows, slot):
            span = pl.ds(at, rows)
            pltpu.make_async_copy(prob_ref.at[:, span], prob_out.at[:, span],
                                  prob_sems.at[slot, 0]).wait()
            pltpu.make_async_copy(inv_ref.at[span], inv_out.at[span], prob_sems.at[slot, 1]).wait()

        wait_all(x_out, out_sems.at[0])
        each_slot(info_ref, plan, finish)
        for one in saves + [save]:
            one.wait()

    saved = saved_shapes(plan)
    boxed = jax.ShapeDtypeStruct((n_units, PITCH, D), BF)
    results = pl.pallas_call(
        kernel,
        out_shape=outs + [boxed] + saved[1:5] + [boxed],
        grid_spec=pltpu.PrefetchScalarGridSpec(
            num_scalar_prefetch=2,
            grid=(1,),
            in_specs=any_specs(n_buf + 2)
            + [
                full_spec((1, 3 * D)),
                image_spec(down.shape, number),
                image_spec(up.shape, number),
                full_spec(table.shape),
                full_spec(marks.shape),
            ],
            out_specs=any_specs(n_buf + 6),
            scratch_shapes=[
                pltpu.VMEM((n_units, PITCH, D), BF),
                pltpu.VMEM((n_units, PITCH, D), BF),
                pltpu.VMEM((3 * D, D), BF),
                pltpu.VMEM((2, 2 * KEYS, 256), BF),
                pltpu.VMEM((2, 2 * KEYS, 256), BF),
                pltpu.VMEM((n_rows, 3 * D), BF),
                pltpu.VMEM((n_rows, RANK), BF),
                pltpu.VMEM((PAIRS, n_rows, 2 * KEYS), BF),
                pltpu.VMEM((n_rows, D), F32),
                pltpu.SemaphoreType.DMA((1,)),
                pltpu.SemaphoreType.DMA((1,)),
                pltpu.SemaphoreType.DMA((3,)),
                pltpu.SemaphoreType.DMA((4,)),
                pltpu.SemaphoreType.DMA((n_slots, 2)),
            ],
        ),
        cost_estimate=cost(10e9, 20e6, 4e6),
        compiler_params=params(),
        name="attention_forward",
    )(codes, info, *units, zero, weight, qkv_bias, down, up, table, marks)
    return results[:n_buf], results[n_buf:]


FF_KINDS = ("pd", "pu", "ed", "eu", "cd", "cu")
HALVES = (("eu", "pd", "pu", "ed", "cu"), ("cd",))
FF_WIDTHS = {"pd": D, "pu": D, "ed": D, "eu": FF, "cd": FF, "cu": D}


def stage_pieces(ranks):
    for h, kinds in enumerate(HALVES):
        at = 0
        for kind in kinds:
            wide = FF_WIDTHS[kind] // ranks
            yield h, at, wide, kind
            at += wide


def feed_forward(units, images, cotangent, number, row_count, weight_src, proj_copies,
                 expand_copies, contract_copies, vectors, adapter_src, adapter_index,
                 adapter_copies, place, codes, plan, rows_block, ranks, previous):
    side, steps, rows_spec = rows_plan(images, row_count, rows_block, number)
    per_step = rows_block * GRID
    tokens = rows_block * side
    outs = unit_shapes(plan)
    n_buf = len(outs)
    copies = [proj_copies, expand_copies, contract_copies]
    chunk = 512
    chunks = FF // chunk
    n_src = len(weight_src)
    stage_width = 2 * FF // ranks
    n_prev = len(previous)
    term_width = 3 * FF // ranks
    at_prev = 2 + n_buf + 2 + n_src + 5 + 4

    def kernel(codes_ref, pick_ref, *refs):
        in_bufs, refs = refs[:n_buf], refs[n_buf:]
        img_ref, cot_ref, refs = refs[0], refs[1], refs[2:]
        w_src, refs = refs[:n_src], refs[n_src:]
        (bp, g2, b2, be, bc), refs = refs[:5], refs[5:]
        a_src, place_ref, placet_ref, refs = refs[0:2], refs[2], refs[3], refs[4 + n_prev :]
        out_bufs, refs = refs[:n_buf], refs[n_buf:]
        block_ref, mid_ref, terms_ref, refs = refs[0], refs[1], refs[2], refs[3:]
        (pd, pu, ed, eu, cd, cu), refs = refs[:6], refs[6:]
        (d_pd, d_pu, d_ed, d_eu, d_cd, d_cu), refs = refs[:6], refs[6:]
        (u_in, u_out, wp, we, wc, stage_a, stage_b, acc_result, acc_second, in_sems, out_sems,
         w_sems, s_sems) = refs
        adapters = dict(zip(FF_KINDS, (pd, pu, ed, eu, cd, cu)))
        grads = dict(zip(FF_KINDS, (d_pd, d_pu, d_ed, d_eu, d_cd, d_cu)))
        step = pl.program_id(0)
        targets = [wp, we, wc]

        def weights(which):
            for src, dst in copies[which]:
                pltpu.make_async_copy(
                    w_src[which].at[src], targets[which].at[dst], w_sems.at[which]
                ).start()

        @pl.when(step == 0)
        def _():
            stages = (stage_a, stage_b)
            for half, src, dst in adapter_copies(pick_ref[number]):
                pltpu.make_async_copy(a_src[half].at[src], stages[half].at[dst],
                                      s_sems.at[half]).start()
            start_in(codes_ref, row_count * GRID, in_bufs, u_in, in_sems.at[0])
            for which in range(3):
                weights(which)
            for grad in grads.values():
                grad[...] = jnp.zeros_like(grad)
            wait_all(stage_a, s_sems.at[0])
            wait_all(stage_b, s_sems.at[1])
            for h, at, wide, kind in stage_pieces(ranks):
                for r in range(ranks):
                    adapters[kind][:, wide * r : wide * r + wide] = stages[h][
                        r, :, at : at + wide
                    ]
            wait_all(wp, w_sems.at[0])
            wait_all(u_in, in_sems.at[0])

        rows = []
        for r in range(rows_block):
            spread = u_in[pl.ds(step * per_step + r * GRID, GRID)].reshape(GRID * PITCH, D)
            rows.append(nn(placet_ref[...], spread).astype(BF))
        att = jnp.concatenate(rows, 0)
        cot = cot_ref[...].reshape(tokens, D)
        p_inner = nt(att, pd[...]).astype(BF)
        middle = (
            img_ref[...].reshape(tokens, D).astype(F32)
            + nt(att, wp[...])
            + bp[...]
            + nn(p_inner, pu[...])
        )
        standard, inverse = norm_parts(middle)
        second = (standard * g2[...] + b2[...]).astype(BF)
        e_inner = nt(second, ed[...]).astype(BF)
        c_mid = nt(cot, cu[...]).astype(BF)
        c_inner = jnp.zeros((tokens, RANK), F32)
        e_mid = jnp.zeros((tokens, RANK), F32)

        @pl.when(step == 0)
        def _():
            wait_all(we, w_sems.at[1])
            wait_all(wc, w_sems.at[2])

        acc_result[...] = middle + bc[...]
        acc_second[...] = jnp.zeros((tokens, D), F32)

        def one_chunk(n, carry):
            c_inner, e_mid = carry
            cols = pl.ds(pl.multiple_of(n * chunk, chunk), chunk)
            hidden = nn(second, we[:, cols]) + be[:, cols] + nn(e_inner, eu[:, cols])
            cdf = 0.5 * (1.0 + lax.erf(hidden * SQRT_HALF))
            slope = cdf + hidden * jnp.exp(-0.5 * hidden * hidden) * INV_SQRT_TAU
            active = (hidden * cdf).astype(BF)
            a_grad = nn(cot, wc[:, cols]) + nn(c_mid, cd[:, cols])
            h_grad = (a_grad * slope).astype(BF)
            acc_result[...] += nt(active, wc[:, cols])
            c_inner = c_inner + nt(active, cd[:, cols])
            acc_second[...] += nt(h_grad, we[:, cols])
            e_mid = e_mid + nt(h_grad, eu[:, cols])
            d_cd[:, cols] += tn(c_mid, active)
            d_eu[:, cols] += tn(e_inner, h_grad)
            return c_inner, e_mid

        c_inner, e_mid = lax.fori_loop(0, chunks, one_chunk, (c_inner, e_mid))
        result = acc_result[...]
        second_grad = acc_second[...]
        c_inner = c_inner.astype(BF)
        e_mid = e_mid.astype(BF)
        result = result + nn(c_inner, cu[...])
        block_ref[...] = result.astype(BF).reshape(rows_block, side, D)
        d_cu[...] += tn(c_inner, cot)
        d_ed[...] += tn(e_mid, second)
        second_grad = second_grad + nn(e_mid, ed[...])
        middle_grad = cot.astype(F32) + norm_back(second_grad, standard, inverse, g2[...])
        mid_ref[...] = middle_grad.reshape(rows_block, side, D)
        branch = middle_grad.astype(BF)
        p_mid = nt(branch, pu[...]).astype(BF)
        d_pu[...] += tn(p_inner, branch)
        d_pd[...] += tn(p_mid, att)
        att_grad = (nn(branch, wp[...]) + nn(p_mid, pd[...])).astype(BF)
        for r in range(rows_block):
            spread = nn(place_ref[...], att_grad[r * side : (r + 1) * side])
            u_out[pl.ds(step * per_step + r * GRID, GRID)] = spread.astype(BF).reshape(
                GRID, PITCH, D
            )
        start_out(codes_ref, step * per_step, per_step, u_out, out_bufs, None, out_sems.at[0])

        @pl.when(step == steps - 1)
        def _():
            at = 0
            for kind in FF_KINDS:
                wide = FF_WIDTHS[kind] // ranks
                for r in range(ranks):
                    terms_ref[r, :, at : at + wide] = grads[kind][
                        :, wide * r : wide * r + wide
                    ].astype(BF)
                at += wide
            if at < term_width:
                terms_ref[:, :, at:] = jnp.zeros((ranks, RANK, term_width - at), BF)
            wait_all(u_out, out_sems.at[0])

    results = pl.pallas_call(
        kernel,
        out_shape=outs
        + [
            jax.ShapeDtypeStruct(images.shape, BF),
            jax.ShapeDtypeStruct((row_count, side, D), F32),
            jax.ShapeDtypeStruct((ranks, images.shape[0] // row_count * RANK, term_width), BF),
        ],
        grid_spec=pltpu.PrefetchScalarGridSpec(
            num_scalar_prefetch=2,
            grid=(steps,),
            in_specs=any_specs(n_buf)
            + [rows_spec, rows_spec]
            + any_specs(n_src)
            + [full_spec(v.shape) for v in vectors]
            + any_specs(2)
            + [full_spec(place.shape), full_spec(place.shape[::-1])]
            + any_specs(n_prev),
            out_specs=any_specs(n_buf)
            + [
                rows_spec,
                pl.BlockSpec((rows_block, side, D), lambda i, *_: (i, 0, 0)),
                pl.BlockSpec((ranks, RANK, term_width), lambda *_: (0, number, 0)),
            ],
            scratch_shapes=[pltpu.VMEM((RANK, FF_WIDTHS[k]), BF) for k in FF_KINDS]
            + [pltpu.VMEM((RANK, FF_WIDTHS[k]), F32) for k in FF_KINDS]
            + [
                pltpu.VMEM((row_count * GRID, PITCH, D), BF),
                pltpu.VMEM((row_count * GRID, PITCH, D), BF),
                pltpu.VMEM((D, D), BF),
                pltpu.VMEM((D, FF), BF),
                pltpu.VMEM((D, FF), BF),
                pltpu.VMEM((ranks, RANK, stage_width), BF),
                pltpu.VMEM((ranks, RANK, FF // ranks), BF),
                pltpu.VMEM((tokens, D), F32),
                pltpu.VMEM((tokens, D), F32),
                pltpu.SemaphoreType.DMA((1,)),
                pltpu.SemaphoreType.DMA((1,)),
                pltpu.SemaphoreType.DMA((3,)),
                pltpu.SemaphoreType.DMA((2,)),
            ],
        ),
        input_output_aliases={at_prev: n_buf, at_prev + 1: n_buf + 2} if n_prev else {},
        cost_estimate=cost(18e9, 20e6, 4e6),
        compiler_params=params(),
        name="feed_forward",
    )(codes, adapter_index, *units, images, cotangent, *weight_src, *vectors, *adapter_src, place,
      place.T, *previous)
    return results[:n_buf], results[n_buf], results[n_buf + 1], results[n_buf + 2]


def attention_backward(units, zero, weight, saved, qkv_bias, down, up, number, table, marks, codes,
                       info, plan, ranks, image_count, previous):
    outs = unit_shapes(plan)
    n_buf = len(outs)
    n_units = plan["units"]
    n_rows = n_units * PITCH
    n_slots = plan["full"] + plan["short"]
    term_width = 4 * D // ranks

    def kernel(codes_ref, info_ref, *refs):
        in_bufs, refs = refs[: n_buf + 1], refs[n_buf + 1 :]
        w_src, refs = refs[0], refs[1:]
        (win_src, mixed_src, inner_src, prob_src, inv_src, att_src), refs = refs[:6], refs[6:]
        bias_ref, down_ref, up_ref, table_ref, marks_ref = refs[:5]
        refs = refs[5 + len(previous) :]
        out_bufs, refs = refs[:n_buf], refs[n_buf:]
        terms_ref, refs = refs[0], refs[1:]
        (g_in, x_out, w_vmem, keys, vals, grads, win_ref, mixed_ref, inner_ref, prob_ref, inv_ref,
         att_ref, in_sems, out_sems, load_sems, prob_sems) = refs
        used = info_ref[2]
        start_in(codes_ref, n_units, in_bufs, g_in, in_sems.at[0])
        loads = [
            pltpu.make_async_copy(src, dst, load_sems.at[n])
            for n, (src, dst) in enumerate(
                ((mixed_src, mixed_ref), (att_src, att_ref), (inner_src, inner_ref),
                 (win_src, win_ref), (w_src, w_vmem)))
        ]

        def slot_loads(at, rows, slot):
            span = pl.ds(at, rows)
            return (
                pltpu.make_async_copy(prob_src.at[:, span], prob_ref.at[:, span],
                                      prob_sems.at[slot, 0]),
                pltpu.make_async_copy(inv_src.at[span], inv_ref.at[span], prob_sems.at[slot, 1]),
            )

        def begin(at, rows, slot):
            for copy in slot_loads(at, rows, slot):
                copy.start()

        for load in loads[:2]:
            load.start()
        each_slot(info_ref, plan, begin)
        for load in loads[2:]:
            load.start()
        bias_low = bias_ref[...].astype(BF)
        for twin in range(2):
            keys[twin, :, 0:128] = jnp.zeros((2 * KEYS, 128), BF)
            keys[twin, :, 128:256] = marks_ref[...]
            vals[twin] = jnp.zeros((2 * KEYS, 128), BF)

        def clear(unit, carry):
            grads[pl.ds(pl.multiple_of(unit * PITCH, PITCH), PITCH)] = jnp.zeros((PITCH, 3 * D), BF)
            return carry

        lax.fori_loop(used, n_units, clear, 0)
        loads[0].wait()
        loads[1].wait()
        wait_all(g_in, in_sems.at[0])
        small = lax.broadcasted_iota(jnp.int32, (PITCH, 128), 1)
        low_half = lax.broadcasted_iota(jnp.int32, (TOK, 128), 1) < 64

        def attend(at, rows, slot):
            for copy in slot_loads(at, rows, slot):
                copy.wait()
            span = pl.ds(at, rows)
            half = low_half[:rows]
            for j in range(PAIRS):
                twin = j % 2
                cols = slice(128 * j, 128 * j + 128)
                key, value = key_value(mixed_ref, bias_low, at, rows, j)
                fill_heads(keys.at[twin], key, low_half)
                fill_heads(vals.at[twin], value, low_half)
                q = mixed_ref[span, cols]
                units_at = pl.ds(at // PITCH, rows // PITCH)
                grad = g_in[units_at, :, cols].reshape(rows, 128).astype(F32) * inv_ref[span, cols]
                grad_low = grad.astype(BF)
                weighed = grad * att_ref[units_at, :, cols].reshape(rows, 128).astype(F32)
                total = jnp.sum(weighed, axis=-1, keepdims=True)
                dot_a = jnp.sum(jnp.where(half, weighed, 0.0), axis=-1, keepdims=True)
                dots = (dot_a, total - dot_a)
                soft = nt(grad_low, vals[twin])
                pieces = []
                for head in range(2):
                    lanes = slice(KEYS * head, KEYS * head + KEYS)
                    prob = prob_ref[j, span, lanes].astype(F32)
                    pieces.append((prob * (soft[:, lanes] - dots[head])).astype(BF))
                both = nn(jnp.concatenate(pieces, 1), keys[twin])
                rel = both[:, 128:256]
                unrolled = []
                for x_at in range(rows // PITCH):
                    slab = rel[PITCH * x_at : PITCH * x_at + PITCH]
                    tall = pltpu.roll(slab, x_at, 1) if x_at else slab
                    wide = pltpu.roll(slab, 0, 1, stride=1, stride_axis=0)
                    unrolled.append(jnp.where(small % 64 < 32, tall, wide).astype(BF))
                q_grad = both[:, 0:128] + nn(jnp.concatenate(unrolled, 0), table_ref[...])
                grads[span, cols] = q_grad.astype(BF)
                q_t = q.T
                g_t = grad_low.T
                k_parts = []
                v_parts = []
                for head in range(2):
                    lanes = slice(KEYS * head, KEYS * head + KEYS)
                    own = slice(64 * head, 64 * head + 64)
                    k_parts.append(nn(q_t[own], pieces[head]))
                    v_parts.append(nn(g_t[own], prob_ref[j, span, lanes]))
                k_grad = jnp.concatenate(k_parts, 0).T[:rows] * HEAD_DIM ** -0.5
                v_grad = jnp.concatenate(v_parts, 0).T[:rows]
                grads[span, D + 128 * j : D + 128 * j + 128] = k_grad.astype(BF)
                grads[span, 2 * D + 128 * j : 2 * D + 128 * j + 128] = v_grad.astype(BF)

        each_slot(info_ref, plan, attend)
        for load in loads[2:]:
            load.wait()
        mixed_grad = grads[...]
        mid = nt(mixed_grad, up_ref[0]).astype(BF)
        normed = nn(mixed_grad, w_vmem[...]) + nn(mid, down_ref[0])
        x_out[...] = normed.astype(BF).reshape(n_units, PITCH, D)
        start_out(codes_ref, 0, n_units, x_out, out_bufs, plan["local"], out_sems.at[0])
        d_up = tn(inner_ref[...], mixed_grad).astype(BF)
        d_down = tn(mid, win_ref[...].reshape(n_rows, D)).astype(BF)
        at = 0
        for value, wide in ((d_down, D // ranks), (d_up, 3 * D // ranks)):
            for r in range(ranks):
                terms_ref[r, :, at : at + wide] = value[:, wide * r : wide * r + wide]
            at += wide
        wait_all(x_out, out_sems.at[0])

    results = pl.pallas_call(
        kernel,
        out_shape=outs + [jax.ShapeDtypeStruct((ranks, image_count * RANK, term_width), BF)],
        grid_spec=pltpu.PrefetchScalarGridSpec(
            num_scalar_prefetch=2,
            grid=(1,),
            in_specs=any_specs(n_buf + 8)
            + [full_spec((1, 3 * D)), image_spec(down.shape, number), image_spec(up.shape, number),
               full_spec(table.shape), full_spec(marks.shape)] + any_specs(len(previous)),
            out_specs=any_specs(n_buf)
            + [pl.BlockSpec((ranks, RANK, term_width), lambda *_: (0, number, 0))],
            scratch_shapes=[
                pltpu.VMEM((n_units, PITCH, D), BF),
                pltpu.VMEM((n_units, PITCH, D), BF),
                pltpu.VMEM((3 * D, D), BF),
                pltpu.VMEM((2, 2 * KEYS, 256), BF),
                pltpu.VMEM((2, 2 * KEYS, 128), BF),
                pltpu.VMEM((n_rows, 3 * D), BF),
                pltpu.VMEM((n_units, PITCH, D), BF),
                pltpu.VMEM((n_rows, 3 * D), BF),
                pltpu.VMEM((n_rows, RANK), BF),
                pltpu.VMEM((PAIRS, n_rows, 2 * KEYS), BF),
                pltpu.VMEM((n_rows, D), F32),
                pltpu.VMEM((n_units, PITCH, D), BF),
                pltpu.SemaphoreType.DMA((1,)),
                pltpu.SemaphoreType.DMA((1,)),
                pltpu.SemaphoreType.DMA((5,)),
                pltpu.SemaphoreType.DMA((n_slots, 2)),
            ],
        ),
        input_output_aliases={2 + n_buf + 8 + 5: n_buf} if previous else {},
        cost_estimate=cost(12e9, 20e6, 4e6),
        compiler_params=params(),
        name="attention_backward",
    )(codes, info, *units, zero, weight, *saved, qkv_bias, down, up, table, marks, *previous)
    return results[:n_buf], results[n_buf]


def first_norm_back(units, images, middle_grad, number, row_count, gain, place_t, codes, plan,
                    rows_block, previous):
    side, steps, rows_spec = rows_plan(images, row_count, rows_block, number)
    per_step = rows_block * GRID
    n_buf = len(units)
    n_prev = len(previous)

    def kernel(codes_ref, *refs):
        in_bufs, refs = refs[:n_buf], refs[n_buf:]
        x_ref, m_ref, g_ref, p_ref, refs = refs[0], refs[1], refs[2], refs[3], refs[4 + n_prev :]
        out_ref, u_in, sems = refs
        step = pl.program_id(0)

        @pl.when(step == 0)
        def _():
            start_in(codes_ref, row_count * GRID, in_bufs, u_in, sems.at[0])

        values = x_ref[...].reshape(rows_block * side, D).astype(F32)
        standard, inverse = norm_parts(values)

        @pl.when(step == 0)
        def _():
            wait_all(u_in, sems.at[0])

        rows = []
        for r in range(rows_block):
            spread = u_in[pl.ds(step * per_step + r * GRID, GRID)].reshape(GRID * PITCH, D)
            rows.append(nn(p_ref[...], spread))
        upstream = jnp.concatenate(rows, 0)
        back = norm_back(upstream, standard, inverse, g_ref[...])
        out_ref[...] = m_ref[...] + back.reshape(rows_block, side, D)

    return pl.pallas_call(
        kernel,
        out_shape=jax.ShapeDtypeStruct(images.shape, F32),
        grid_spec=pltpu.PrefetchScalarGridSpec(
            num_scalar_prefetch=1,
            grid=(steps,),
            in_specs=any_specs(n_buf)
            + [
                rows_spec,
                pl.BlockSpec((rows_block, side, D), lambda i, *_: (i, 0, 0)),
                full_spec((1, D)),
                full_spec(place_t.shape),
            ]
            + any_specs(n_prev),
            out_specs=rows_spec,
            scratch_shapes=[
                pltpu.VMEM((row_count * GRID, PITCH, D), BF),
                pltpu.SemaphoreType.DMA((1,)),
            ],
        ),
        input_output_aliases={1 + n_buf + 4: 0} if n_prev else {},
        cost_estimate=cost(1e9, 8e6),
        compiler_params=params(),
        name="first_norm_back",
    )(codes, *units, images, middle_grad, gain, place_t, *previous)


KINDS = ("qd", "qu", "pd", "pu", "ed", "eu", "cd", "cu")
WIDTHS = {"qd": D, "qu": 3 * D, "pd": D, "pu": D, "ed": D, "eu": FF, "cd": FF, "cu": D}


def packed_form(groups, ranks):
    return groups == 4 and ranks == 8


def shift_z(value, step):
    return lax.ppermute(value, "rows", [(r, (r + 2 * step) % 8) for r in range(8)])


def flip_y(value):
    return lax.ppermute(value, "rows", [(r, r ^ 1) for r in range(8)])


def flip_x(value):
    return lax.ppermute(value, "dp", [(d, d ^ 2) for d in range(4)])


def flip_core(value):
    return lax.ppermute(value, "dp", [(d, d ^ 1) for d in range(4)])


NQ, NP = 144, 48
MOVES = ((0, 0, 0), (0, 0, 1), (0, 1, 0), (0, 1, 1), (1, 0, 0), (1, 0, 1), (1, 1, 0), (1, 1, 1),
         (0, 0, 2), (0, 0, 3), (1, 0, 2), (1, 0, 3), (0, 1, 2), (0, 1, 3), (1, 1, 2), (1, 1, 3))


def piece_table():
    table = np.zeros((4, 8, 32), np.int32)
    for d in range(4):
        for r in range(8):
            for number, (kx, ky, kz) in enumerate(MOVES):
                for kc in range(2):
                    source_d = (d ^ (2 * kx)) ^ kc
                    source_r = ((r // 2 - kz) % 4) * 2 + ((r % 2) ^ ky)
                    table[d, r, source_r * 4 + source_d] = 16 * kc + number
    return table


def pack(qkv, proj, expand, contract, adapters):
    core = (lax.axis_index("dp") % 2).reshape(1)
    rows = qkv.shape[0]
    ne, nc = expand.shape[0] // 2, contract.shape[0]
    n_ad = len(adapters)
    lists = KINDS

    def kernel(core_ref, q_ref, p_ref, e_ref, c_ref, *refs):
        ads = dict(zip(lists, refs[:n_ad]))
        second, own, other, extra = refs[n_ad:]

        def turned(value):
            wide = value.shape[1]
            eye = (
                lax.broadcasted_iota(jnp.int32, (wide, wide), 0)
                == lax.broadcasted_iota(jnp.int32, (wide, wide), 1)
            )
            return nt(eye.astype(F32).astype(BF), value).astype(BF)

        q_t = turned(q_ref[...])
        p_t = turned(p_ref[...])
        for half, chosen in ((0, 0), (1, 1)):
            @pl.when(core_ref[0] == chosen)
            def _():
                own[0:NQ] = q_t[half * NQ : half * NQ + NQ]
                own[NQ:] = p_t[half * NP : half * NP + NP]
                other[0:NQ] = q_t[(1 - half) * NQ : (1 - half) * NQ + NQ]
                other[NQ:] = p_t[(1 - half) * NP : (1 - half) * NP + NP]

        second[0:ne, 0 : expand.shape[1]] = e_ref[0:ne]
        second[0:ne, expand.shape[1] :] = e_ref[ne:]
        second[ne : ne + nc] = c_ref[...]
        base = ne + nc
        for i in range(2):
            rows_i = slice(base + i * RANK, base + i * RANK + RANK)
            at = 0
            for kind in HALVES[0]:
                wide = ads[kind].shape[2]
                second[rows_i, at : at + wide] = ads[kind][i]
                at += wide
            wide = ads["cd"].shape[2]
            second[base + 2 * RANK :, i * wide : i * wide + wide] = ads["cd"][i]
            at = ads["qu"].shape[2]
            extra[i * RANK : i * RANK + RANK, 0:at] = ads["qu"][i]
            extra[i * RANK : i * RANK + RANK, at:] = ads["qd"][i]

    shapes = [(ne + nc + 3 * RANK, D), (NQ + NP, rows), (NQ + NP, rows), (2 * RANK, 384)]
    return pl.pallas_call(
        kernel,
        out_shape=[jax.ShapeDtypeStruct(shape, BF) for shape in shapes],
        grid_spec=pltpu.PrefetchScalarGridSpec(
            num_scalar_prefetch=1,
            grid=(1,),
            in_specs=[full_spec(v.shape) for v in (qkv, proj, expand, contract) + adapters],
            out_specs=[full_spec(shape) for shape in shapes],
        ),
        cost_estimate=cost(1e8, 2e6),
        compiler_params=params(),
        name="pack",
    )(core, qkv, proj, expand, contract, *adapters)


def first_piece(own, other, extra):
    core = lax.axis_index("dp") % 2
    other = flip_core(other)
    joined = jnp.where(
        core == 0, jnp.concatenate((own, other), 1), jnp.concatenate((other, own), 1)
    )
    return jnp.concatenate((joined, extra), 0)


def gather_first(piece, norms):
    line = jnp.stack([piece] + [shift_z(piece, k) for k in (1, 2, 3)])
    line = after(line, *norms)
    left, right = line[:2], line[2:]
    left = jnp.concatenate((left, flip_y(left)))
    right = jnp.concatenate((right, flip_x(right)))
    left, right = lax.optimization_barrier((left, right))
    pieces = jnp.concatenate((left, flip_x(left), right, flip_y(right)))
    return (left, right), pieces, flip_core(pieces), line


def assemble(pieces, others, table, adapter_index, image_count):
    def kernel(table_ref, pick_ref, a_ref, b_ref, wq, wp, down_ref, up_ref, stage, w_sems, s_sems):
        def fetch(block, src_rows, dst, sem):
            code = table_ref[block]
            index = code % 16

            @pl.when(code < 16)
            def _():
                pltpu.make_async_copy(a_ref.at[index, src_rows], dst, sem).start()

            @pl.when(code >= 16)
            def _():
                pltpu.make_async_copy(b_ref.at[index, src_rows], dst, sem).start()

        for n in range(image_count):
            chosen = pick_ref[n]
            rows = pl.ds(pl.multiple_of(NQ + NP + RANK * (chosen % 2), 16), RANK)
            for r in range(8):
                fetch(r * 4 + chosen // 2, rows, stage.at[n, r], s_sems.at[0])
        for r in range(8):
            for d in range(4):
                x, c = divmod(d, 2)
                lanes = slice(384 * x, 384 * x + 384)
                top = 2 * NQ * r + NQ * c
                fetch(r * 4 + d, slice(0, NQ), wq.at[top : top + NQ, lanes], w_sems.at[0])
                top = 2 * NP * r + NP * c
                fetch(r * 4 + d, slice(NQ, NQ + NP), wp.at[top : top + NP, lanes], w_sems.at[1])
        wait_all(stage, s_sems.at[0])
        for n in range(image_count):
            for r in range(8):
                up_ref[n, :, 288 * r : 288 * r + 288] = stage[n, r, :, 0:288]
                down_ref[n, :, 96 * r : 96 * r + 96] = stage[n, r, :, 288:384]
        wait_all(wq, w_sems.at[0])
        wait_all(wp, w_sems.at[1])

    return pl.pallas_call(
        kernel,
        out_shape=[
            jax.ShapeDtypeStruct((3 * D, D), BF),
            jax.ShapeDtypeStruct((D, D), BF),
            jax.ShapeDtypeStruct((image_count, RANK, D), BF),
            jax.ShapeDtypeStruct((image_count, RANK, 3 * D), BF),
        ],
        grid_spec=pltpu.PrefetchScalarGridSpec(
            num_scalar_prefetch=2,
            grid=(1,),
            in_specs=any_specs(2),
            out_specs=[
                full_spec((3 * D, D)),
                full_spec((D, D)),
                full_spec((image_count, RANK, D)),
                full_spec((image_count, RANK, 3 * D)),
            ],
            scratch_shapes=[
                pltpu.VMEM((image_count, 8, RANK, 384), BF),
                pltpu.SemaphoreType.DMA((2,)),
                pltpu.SemaphoreType.DMA((1,)),
            ],
        ),
        cost_estimate=cost(1e6, 10e6),
        compiler_params=params(),
        name="assemble",
    )(table, adapter_index, pieces, others)


def second_copies(groups, ranks):
    ne, nc = FF // (groups * ranks), D // ranks
    wide = FF // ranks
    expand, contract = [], []
    for r in range(ranks):
        for d in range(groups):
            b = r * groups + d
            for h in range(2):
                top = d * 2 * ne + h * ne
                expand.append(
                    (
                        (b, slice(0, ne), slice(h * wide, h * wide + wide)),
                        (slice(top, top + ne), slice(r * wide, r * wide + wide)),
                    )
                )
            contract.append(
                ((b, slice(ne, ne + nc)), (slice(nc * r, nc * r + nc), slice(D * d, D * d + D)))
            )
    return expand, contract, ne + nc


def second_adapters(base, groups, ranks):
    per_group = ADAPTERS // groups
    wide = FF // ranks

    def copies(chosen):
        found = []
        for r in range(ranks):
            block = r * groups + chosen // per_group
            own = chosen % per_group
            rows = pl.ds(pl.multiple_of(base + own * RANK, RANK), RANK)
            found.append((0, (block, rows), (r,)))
            rows = slice(base + 2 * RANK, base + 3 * RANK)
            found.append((1, (block, rows, pl.ds(pl.multiple_of(own * wide, 128), wide)), (r,)))
        return found

    return copies


def plain_stage(chosen, ranks):
    images = chosen[0].shape[0]
    lists = dict(zip(FF_KINDS, chosen))
    halves = []
    for kinds in HALVES:
        parts = [lists[k].reshape(images, RANK, ranks, -1).transpose(0, 2, 1, 3) for k in kinds]
        halves.append(jnp.concatenate(parts, 3))
    return [[half[n] for half in halves] for n in range(images)]


def gather_plain(weights, adapters, adapter_index):
    full = []
    for m in weights:
        m = lax.all_gather(m, "dp", axis=0, tiled=True)
        full.append(lax.all_gather(m, "rows", axis=1, tiled=True))
    qkv, proj, expand, contract = full
    chosen = []
    for m in adapters:
        m = lax.all_gather(m, "dp", axis=0, tiled=True)
        m = jnp.take(m, adapter_index[:, 0], axis=0)
        chosen.append(lax.all_gather(m, "rows", axis=2, tiled=True))
    return [qkv.T, proj.T, expand, contract.T], chosen


def rows_sum(packed):
    moved = lax.all_to_all(packed, "rows", split_axis=0, concat_axis=0, tiled=True)
    return jnp.sum(moved.astype(F32), axis=0)


def adapters_sum(sums, widths, adapter_index, groups):
    per_group = ADAPTERS // groups
    local = sums
    hit = (adapter_index[None, :] == jnp.arange(ADAPTERS)[:, None]).astype(F32)
    spread = jnp.sum(hit[:, :, None, None] * local[None], axis=1).astype(BF)
    spread = spread.reshape(groups, per_group, RANK, -1)
    moved = lax.all_to_all(spread, "dp", split_axis=0, concat_axis=0, tiled=True)
    total = jnp.sum(moved.astype(F32), axis=0)
    outs = []
    at = 0
    for wide in widths:
        outs.append(total[:, :, at : at + wide])
        at += wide
    return outs


def per_device(
    images, norm1_gain, norm1_bias, qkv_weight, qkv_bias, height_table, width_table, proj_weight,
    proj_bias, norm2_gain, norm2_bias, expand_weight, expand_bias, contract_weight, contract_bias,
    adapter_index, qkv_down, qkv_up, proj_down, proj_up, expand_down, expand_up, contract_down,
    contract_up, cotangent,
):
    image_count, row_count, side, _ = images.shape
    ranks = lax.axis_size("rows")
    groups = lax.axis_size("dp")
    rank = lax.axis_index("rows")
    plan = make_plan(ranks, row_count, 1)
    packed = packed_form(groups, ranks)
    pieces_at = piece_table() if packed else np.zeros((groups, ranks, 1), np.int32)
    tables = [np.broadcast_to(plan[k][None], (groups,) + plan[k].shape)
              for k in ("rows", "wins", "info")] + [pieces_at]
    ends = np.cumsum([0] + [t.shape[2] for t in tables])
    mine = jnp.asarray(np.concatenate(tables, 2))[lax.axis_index("dp"), rank]
    rows_code, win_code, info, piece_code = [mine[a:b] for a, b in zip(ends[:-1], ends[1:])]
    rows_block = 4 if row_count % 4 == 0 else row_count
    ff_block = row_count
    place = jnp.asarray(place_matrix(side), BF)
    marks_fwd, marks_bwd = [jnp.asarray(m, BF) for m in key_marks()]
    table_fwd, table_bwd = pair_tables(height_table, width_table)
    zero = jnp.zeros((1, PITCH, D), BF)
    row_vector = lambda v: v.reshape(1, -1)
    picked = adapter_index[:, 0]
    flat_images = images.reshape(image_count * row_count, side, D)
    flat_cotangent = cotangent.reshape(image_count * row_count, side, D)

    adapters = (qkv_down, qkv_up, proj_down, proj_up, expand_down, expand_up, contract_down,
                contract_up)
    whole = [((slice(None),), (slice(None),))]
    gain_one, bias_one = row_vector(norm1_gain), row_vector(norm1_bias)
    split = range(image_count)
    if packed:
        second, own, other, extra = pack(qkv_weight, proj_weight, expand_weight,
                                         contract_weight.T, adapters)
        piece = first_piece(own, other, extra)
        gain_one = after(gain_one, piece)
    sent = [first_norm(flat_images, n, row_count, gain_one, bias_one, place, rows_code, plan,
                       rows_block) for n in split]
    if packed:
        ready, pieces, others, line = gather_first(piece, [v[0] for v in sent])
        second = lax.all_gather(after(second, line), ("rows", "dp"), axis=0, tiled=False)
        units = [exchange([after(v, *ready) for v in sent[n]], plan, False) for n in split]
        others = after(others, *units[0])
        qkv_full, proj_full, down_one, up_one = assemble(pieces, others, piece_code, picked,
                                                         image_count)
        expand_copies, contract_copies, base = second_copies(groups, ranks)
        adapter_copies = second_adapters(base, groups, ranks)
        ff_src = [proj_full, second, second]
        adapter_src = [[second, second]] * image_count
    else:
        units = [exchange(sent[n], plan, False) for n in split]
        weights = (qkv_weight, proj_weight, expand_weight, contract_weight)
        full, chosen = gather_plain(weights, adapters, adapter_index)
        expand_copies = contract_copies = whole
        qkv_full = full[0]
        down_one, up_one = chosen[:2]
        ff_src = full[1:]
        everything = (slice(None),)
        adapter_copies = lambda index: [(h, everything, everything) for h in range(2)]
        adapter_src = plain_stage(chosen[2:], ranks)
    vectors = [row_vector(v) for v in (proj_bias, norm2_gain, norm2_bias, expand_bias,
                                       contract_bias)]
    forward = [attention_forward(units[n], zero, qkv_full, row_vector(qkv_bias), down_one, up_one,
                                 n, table_fwd, marks_fwd, win_code, info, plan) for n in split]
    units = [exchange(forward[n][0], plan, True) for n in split]
    ff = []
    for n in split:
        ff.append(feed_forward(units[n], flat_images, flat_cotangent, n, row_count, ff_src, whole,
                               expand_copies, contract_copies, vectors, adapter_src[n], picked,
                               adapter_copies, place, rows_code, plan, ff_block, ranks,
                               [v for f in ff[-1:] for v in (f[1], f[3])]))
    units = [exchange(ff[n][0], plan, False) for n in split]
    backward = []
    for n in split:
        backward.append(attention_backward(units[n], zero, qkv_full, forward[n][1],
                                           row_vector(qkv_bias), down_one, up_one, n, table_bwd,
                                           marks_bwd, win_code, info, plan, ranks, image_count,
                                           [b[1] for b in backward[-1:]]))
    units = [exchange(backward[n][0], plan, True) for n in split]
    early_sums = after(rows_sum(ff[-1][3]), backward[0][0][0]).reshape(image_count, RANK, -1)
    early = adapters_sum(early_sums, [FF_WIDTHS[k] // ranks for k in FF_KINDS], picked, groups)
    gain_one = after(gain_one, early[0])
    back = []
    for n in split:
        back.append(first_norm_back(units[n], flat_images, ff[n][2], n, row_count, gain_one,
                                    place.T, rows_code, plan, rows_block, back[-1:]))
    late_terms = after(backward[-1][1], back[0])
    late_sums = rows_sum(late_terms).reshape(image_count, RANK, -1)
    late = adapters_sum(late_sums, [D // ranks, 3 * D // ranks], picked, groups)
    return (ff[-1][1].reshape(images.shape), back[-1].reshape(images.shape), *late, *early)


def solution(mesh):
    whole = P()
    both = P("dp", "rows")
    adapter = P("dp", None, "rows")
    image = P("dp", "rows", None, None)
    placed = (image, whole, whole, both, whole, whole, whole, both, whole, whole, whole, both,
              whole, both, whole, P("dp", None), *([adapter] * 8), image)
    return jax.shard_map(
        per_device,
        mesh=mesh,
        in_specs=placed,
        out_specs=(image, image, *([adapter] * 8)),
        check_vma=False,
    )
```

```python
import itertools

import jax
import jax.numpy as jnp
import numpy as np
from jax import lax
from jax.experimental import pallas as pl
from jax.experimental.pallas import tpu as pltpu
from jax.sharding import PartitionSpec as P

HEAD_DIM = 64
WIN = 14
PITCH = 16
ADAPTERS = 8
RANK = 16
GRID = 5
D = 768
FF = 3072
HEADS = 12
PAIRS = HEADS // 2
TOK = WIN * PITCH
KEYS = 256
EPSILON = 1e-06
SQRT_HALF = 0.7071067811865476
INV_SQRT_TAU = 0.3989422804014327
SHIFT = 1024
SHORT = 8
CUT = SHORT * PITCH
BF = jnp.bfloat16
F32 = jnp.float32
VMEM_LIMIT = 60 * 1024 * 1024


def choose_owner(ranks, row_count, images):
    side_rows = ranks * row_count
    total = GRID * GRID * images
    weight = np.array(
        [0.77 if side_rows - (w // (GRID * images)) * WIN <= SHORT else 1.0 for w in range(total)]
    )

    def owner_of(cuts):
        return np.repeat(np.arange(ranks), np.diff([0] + list(cuts) + [total]))

    def cost_of(cuts):
        if min(np.diff([0] + list(cuts) + [total])) < 0:
            return 1e9
        owner = owner_of(cuts)
        load = np.bincount(owner, weights=weight, minlength=ranks).max()
        return 12.0 * load + color_edges(owner, ranks, row_count, images)[0]

    def filled(limit):
        cuts, load = [], 0.0
        for window in range(total):
            if load + weight[window] > limit + 1e-9:
                cuts.append(window)
                load = 0.0
            load += weight[window]
        return cuts + [total] * (ranks - 1 - len(cuts))

    limits = sorted({weight[a:b].sum() for a in range(total) for b in range(a + 1, total + 1)})
    least = next(limit for limit in limits if len(filled(limit)) == ranks - 1)
    reach = np.cumsum(weight) / weight.sum() * ranks
    even = [int(np.searchsorted(reach, r - 0.5)) for r in range(1, ranks)]
    found = (1e10, None)
    for cuts in (filled(least), even):
        best = cost_of(cuts)
        for _ in range(12):
            moved = False
            for place in range(ranks - 1):
                for width in (1, 2, 3):
                    for step in (-1, 1):
                        trial = list(cuts)
                        for extra in range(width):
                            if place + extra < ranks - 1:
                                trial[place + extra] += step
                        cost = cost_of(trial)
                        if cost < best - 1e-9:
                            best, cuts, moved = cost, trial, True
            if not moved:
                break
        if best < found[0] - 1e-9:
            found = (best, list(cuts))
    return owner_of(found[1])


def color_edges(owner, ranks, row_count, images):
    edges = {}
    local = [[] for _ in range(ranks)]
    for rank in range(ranks):
        for img in range(images):
            for k in range(row_count):
                row = rank * row_count + k
                for col in range(GRID):
                    window = (row // WIN) * images * GRID + img * GRID + col
                    unit = (img, k, col, window, row % WIN)
                    if owner[window] == rank:
                        local[rank].append(unit)
                    else:
                        edges.setdefault((rank, int(owner[window])), []).append(unit)
    colors = []
    for (src, dst), units in sorted(edges.items(), key=lambda e: (-len(e[1]), e[0])):
        for color in colors:
            if src not in color["src"] and dst not in color["dst"]:
                break
        else:
            color = {"src": set(), "dst": set(), "pairs": [], "units": []}
            colors.append(color)
        color["src"].add(src)
        color["dst"].add(dst)
        color["pairs"].append((src, dst))
        color["units"].append(units)
    sizes = [max(len(u) for u in c["units"]) for c in colors]
    cost = 0.4 * sum(sizes) + 3.0 * len(sizes)
    return cost, local, colors, sizes


def make_plan(ranks, row_count, images):
    total = GRID * GRID * images
    owner = choose_owner(ranks, row_count, images)
    _, local, colors, sizes = color_edges(owner, ranks, row_count, images)
    kinds = [ranks * row_count - w // (images * GRID) * WIN <= SHORT for w in range(total)]
    heights = [SHORT if short else WIN for short in kinds]
    most = int(np.bincount(owner, weights=heights, minlength=ranks).max())
    full_most = int(np.bincount(owner, weights=~np.array(kinds), minlength=ranks).max())
    short_most = int(np.bincount(owner, weights=np.array(kinds), minlength=ranks).max())
    skip = (len(colors) + 1) * SHIFT
    rows_code = np.full((ranks, images, row_count, GRID), skip, np.int32)
    win_code = np.full((ranks, most), skip, np.int32)
    first = np.searchsorted(owner, np.arange(ranks))

    def put(rank, unit, code, dst):
        img, k, col, window, place = unit
        rows_code[rank, img, k, col] = code
        win_code[dst, sum(heights[first[dst] : window]) + place] = code

    for rank in range(ranks):
        for number, unit in enumerate(local[rank]):
            put(rank, unit, number, rank)
    for which, color in enumerate(colors):
        for (src, dst), units in zip(color["pairs"], color["units"]):
            for number, unit in enumerate(units):
                put(src, unit, (which + 1) * SHIFT + number, dst)
    slot_info = np.zeros((ranks, 3), np.int32)
    for rank in range(ranks):
        mine = [kinds[w] for w in np.flatnonzero(owner == rank)]
        slot_info[rank] = (mine.count(False), mine.count(True),
                           sum(SHORT if short else WIN for short in mine))
    return {
        "rows": rows_code.reshape(ranks, -1),
        "wins": win_code,
        "info": slot_info,
        "units": most,
        "full": full_most,
        "short": short_most,
        "local": max(max(len(u) for u in local), 1),
        "sizes": sizes,
        "pairs": [c["pairs"] for c in colors],
    }


def place_matrix(side):
    out = np.zeros((GRID * PITCH, side), np.float32)
    for token in range(side):
        out[token // WIN * PITCH + token % WIN, token] = 1.0
    return out


def key_marks():
    fwd = np.zeros((2 * KEYS, 128), np.float32)
    bwd = np.zeros((2 * KEYS, 128), np.float32)
    for head in range(2):
        for key in range(KEYS):
            row = head * KEYS + key
            u, w = divmod(key, PITCH)
            if key >= TOK or w >= WIN:
                fwd[row, 14] = -1e30
                continue
            base = 64 * head
            for lane in (base + u, base + 32 + w):
                fwd[row, lane] = 1.0
            bwd[row, base + 13 - u] = 1.0
            bwd[row, base + 32 + 13 - w] = 1.0
    return fwd, bwd


def pair_tables(height_table, width_table):
    rev = jnp.pad(jnp.stack((height_table[::-1], width_table[::-1])), ((0, 0), (2, 3), (0, 0)))
    half = rev.reshape(64, HEAD_DIM).T
    zero = jnp.zeros_like(half)
    fwd = jnp.concatenate(
        (jnp.concatenate((half, zero), 1), jnp.concatenate((zero, half), 1)), 0
    )
    straight = jnp.pad(jnp.stack((height_table, width_table)), ((0, 0), (0, 5), (0, 0)))
    back = straight.reshape(64, HEAD_DIM)
    blank = jnp.zeros_like(back)
    bwd = jnp.concatenate(
        (jnp.concatenate((back, blank), 1), jnp.concatenate((blank, back), 1)), 0
    )
    return fwd, bwd


def nn(a, b):
    return lax.dot_general(a, b, (((1,), (0,)), ((), ())), preferred_element_type=F32)


def nt(a, b):
    return lax.dot_general(a, b, (((1,), (1,)), ((), ())), preferred_element_type=F32)


def tn(a, b):
    return lax.dot_general(a, b, (((0,), (0,)), ((), ())), preferred_element_type=F32)


def start_in(codes, count, bufs, dst, sem):
    def body(u, carry):
        code = codes[u]
        which = code // SHIFT
        index = code % SHIFT
        for number, buf in enumerate(bufs):
            @pl.when(which == number)
            def _():
                pltpu.make_async_copy(buf.at[index], dst.at[u], sem).start()
        return carry

    lax.fori_loop(0, count, body, 0)


def start_out(codes, first, count, src, bufs, spare, sem):
    def body(u, carry):
        code = codes[u]
        which = code // SHIFT
        index = code % SHIFT
        for number, buf in enumerate(bufs):
            @pl.when(which == number)
            def _():
                pltpu.make_async_copy(src.at[u], buf.at[index], sem).start()

        if spare is not None:
            @pl.when(which >= len(bufs))
            def _():
                pltpu.make_async_copy(src.at[u], bufs[0].at[spare + u], sem).start()
        return carry

    lax.fori_loop(first, first + count, body, 0)


def wait_all(whole, sem):
    pltpu.make_async_copy(whole, whole, sem).wait()


def norm_parts(values):
    average = jnp.mean(values, axis=-1, keepdims=True)
    centred = values - average
    variance = jnp.mean(centred * centred, axis=-1, keepdims=True)
    inverse = lax.rsqrt(variance + EPSILON)
    return centred * inverse, inverse


def norm_back(upstream, standard, inverse, gain):
    scaled = upstream * gain
    first_term = jnp.mean(scaled, axis=-1, keepdims=True)
    second_term = jnp.mean(scaled * standard, axis=-1, keepdims=True)
    return inverse * (scaled - first_term - standard * second_term)


def any_specs(count):
    return [pl.BlockSpec(memory_space=pl.ANY)] * count


def full_spec(shape):
    return pl.BlockSpec(shape, lambda *_: (0,) * len(shape))


def unit_shapes(plan):
    counts = [plan["local"] + plan["units"]] + plan["sizes"]
    return [jax.ShapeDtypeStruct((n, PITCH, D), BF) for n in counts]


def after(value, *others):
    return lax.optimization_barrier((value, *others))[0]


def exchange(bufs, plan, back):
    moved = [bufs[0]]
    for buf, pairs in zip(bufs[1:], plan["pairs"]):
        pairs = [(b, a) for a, b in pairs] if back else list(pairs)
        moved.append(lax.ppermute(buf, "rows", pairs))
    return moved


def cost(flops, moved, special=0):
    return pl.CostEstimate(flops=int(flops), bytes_accessed=int(moved), transcendentals=int(special))


def params():
    return pltpu.CompilerParams(vmem_limit_bytes=VMEM_LIMIT)


def rows_plan(images, row_count, rows_block, number):
    side = images.shape[1]
    steps = row_count // rows_block
    spec = pl.BlockSpec((rows_block, side, D), lambda i, *_: (number * steps + i, 0, 0))
    return side, steps, spec


def first_norm(images, number, row_count, gain, bias, place, codes, plan, rows_block):
    side, steps, rows_spec = rows_plan(images, row_count, rows_block, number)
    per_step = rows_block * GRID
    outs = unit_shapes(plan)

    def kernel(codes_ref, x_ref, g_ref, b_ref, p_ref, *rest):
        bufs, scratch, sems = rest[: len(outs)], rest[len(outs)], rest[len(outs) + 1]
        step = pl.program_id(0)
        values = x_ref[...].reshape(rows_block * side, D).astype(F32)
        standard, _ = norm_parts(values)
        normed = (standard * g_ref[...] + b_ref[...]).astype(BF)
        for r in range(rows_block):
            spread = nn(p_ref[...], normed[r * side : (r + 1) * side])
            scratch[pl.ds(step * per_step + r * GRID, GRID)] = spread.astype(BF).reshape(
                GRID, PITCH, D
            )
        start_out(codes_ref, step * per_step, per_step, scratch, bufs, None, sems.at[0])

        @pl.when(step == steps - 1)
        def _():
            wait_all(scratch, sems.at[0])

    return pl.pallas_call(
        kernel,
        out_shape=outs,
        grid_spec=pltpu.PrefetchScalarGridSpec(
            num_scalar_prefetch=1,
            grid=(steps,),
            in_specs=[rows_spec, full_spec((1, D)), full_spec((1, D)), full_spec(place.shape)],
            out_specs=any_specs(len(outs)),
            scratch_shapes=[
                pltpu.VMEM((row_count * GRID, PITCH, D), BF),
                pltpu.SemaphoreType.DMA((1,)),
            ],
        ),
        cost_estimate=cost(1e9, 8e6),
        compiler_params=params(),
        name="first_norm",
    )(codes, images, gain, bias, place)


def image_spec(shape, number):
    return pl.BlockSpec((1,) + shape[1:], lambda *_: (number,) + (0,) * (len(shape) - 1))


def saved_shapes(plan):
    rows = plan["units"] * PITCH
    return [
        jax.ShapeDtypeStruct((rows, D), BF),
        jax.ShapeDtypeStruct((rows, 3 * D), BF),
        jax.ShapeDtypeStruct((rows, RANK), BF),
        jax.ShapeDtypeStruct((PAIRS, rows, 2 * KEYS), BF),
        jax.ShapeDtypeStruct((rows, D), F32),
        jax.ShapeDtypeStruct((rows, D), BF),
    ]


def each_slot(info_ref, plan, body):
    n_full = info_ref[0]
    if plan["full"]:
        def full(slot, carry):
            body(pl.multiple_of(slot * TOK, 32), TOK, slot)
            return carry

        lax.fori_loop(0, n_full, full, 0)
    if plan["short"]:
        def short(slot, carry):
            body(pl.multiple_of(n_full * TOK + slot * CUT, 32), CUT, n_full + slot)
            return carry

        lax.fori_loop(0, info_ref[1], short, 0)


def key_value(mixed_ref, bias_low, at, rows, j):
    out = []
    for part in (1, 2):
        cols = slice(part * D + 128 * j, part * D + 128 * j + 128)
        own = mixed_ref[pl.ds(at, rows), cols]
        if rows < TOK:
            rest = jnp.broadcast_to(bias_low[:, cols], (TOK - rows, 128))
            own = jnp.concatenate((own, rest), 0)
        out.append(own)
    return out[0] * jnp.asarray(HEAD_DIM ** -0.5, BF), out[1]


def fill_heads(ref, value, low_half):
    nil = jnp.zeros_like(value)
    ref[0:TOK, 0:128] = jnp.where(low_half, value, nil)
    ref[KEYS : KEYS + TOK, 0:128] = jnp.where(low_half, nil, value)


def attention_forward(units, zero, weight, qkv_bias, down, up, number, table, marks, codes, info,
                      plan):
    outs = unit_shapes(plan)
    n_buf = len(outs)
    n_units = plan["units"]
    n_rows = n_units * PITCH
    n_slots = plan["full"] + plan["short"]

    def kernel(codes_ref, info_ref, *refs):
        in_bufs = refs[: n_buf + 1]
        w_src, bias_ref, down_ref, up_ref, table_ref, marks_ref = refs[n_buf + 1 : n_buf + 7]
        refs = refs[n_buf + 7 :]
        out_bufs = refs[:n_buf]
        win_out, mixed_out, inner_out, prob_out, inv_out, att_out = refs[n_buf : n_buf + 6]
        (x_in, x_out, w_vmem, keys, vals, mixed_ref, inner_ref, prob_ref, inv_ref, in_sems,
         out_sems, w_sems, save_sems, prob_sems) = refs[n_buf + 6 :]
        used = info_ref[2]
        fetches = []
        for part in range(3):
            rows = slice(part * D, (part + 1) * D)
            fetches.append(pltpu.make_async_copy(w_src.at[rows], w_vmem.at[rows], w_sems.at[part]))
            fetches[-1].start()
        start_in(codes_ref, n_units, in_bufs, x_in, in_sems.at[0])
        bias_low = bias_ref[...].astype(BF)
        lane = lax.broadcasted_iota(jnp.int32, (KEYS, 128), 1)
        for twin in range(2):
            keys[twin, :, 0:128] = jnp.zeros((2 * KEYS, 128), BF)
            keys[twin, :, 128:256] = marks_ref[...]
            vals[twin, :, 0:128] = jnp.zeros((2 * KEYS, 128), BF)
            vals[twin, 0:KEYS, 128:256] = (lane < 64).astype(BF)
            vals[twin, KEYS:, 128:256] = (lane >= 64).astype(BF)

        wait_all(x_in, in_sems.at[0])
        x = x_in[...].reshape(n_rows, D)
        saves = [pltpu.make_async_copy(x_in, win_out, save_sems.at[0])]
        inner = nt(x, down_ref[0]).astype(BF)
        inner_ref[...] = inner
        def part_columns(part, carry):
            rows = pl.ds(pl.multiple_of(part * D, D), D)
            pltpu.make_async_copy(w_src.at[rows], w_vmem.at[rows], w_sems.at[part]).wait()
            mixed = nt(x_in[...].reshape(n_rows, D), w_vmem[rows])
            mixed = mixed + bias_ref[:, rows] + nn(inner_ref[...], up_ref[0, :, rows])
            mixed_ref[:, rows] = mixed.astype(BF)
            return carry

        lax.fori_loop(0, 3, part_columns, 0)
        saves.append(pltpu.make_async_copy(mixed_ref, mixed_out, save_sems.at[1]))
        saves.append(pltpu.make_async_copy(inner_ref, inner_out, save_sems.at[2]))
        for save in saves:
            save.start()
        small = lax.broadcasted_iota(jnp.int32, (PITCH, 128), 1)
        low_half = lax.broadcasted_iota(jnp.int32, (TOK, 128), 1) < 64

        def attend(at, rows, slot):
            for j in range(PAIRS):
                twin = j % 2
                key, value = key_value(mixed_ref, bias_low, at, rows, j)
                fill_heads(keys.at[twin], key, low_half)
                fill_heads(vals.at[twin], value, low_half)
                cols = slice(128 * j, 128 * j + 128)
                q = mixed_ref[pl.ds(at, rows), cols]
                rel = nn(q, table_ref[...])
                pieces = []
                for x_at in range(rows // PITCH):
                    slab = rel[PITCH * x_at : PITCH * x_at + PITCH]
                    tall = pltpu.roll(slab, 113 + x_at, 1)
                    wide = pltpu.roll(slab, 113, 1, stride=1, stride_axis=0)
                    both = jnp.where(small % 64 < 32, tall, wide)
                    pieces.append(jnp.where(small == 14, 1.0, both).astype(BF))
                query = jnp.concatenate((q, jnp.concatenate(pieces, 0)), 1)
                scores = nt(query, keys[twin])
                probs = []
                for head in range(2):
                    part = scores[:, KEYS * head : KEYS * head + KEYS]
                    top = jnp.max(part, axis=-1, keepdims=True)
                    probs.append(jnp.exp(part - top).astype(BF))
                prob = jnp.concatenate(probs, 1)
                prob_ref[j, pl.ds(at, rows)] = prob
                summed = nn(prob, vals[twin])
                inverse = 1.0 / summed[:, 128:256]
                inv_ref[pl.ds(at, rows), cols] = inverse
                att = (summed[:, 0:128] * inverse).astype(BF)
                x_out[pl.ds(at // PITCH, rows // PITCH), :, cols] = att.reshape(
                    rows // PITCH, PITCH, 128
                )
            span = pl.ds(at, rows)
            pltpu.make_async_copy(prob_ref.at[:, span], prob_out.at[:, span],
                                  prob_sems.at[slot, 0]).start()
            pltpu.make_async_copy(inv_ref.at[span], inv_out.at[span], prob_sems.at[slot, 1]).start()
            start_out(codes_ref, at // PITCH, rows // PITCH, x_out, out_bufs, None, out_sems.at[0])

        each_slot(info_ref, plan, attend)
        start_out(codes_ref, used, n_units - used, x_out, out_bufs, plan["local"], out_sems.at[0])
        save = pltpu.make_async_copy(x_out, att_out, save_sems.at[3])
        save.start()

        def finish(at, rows, slot):
            span = pl.ds(at, rows)
            pltpu.make_async_copy(prob_ref.at[:, span], prob_out.at[:, span],
                                  prob_sems.at[slot, 0]).wait()
            pltpu.make_async_copy(inv_ref.at[span], inv_out.at[span], prob_sems.at[slot, 1]).wait()

        wait_all(x_out, out_sems.at[0])
        each_slot(info_ref, plan, finish)
        for one in saves + [save]:
            one.wait()

    saved = saved_shapes(plan)
    boxed = jax.ShapeDtypeStruct((n_units, PITCH, D), BF)
    results = pl.pallas_call(
        kernel,
        out_shape=outs + [boxed] + saved[1:5] + [boxed],
        grid_spec=pltpu.PrefetchScalarGridSpec(
            num_scalar_prefetch=2,
            grid=(1,),
            in_specs=any_specs(n_buf + 2)
            + [
                full_spec((1, 3 * D)),
                image_spec(down.shape, number),
                image_spec(up.shape, number),
                full_spec(table.shape),
                full_spec(marks.shape),
            ],
            out_specs=any_specs(n_buf + 6),
            scratch_shapes=[
                pltpu.VMEM((n_units, PITCH, D), BF),
                pltpu.VMEM((n_units, PITCH, D), BF),
                pltpu.VMEM((3 * D, D), BF),
                pltpu.VMEM((2, 2 * KEYS, 256), BF),
                pltpu.VMEM((2, 2 * KEYS, 256), BF),
                pltpu.VMEM((n_rows, 3 * D), BF),
                pltpu.VMEM((n_rows, RANK), BF),
                pltpu.VMEM((PAIRS, n_rows, 2 * KEYS), BF),
                pltpu.VMEM((n_rows, D), F32),
                pltpu.SemaphoreType.DMA((1,)),
                pltpu.SemaphoreType.DMA((1,)),
                pltpu.SemaphoreType.DMA((3,)),
                pltpu.SemaphoreType.DMA((4,)),
                pltpu.SemaphoreType.DMA((n_slots, 2)),
            ],
        ),
        cost_estimate=cost(10e9, 20e6, 4e6),
        compiler_params=params(),
        name="attention_forward",
    )(codes, info, *units, zero, weight, qkv_bias, down, up, table, marks)
    return results[:n_buf], results[n_buf:]


FF_KINDS = ("pd", "pu", "ed", "eu", "cd", "cu")
HALVES = (("eu", "pd", "pu", "ed", "cu"), ("cd",))
FF_WIDTHS = {"pd": D, "pu": D, "ed": D, "eu": FF, "cd": FF, "cu": D}


def stage_pieces(ranks):
    for h, kinds in enumerate(HALVES):
        at = 0
        for kind in kinds:
            wide = FF_WIDTHS[kind] // ranks
            yield h, at, wide, kind
            at += wide


def feed_forward(units, images, cotangent, number, row_count, weight_src, proj_copies,
                 expand_copies, contract_copies, vectors, adapter_src, adapter_index,
                 adapter_copies, place, codes, plan, rows_block, ranks, previous):
    side, steps, rows_spec = rows_plan(images, row_count, rows_block, number)
    per_step = rows_block * GRID
    tokens = rows_block * side
    outs = unit_shapes(plan)
    n_buf = len(outs)
    copies = [proj_copies, expand_copies, contract_copies]
    chunk = 512
    chunks = FF // chunk
    n_src = len(weight_src)
    stage_width = 2 * FF // ranks
    n_prev = len(previous)
    term_width = 3 * FF // ranks
    at_prev = 2 + n_buf + 2 + n_src + 5 + 4

    def kernel(codes_ref, pick_ref, *refs):
        in_bufs, refs = refs[:n_buf], refs[n_buf:]
        img_ref, cot_ref, refs = refs[0], refs[1], refs[2:]
        w_src, refs = refs[:n_src], refs[n_src:]
        (bp, g2, b2, be, bc), refs = refs[:5], refs[5:]
        a_src, place_ref, placet_ref, refs = refs[0:2], refs[2], refs[3], refs[4 + n_prev :]
        out_bufs, refs = refs[:n_buf], refs[n_buf:]
        block_ref, mid_ref, terms_ref, refs = refs[0], refs[1], refs[2], refs[3:]
        (pd, pu, ed, eu, cd, cu), refs = refs[:6], refs[6:]
        (d_pd, d_pu, d_ed, d_eu, d_cd, d_cu), refs = refs[:6], refs[6:]
        (u_in, u_out, wp, we, wc, stage_a, stage_b, acc_result, acc_second, in_sems, out_sems,
         w_sems, s_sems) = refs
        adapters = dict(zip(FF_KINDS, (pd, pu, ed, eu, cd, cu)))
        grads = dict(zip(FF_KINDS, (d_pd, d_pu, d_ed, d_eu, d_cd, d_cu)))
        step = pl.program_id(0)
        targets = [wp, we, wc]

        def weights(which):
            for src, dst in copies[which]:
                pltpu.make_async_copy(
                    w_src[which].at[src], targets[which].at[dst], w_sems.at[which]
                ).start()

        @pl.when(step == 0)
        def _():
            stages = (stage_a, stage_b)
            for half, src, dst in adapter_copies(pick_ref[number]):
                pltpu.make_async_copy(a_src[half].at[src], stages[half].at[dst],
                                      s_sems.at[half]).start()
            start_in(codes_ref, row_count * GRID, in_bufs, u_in, in_sems.at[0])
            for which in range(3):
                weights(which)
            for grad in grads.values():
                grad[...] = jnp.zeros_like(grad)
            wait_all(stage_a, s_sems.at[0])
            wait_all(stage_b, s_sems.at[1])
            for h, at, wide, kind in stage_pieces(ranks):
                for r in range(ranks):
                    adapters[kind][:, wide * r : wide * r + wide] = stages[h][
                        r, :, at : at + wide
                    ]
            wait_all(wp, w_sems.at[0])
            wait_all(u_in, in_sems.at[0])

        rows = []
        for r in range(rows_block):
            spread = u_in[pl.ds(step * per_step + r * GRID, GRID)].reshape(GRID * PITCH, D)
            rows.append(nn(placet_ref[...], spread).astype(BF))
        att = jnp.concatenate(rows, 0)
        cot = cot_ref[...].reshape(tokens, D)
        p_inner = nt(att, pd[...]).astype(BF)
        middle = (
            img_ref[...].reshape(tokens, D).astype(F32)
            + nt(att, wp[...])
            + bp[...]
            + nn(p_inner, pu[...])
        )
        standard, inverse = norm_parts(middle)
        second = (standard * g2[...] + b2[...]).astype(BF)
        e_inner = nt(second, ed[...]).astype(BF)
        c_mid = nt(cot, cu[...]).astype(BF)
        c_inner = jnp.zeros((tokens, RANK), F32)
        e_mid = jnp.zeros((tokens, RANK), F32)

        @pl.when(step == 0)
        def _():
            wait_all(we, w_sems.at[1])
            wait_all(wc, w_sems.at[2])

        acc_result[...] = middle + bc[...]
        acc_second[...] = jnp.zeros((tokens, D), F32)

        def one_chunk(n, carry):
            c_inner, e_mid = carry
            cols = pl.ds(pl.multiple_of(n * chunk, chunk), chunk)
            hidden = nn(second, we[:, cols]) + be[:, cols] + nn(e_inner, eu[:, cols])
            cdf = 0.5 * (1.0 + lax.erf(hidden * SQRT_HALF))
            slope = cdf + hidden * jnp.exp(-0.5 * hidden * hidden) * INV_SQRT_TAU
            active = (hidden * cdf).astype(BF)
            a_grad = nn(cot, wc[:, cols]) + nn(c_mid, cd[:, cols])
            h_grad = (a_grad * slope).astype(BF)
            acc_result[...] += nt(active, wc[:, cols])
            c_inner = c_inner + nt(active, cd[:, cols])
            acc_second[...] += nt(h_grad, we[:, cols])
            e_mid = e_mid + nt(h_grad, eu[:, cols])
            d_cd[:, cols] += tn(c_mid, active)
            d_eu[:, cols] += tn(e_inner, h_grad)
            return c_inner, e_mid

        c_inner, e_mid = lax.fori_loop(0, chunks, one_chunk, (c_inner, e_mid))
        result = acc_result[...]
        second_grad = acc_second[...]
        c_inner = c_inner.astype(BF)
        e_mid = e_mid.astype(BF)
        result = result + nn(c_inner, cu[...])
        block_ref[...] = result.astype(BF).reshape(rows_block, side, D)
        d_cu[...] += tn(c_inner, cot)
        d_ed[...] += tn(e_mid, second)
        second_grad = second_grad + nn(e_mid, ed[...])
        middle_grad = cot.astype(F32) + norm_back(second_grad, standard, inverse, g2[...])
        mid_ref[...] = middle_grad.reshape(rows_block, side, D)
        branch = middle_grad.astype(BF)
        p_mid = nt(branch, pu[...]).astype(BF)
        d_pu[...] += tn(p_inner, branch)
        d_pd[...] += tn(p_mid, att)
        att_grad = (nn(branch, wp[...]) + nn(p_mid, pd[...])).astype(BF)
        for r in range(rows_block):
            spread = nn(place_ref[...], att_grad[r * side : (r + 1) * side])
            u_out[pl.ds(step * per_step + r * GRID, GRID)] = spread.astype(BF).reshape(
                GRID, PITCH, D
            )
        start_out(codes_ref, step * per_step, per_step, u_out, out_bufs, None, out_sems.at[0])

        @pl.when(step == steps - 1)
        def _():
            at = 0
            for kind in FF_KINDS:
                wide = FF_WIDTHS[kind] // ranks
                for r in range(ranks):
                    terms_ref[r, :, at : at + wide] = grads[kind][
                        :, wide * r : wide * r + wide
                    ].astype(BF)
                at += wide
            if at < term_width:
                terms_ref[:, :, at:] = jnp.zeros((ranks, RANK, term_width - at), BF)
            wait_all(u_out, out_sems.at[0])

    results = pl.pallas_call(
        kernel,
        out_shape=outs
        + [
            jax.ShapeDtypeStruct(images.shape, BF),
            jax.ShapeDtypeStruct((row_count, side, D), F32),
            jax.ShapeDtypeStruct((ranks, images.shape[0] // row_count * RANK, term_width), BF),
        ],
        grid_spec=pltpu.PrefetchScalarGridSpec(
            num_scalar_prefetch=2,
            grid=(steps,),
            in_specs=any_specs(n_buf)
            + [rows_spec, rows_spec]
            + any_specs(n_src)
            + [full_spec(v.shape) for v in vectors]
            + any_specs(2)
            + [full_spec(place.shape), full_spec(place.shape[::-1])]
            + any_specs(n_prev),
            out_specs=any_specs(n_buf)
            + [
                rows_spec,
                pl.BlockSpec((rows_block, side, D), lambda i, *_: (i, 0, 0)),
                pl.BlockSpec((ranks, RANK, term_width), lambda *_: (0, number, 0)),
            ],
            scratch_shapes=[pltpu.VMEM((RANK, FF_WIDTHS[k]), BF) for k in FF_KINDS]
            + [pltpu.VMEM((RANK, FF_WIDTHS[k]), F32) for k in FF_KINDS]
            + [
                pltpu.VMEM((row_count * GRID, PITCH, D), BF),
                pltpu.VMEM((row_count * GRID, PITCH, D), BF),
                pltpu.VMEM((D, D), BF),
                pltpu.VMEM((D, FF), BF),
                pltpu.VMEM((D, FF), BF),
                pltpu.VMEM((ranks, RANK, stage_width), BF),
                pltpu.VMEM((ranks, RANK, FF // ranks), BF),
                pltpu.VMEM((tokens, D), F32),
                pltpu.VMEM((tokens, D), F32),
                pltpu.SemaphoreType.DMA((1,)),
                pltpu.SemaphoreType.DMA((1,)),
                pltpu.SemaphoreType.DMA((3,)),
                pltpu.SemaphoreType.DMA((2,)),
            ],
        ),
        input_output_aliases={at_prev: n_buf, at_prev + 1: n_buf + 2} if n_prev else {},
        cost_estimate=cost(18e9, 20e6, 4e6),
        compiler_params=params(),
        name="feed_forward",
    )(codes, adapter_index, *units, images, cotangent, *weight_src, *vectors, *adapter_src, place,
      place.T, *previous)
    return results[:n_buf], results[n_buf], results[n_buf + 1], results[n_buf + 2]


def attention_backward(units, zero, weight, saved, qkv_bias, down, up, number, table, marks, codes,
                       info, plan, ranks, image_count, previous):
    outs = unit_shapes(plan)
    n_buf = len(outs)
    n_units = plan["units"]
    n_rows = n_units * PITCH
    n_slots = plan["full"] + plan["short"]
    term_width = 4 * D // ranks

    def kernel(codes_ref, info_ref, *refs):
        in_bufs, refs = refs[: n_buf + 1], refs[n_buf + 1 :]
        w_src, refs = refs[0], refs[1:]
        (win_src, mixed_src, inner_src, prob_src, inv_src, att_src), refs = refs[:6], refs[6:]
        bias_ref, down_ref, up_ref, table_ref, marks_ref = refs[:5]
        refs = refs[5 + len(previous) :]
        out_bufs, refs = refs[:n_buf], refs[n_buf:]
        terms_ref, refs = refs[0], refs[1:]
        (g_in, x_out, w_vmem, keys, vals, grads, win_ref, mixed_ref, inner_ref, prob_ref, inv_ref,
         att_ref, in_sems, out_sems, load_sems, prob_sems) = refs
        used = info_ref[2]
        start_in(codes_ref, n_units, in_bufs, g_in, in_sems.at[0])
        loads = [
            pltpu.make_async_copy(src, dst, load_sems.at[n])
            for n, (src, dst) in enumerate(
                ((mixed_src, mixed_ref), (att_src, att_ref), (inner_src, inner_ref),
                 (win_src, win_ref), (w_src, w_vmem)))
        ]

        def slot_loads(at, rows, slot):
            span = pl.ds(at, rows)
            return (
                pltpu.make_async_copy(prob_src.at[:, span], prob_ref.at[:, span],
                                      prob_sems.at[slot, 0]),
                pltpu.make_async_copy(inv_src.at[span], inv_ref.at[span], prob_sems.at[slot, 1]),
            )

        def begin(at, rows, slot):
            for copy in slot_loads(at, rows, slot):
                copy.start()

        for load in loads[:2]:
            load.start()
        each_slot(info_ref, plan, begin)
        for load in loads[2:]:
            load.start()
        bias_low = bias_ref[...].astype(BF)
        for twin in range(2):
            keys[twin, :, 0:128] = jnp.zeros((2 * KEYS, 128), BF)
            keys[twin, :, 128:256] = marks_ref[...]
            vals[twin] = jnp.zeros((2 * KEYS, 128), BF)

        def clear(unit, carry):
            grads[pl.ds(pl.multiple_of(unit * PITCH, PITCH), PITCH)] = jnp.zeros((PITCH, 3 * D), BF)
            return carry

        lax.fori_loop(used, n_units, clear, 0)
        loads[0].wait()
        loads[1].wait()
        wait_all(g_in, in_sems.at[0])
        small = lax.broadcasted_iota(jnp.int32, (PITCH, 128), 1)
        low_half = lax.broadcasted_iota(jnp.int32, (TOK, 128), 1) < 64

        def attend(at, rows, slot):
            for copy in slot_loads(at, rows, slot):
                copy.wait()
            span = pl.ds(at, rows)
            half = low_half[:rows]
            for j in range(PAIRS):
                twin = j % 2
                cols = slice(128 * j, 128 * j + 128)
                key, value = key_value(mixed_ref, bias_low, at, rows, j)
                fill_heads(keys.at[twin], key, low_half)
                fill_heads(vals.at[twin], value, low_half)
                q = mixed_ref[span, cols]
                units_at = pl.ds(at // PITCH, rows // PITCH)
                grad = g_in[units_at, :, cols].reshape(rows, 128).astype(F32) * inv_ref[span, cols]
                grad_low = grad.astype(BF)
                weighed = grad * att_ref[units_at, :, cols].reshape(rows, 128).astype(F32)
                total = jnp.sum(weighed, axis=-1, keepdims=True)
                dot_a = jnp.sum(jnp.where(half, weighed, 0.0), axis=-1, keepdims=True)
                dots = (dot_a, total - dot_a)
                soft = nt(grad_low, vals[twin])
                pieces = []
                for head in range(2):
                    lanes = slice(KEYS * head, KEYS * head + KEYS)
                    prob = prob_ref[j, span, lanes].astype(F32)
                    pieces.append((prob * (soft[:, lanes] - dots[head])).astype(BF))
                both = nn(jnp.concatenate(pieces, 1), keys[twin])
                rel = both[:, 128:256]
                unrolled = []
                for x_at in range(rows // PITCH):
                    slab = rel[PITCH * x_at : PITCH * x_at + PITCH]
                    tall = pltpu.roll(slab, x_at, 1) if x_at else slab
                    wide = pltpu.roll(slab, 0, 1, stride=1, stride_axis=0)
                    unrolled.append(jnp.where(small % 64 < 32, tall, wide).astype(BF))
                q_grad = both[:, 0:128] + nn(jnp.concatenate(unrolled, 0), table_ref[...])
                grads[span, cols] = q_grad.astype(BF)
                q_t = q.T
                g_t = grad_low.T
                k_parts = []
                v_parts = []
                for head in range(2):
                    lanes = slice(KEYS * head, KEYS * head + KEYS)
                    own = slice(64 * head, 64 * head + 64)
                    k_parts.append(nn(q_t[own], pieces[head]))
                    v_parts.append(nn(g_t[own], prob_ref[j, span, lanes]))
                k_grad = jnp.concatenate(k_parts, 0).T[:rows] * HEAD_DIM ** -0.5
                v_grad = jnp.concatenate(v_parts, 0).T[:rows]
                grads[span, D + 128 * j : D + 128 * j + 128] = k_grad.astype(BF)
                grads[span, 2 * D + 128 * j : 2 * D + 128 * j + 128] = v_grad.astype(BF)

        each_slot(info_ref, plan, attend)
        for load in loads[2:]:
            load.wait()
        mixed_grad = grads[...]
        mid = nt(mixed_grad, up_ref[0]).astype(BF)

        def some_columns(piece, carry):
            cols = pl.ds(pl.multiple_of(piece * 256, 256), 256)
            normed = nn(grads[...], w_vmem[:, cols]) + nn(mid, down_ref[0, :, cols])
            x_out[:, :, cols] = normed.astype(BF).reshape(n_units, PITCH, 256)
            return carry

        lax.fori_loop(0, 3, some_columns, 0)
        start_out(codes_ref, 0, n_units, x_out, out_bufs, plan["local"], out_sems.at[0])
        d_up = tn(inner_ref[...], mixed_grad).astype(BF)
        d_down = tn(mid, win_ref[...].reshape(n_rows, D)).astype(BF)
        at = 0
        for value, wide in ((d_down, D // ranks), (d_up, 3 * D // ranks)):
            for r in range(ranks):
                terms_ref[r, :, at : at + wide] = value[:, wide * r : wide * r + wide]
            at += wide
        wait_all(x_out, out_sems.at[0])

    results = pl.pallas_call(
        kernel,
        out_shape=outs + [jax.ShapeDtypeStruct((ranks, image_count * RANK, term_width), BF)],
        grid_spec=pltpu.PrefetchScalarGridSpec(
            num_scalar_prefetch=2,
            grid=(1,),
            in_specs=any_specs(n_buf + 8)
            + [full_spec((1, 3 * D)), image_spec(down.shape, number), image_spec(up.shape, number),
               full_spec(table.shape), full_spec(marks.shape)] + any_specs(len(previous)),
            out_specs=any_specs(n_buf)
            + [pl.BlockSpec((ranks, RANK, term_width), lambda *_: (0, number, 0))],
            scratch_shapes=[
                pltpu.VMEM((n_units, PITCH, D), BF),
                pltpu.VMEM((n_units, PITCH, D), BF),
                pltpu.VMEM((3 * D, D), BF),
                pltpu.VMEM((2, 2 * KEYS, 256), BF),
                pltpu.VMEM((2, 2 * KEYS, 128), BF),
                pltpu.VMEM((n_rows, 3 * D), BF),
                pltpu.VMEM((n_units, PITCH, D), BF),
                pltpu.VMEM((n_rows, 3 * D), BF),
                pltpu.VMEM((n_rows, RANK), BF),
                pltpu.VMEM((PAIRS, n_rows, 2 * KEYS), BF),
                pltpu.VMEM((n_rows, D), F32),
                pltpu.VMEM((n_units, PITCH, D), BF),
                pltpu.SemaphoreType.DMA((1,)),
                pltpu.SemaphoreType.DMA((1,)),
                pltpu.SemaphoreType.DMA((5,)),
                pltpu.SemaphoreType.DMA((n_slots, 2)),
            ],
        ),
        input_output_aliases={2 + n_buf + 8 + 5: n_buf} if previous else {},
        cost_estimate=cost(12e9, 20e6, 4e6),
        compiler_params=params(),
        name="attention_backward",
    )(codes, info, *units, zero, weight, *saved, qkv_bias, down, up, table, marks, *previous)
    return results[:n_buf], results[n_buf]


def first_norm_back(units, images, middle_grad, number, row_count, gain, place_t, codes, plan,
                    rows_block, previous):
    side, steps, rows_spec = rows_plan(images, row_count, rows_block, number)
    per_step = rows_block * GRID
    n_buf = len(units)
    n_prev = len(previous)

    def kernel(codes_ref, *refs):
        in_bufs, refs = refs[:n_buf], refs[n_buf:]
        x_ref, m_ref, g_ref, p_ref, refs = refs[0], refs[1], refs[2], refs[3], refs[4 + n_prev :]
        out_ref, u_in, sems = refs
        step = pl.program_id(0)

        @pl.when(step == 0)
        def _():
            start_in(codes_ref, row_count * GRID, in_bufs, u_in, sems.at[0])

        values = x_ref[...].reshape(rows_block * side, D).astype(F32)
        standard, inverse = norm_parts(values)

        @pl.when(step == 0)
        def _():
            wait_all(u_in, sems.at[0])

        rows = []
        for r in range(rows_block):
            spread = u_in[pl.ds(step * per_step + r * GRID, GRID)].reshape(GRID * PITCH, D)
            rows.append(nn(p_ref[...], spread))
        upstream = jnp.concatenate(rows, 0)
        back = norm_back(upstream, standard, inverse, g_ref[...])
        out_ref[...] = m_ref[...] + back.reshape(rows_block, side, D)

    return pl.pallas_call(
        kernel,
        out_shape=jax.ShapeDtypeStruct(images.shape, F32),
        grid_spec=pltpu.PrefetchScalarGridSpec(
            num_scalar_prefetch=1,
            grid=(steps,),
            in_specs=any_specs(n_buf)
            + [
                rows_spec,
                pl.BlockSpec((rows_block, side, D), lambda i, *_: (i, 0, 0)),
                full_spec((1, D)),
                full_spec(place_t.shape),
            ]
            + any_specs(n_prev),
            out_specs=rows_spec,
            scratch_shapes=[
                pltpu.VMEM((row_count * GRID, PITCH, D), BF),
                pltpu.SemaphoreType.DMA((1,)),
            ],
        ),
        input_output_aliases={1 + n_buf + 4: 0} if n_prev else {},
        cost_estimate=cost(1e9, 8e6),
        compiler_params=params(),
        name="first_norm_back",
    )(codes, *units, images, middle_grad, gain, place_t, *previous)


KINDS = ("qd", "qu", "pd", "pu", "ed", "eu", "cd", "cu")
WIDTHS = {"qd": D, "qu": 3 * D, "pd": D, "pu": D, "ed": D, "eu": FF, "cd": FF, "cu": D}


def packed_form(groups, ranks):
    return groups == 4 and ranks == 8


def shift_z(value, step):
    return lax.ppermute(value, "rows", [(r, (r + 2 * step) % 8) for r in range(8)])


def flip_y(value):
    return lax.ppermute(value, "rows", [(r, r ^ 1) for r in range(8)])


def flip_x(value):
    return lax.ppermute(value, "dp", [(d, d ^ 2) for d in range(4)])


def flip_core(value):
    return lax.ppermute(value, "dp", [(d, d ^ 1) for d in range(4)])


NQ, NP = 144, 48
MOVES = ((0, 0, 0), (0, 0, 1), (0, 1, 0), (0, 1, 1), (1, 0, 0), (1, 0, 1), (1, 1, 0), (1, 1, 1),
         (0, 0, 2), (0, 0, 3), (1, 0, 2), (1, 0, 3), (0, 1, 2), (0, 1, 3), (1, 1, 2), (1, 1, 3))


def piece_table():
    table = np.zeros((4, 8, 32), np.int32)
    for d in range(4):
        for r in range(8):
            for number, (kx, ky, kz) in enumerate(MOVES):
                for kc in range(2):
                    source_d = (d ^ (2 * kx)) ^ kc
                    source_r = ((r // 2 - kz) % 4) * 2 + ((r % 2) ^ ky)
                    table[d, r, source_r * 4 + source_d] = 16 * kc + number
    return table


def pack(qkv, proj, expand, contract, adapters):
    core = (lax.axis_index("dp") % 2).reshape(1)
    rows = qkv.shape[0]
    ne, nc = expand.shape[0] // 2, contract.shape[0]
    n_ad = len(adapters)
    lists = KINDS

    def kernel(core_ref, q_ref, p_ref, e_ref, c_ref, *refs):
        ads = dict(zip(lists, refs[:n_ad]))
        second, own, other, extra = refs[n_ad:]

        def turned(value):
            wide = value.shape[1]
            eye = (
                lax.broadcasted_iota(jnp.int32, (wide, wide), 0)
                == lax.broadcasted_iota(jnp.int32, (wide, wide), 1)
            )
            return nt(eye.astype(F32).astype(BF), value).astype(BF)

        q_t = turned(q_ref[...])
        p_t = turned(p_ref[...])
        for half, chosen in ((0, 0), (1, 1)):
            @pl.when(core_ref[0] == chosen)
            def _():
                own[0:NQ] = q_t[half * NQ : half * NQ + NQ]
                own[NQ:] = p_t[half * NP : half * NP + NP]
                other[0:NQ] = q_t[(1 - half) * NQ : (1 - half) * NQ + NQ]
                other[NQ:] = p_t[(1 - half) * NP : (1 - half) * NP + NP]

        second[0:ne, 0 : expand.shape[1]] = e_ref[0:ne]
        second[0:ne, expand.shape[1] :] = e_ref[ne:]
        second[ne : ne + nc] = c_ref[...]
        base = ne + nc
        for i in range(2):
            rows_i = slice(base + i * RANK, base + i * RANK + RANK)
            at = 0
            for kind in HALVES[0]:
                wide = ads[kind].shape[2]
                second[rows_i, at : at + wide] = ads[kind][i]
                at += wide
            wide = ads["cd"].shape[2]
            second[base + 2 * RANK :, i * wide : i * wide + wide] = ads["cd"][i]
            at = ads["qu"].shape[2]
            extra[i * RANK : i * RANK + RANK, 0:at] = ads["qu"][i]
            extra[i * RANK : i * RANK + RANK, at:] = ads["qd"][i]

    shapes = [(ne + nc + 3 * RANK, D), (NQ + NP, rows), (NQ + NP, rows), (2 * RANK, 384)]
    return pl.pallas_call(
        kernel,
        out_shape=[jax.ShapeDtypeStruct(shape, BF) for shape in shapes],
        grid_spec=pltpu.PrefetchScalarGridSpec(
            num_scalar_prefetch=1,
            grid=(1,),
            in_specs=[full_spec(v.shape) for v in (qkv, proj, expand, contract) + adapters],
            out_specs=[full_spec(shape) for shape in shapes],
        ),
        cost_estimate=cost(1e8, 2e6),
        compiler_params=params(),
        name="pack",
    )(core, qkv, proj, expand, contract, *adapters)


def first_piece(own, other, extra):
    core = lax.axis_index("dp") % 2
    other = flip_core(other)
    joined = jnp.where(
        core == 0, jnp.concatenate((own, other), 1), jnp.concatenate((other, own), 1)
    )
    return jnp.concatenate((joined, extra), 0)


def gather_first(piece, norms):
    line = jnp.stack([piece] + [shift_z(piece, k) for k in (1, 2, 3)])
    line = after(line, *norms)
    left, right = line[:2], line[2:]
    left = jnp.concatenate((left, flip_y(left)))
    right = jnp.concatenate((right, flip_x(right)))
    left, right = lax.optimization_barrier((left, right))
    pieces = jnp.concatenate((left, flip_x(left), right, flip_y(right)))
    return (left, right), pieces, flip_core(pieces), line


def assemble(pieces, others, table, adapter_index, image_count):
    def kernel(table_ref, pick_ref, a_ref, b_ref, wq, wp, down_ref, up_ref, stage, w_sems, s_sems):
        def fetch(block, src_rows, dst, sem):
            code = table_ref[block]
            index = code % 16

            @pl.when(code < 16)
            def _():
                pltpu.make_async_copy(a_ref.at[index, src_rows], dst, sem).start()

            @pl.when(code >= 16)
            def _():
                pltpu.make_async_copy(b_ref.at[index, src_rows], dst, sem).start()

        for n in range(image_count):
            chosen = pick_ref[n]
            rows = pl.ds(pl.multiple_of(NQ + NP + RANK * (chosen % 2), 16), RANK)
            for r in range(8):
                fetch(r * 4 + chosen // 2, rows, stage.at[n, r], s_sems.at[0])
        for r in range(8):
            for d in range(4):
                x, c = divmod(d, 2)
                lanes = slice(384 * x, 384 * x + 384)
                top = 2 * NQ * r + NQ * c
                fetch(r * 4 + d, slice(0, NQ), wq.at[top : top + NQ, lanes], w_sems.at[0])
                top = 2 * NP * r + NP * c
                fetch(r * 4 + d, slice(NQ, NQ + NP), wp.at[top : top + NP, lanes], w_sems.at[1])
        wait_all(stage, s_sems.at[0])
        for n in range(image_count):
            for r in range(8):
                up_ref[n, :, 288 * r : 288 * r + 288] = stage[n, r, :, 0:288]
                down_ref[n, :, 96 * r : 96 * r + 96] = stage[n, r, :, 288:384]
        wait_all(wq, w_sems.at[0])
        wait_all(wp, w_sems.at[1])

    return pl.pallas_call(
        kernel,
        out_shape=[
            jax.ShapeDtypeStruct((3 * D, D), BF),
            jax.ShapeDtypeStruct((D, D), BF),
            jax.ShapeDtypeStruct((image_count, RANK, D), BF),
            jax.ShapeDtypeStruct((image_count, RANK, 3 * D), BF),
        ],
        grid_spec=pltpu.PrefetchScalarGridSpec(
            num_scalar_prefetch=2,
            grid=(1,),
            in_specs=any_specs(2),
            out_specs=[
                full_spec((3 * D, D)),
                full_spec((D, D)),
                full_spec((image_count, RANK, D)),
                full_spec((image_count, RANK, 3 * D)),
            ],
            scratch_shapes=[
                pltpu.VMEM((image_count, 8, RANK, 384), BF),
                pltpu.SemaphoreType.DMA((2,)),
                pltpu.SemaphoreType.DMA((1,)),
            ],
        ),
        cost_estimate=cost(1e6, 10e6),
        compiler_params=params(),
        name="assemble",
    )(table, adapter_index, pieces, others)


def second_copies(groups, ranks):
    ne, nc = FF // (groups * ranks), D // ranks
    wide = FF // ranks
    expand, contract = [], []
    for r in range(ranks):
        for d in range(groups):
            b = r * groups + d
            for h in range(2):
                top = d * 2 * ne + h * ne
                expand.append(
                    (
                        (b, slice(0, ne), slice(h * wide, h * wide + wide)),
                        (slice(top, top + ne), slice(r * wide, r * wide + wide)),
                    )
                )
            contract.append(
                ((b, slice(ne, ne + nc)), (slice(nc * r, nc * r + nc), slice(D * d, D * d + D)))
            )
    return expand, contract, ne + nc


def second_adapters(base, groups, ranks):
    per_group = ADAPTERS // groups
    wide = FF // ranks

    def copies(chosen):
        found = []
        for r in range(ranks):
            block = r * groups + chosen // per_group
            own = chosen % per_group
            rows = pl.ds(pl.multiple_of(base + own * RANK, RANK), RANK)
            found.append((0, (block, rows), (r,)))
            rows = slice(base + 2 * RANK, base + 3 * RANK)
            found.append((1, (block, rows, pl.ds(pl.multiple_of(own * wide, 128), wide)), (r,)))
        return found

    return copies


def plain_stage(chosen, ranks):
    images = chosen[0].shape[0]
    lists = dict(zip(FF_KINDS, chosen))
    halves = []
    for kinds in HALVES:
        parts = [lists[k].reshape(images, RANK, ranks, -1).transpose(0, 2, 1, 3) for k in kinds]
        halves.append(jnp.concatenate(parts, 3))
    return [[half[n] for half in halves] for n in range(images)]


def gather_plain(weights, adapters, adapter_index):
    full = []
    for m in weights:
        m = lax.all_gather(m, "dp", axis=0, tiled=True)
        full.append(lax.all_gather(m, "rows", axis=1, tiled=True))
    qkv, proj, expand, contract = full
    chosen = []
    for m in adapters:
        m = lax.all_gather(m, "dp", axis=0, tiled=True)
        m = jnp.take(m, adapter_index[:, 0], axis=0)
        chosen.append(lax.all_gather(m, "rows", axis=2, tiled=True))
    return [qkv.T, proj.T, expand, contract.T], chosen


def rows_sum(packed):
    moved = lax.all_to_all(packed, "rows", split_axis=0, concat_axis=0, tiled=True)
    return jnp.sum(moved.astype(F32), axis=0)


def adapters_sum(sums, widths, adapter_index, groups):
    per_group = ADAPTERS // groups
    local = sums
    hit = (adapter_index[None, :] == jnp.arange(ADAPTERS)[:, None]).astype(F32)
    spread = jnp.sum(hit[:, :, None, None] * local[None], axis=1).astype(BF)
    spread = spread.reshape(groups, per_group, RANK, -1)
    moved = lax.all_to_all(spread, "dp", split_axis=0, concat_axis=0, tiled=True)
    total = jnp.sum(moved.astype(F32), axis=0)
    outs = []
    at = 0
    for wide in widths:
        outs.append(total[:, :, at : at + wide])
        at += wide
    return outs


def per_device(
    images, norm1_gain, norm1_bias, qkv_weight, qkv_bias, height_table, width_table, proj_weight,
    proj_bias, norm2_gain, norm2_bias, expand_weight, expand_bias, contract_weight, contract_bias,
    adapter_index, qkv_down, qkv_up, proj_down, proj_up, expand_down, expand_up, contract_down,
    contract_up, cotangent,
):
    image_count, row_count, side, _ = images.shape
    ranks = lax.axis_size("rows")
    groups = lax.axis_size("dp")
    rank = lax.axis_index("rows")
    plan = make_plan(ranks, row_count, 1)
    packed = packed_form(groups, ranks)
    pieces_at = piece_table() if packed else np.zeros((groups, ranks, 1), np.int32)
    tables = [np.broadcast_to(plan[k][None], (groups,) + plan[k].shape)
              for k in ("rows", "wins", "info")] + [pieces_at]
    ends = np.cumsum([0] + [t.shape[2] for t in tables])
    mine = jnp.asarray(np.concatenate(tables, 2))[lax.axis_index("dp"), rank]
    rows_code, win_code, info, piece_code = [mine[a:b] for a, b in zip(ends[:-1], ends[1:])]
    rows_block = 4 if row_count % 4 == 0 else row_count
    ff_block = row_count
    place = jnp.asarray(place_matrix(side), BF)
    marks_fwd, marks_bwd = [jnp.asarray(m, BF) for m in key_marks()]
    table_fwd, table_bwd = pair_tables(height_table, width_table)
    zero = jnp.zeros((1, PITCH, D), BF)
    row_vector = lambda v: v.reshape(1, -1)
    picked = adapter_index[:, 0]
    flat_images = images.reshape(image_count * row_count, side, D)
    flat_cotangent = cotangent.reshape(image_count * row_count, side, D)

    adapters = (qkv_down, qkv_up, proj_down, proj_up, expand_down, expand_up, contract_down,
                contract_up)
    whole = [((slice(None),), (slice(None),))]
    gain_one, bias_one = row_vector(norm1_gain), row_vector(norm1_bias)
    split = range(image_count)
    if packed:
        second, own, other, extra = pack(qkv_weight, proj_weight, expand_weight,
                                         contract_weight.T, adapters)
        piece = first_piece(own, other, extra)
        gain_one = after(gain_one, piece)
    sent = [first_norm(flat_images, n, row_count, gain_one, bias_one, place, rows_code, plan,
                       rows_block) for n in split]
    if packed:
        ready, pieces, others, line = gather_first(piece, [v[0] for v in sent])
        second = lax.all_gather(after(second, line), ("rows", "dp"), axis=0, tiled=False)
        units = [exchange([after(v, *ready) for v in sent[n]], plan, False) for n in split]
        others = after(others, *units[0])
        qkv_full, proj_full, down_one, up_one = assemble(pieces, others, piece_code, picked,
                                                         image_count)
        expand_copies, contract_copies, base = second_copies(groups, ranks)
        adapter_copies = second_adapters(base, groups, ranks)
        ff_src = [proj_full, second, second]
        adapter_src = [[second, second]] * image_count
    else:
        units = [exchange(sent[n], plan, False) for n in split]
        weights = (qkv_weight, proj_weight, expand_weight, contract_weight)
        full, chosen = gather_plain(weights, adapters, adapter_index)
        expand_copies = contract_copies = whole
        qkv_full = full[0]
        down_one, up_one = chosen[:2]
        ff_src = full[1:]
        everything = (slice(None),)
        adapter_copies = lambda index: [(h, everything, everything) for h in range(2)]
        adapter_src = plain_stage(chosen[2:], ranks)
    vectors = [row_vector(v) for v in (proj_bias, norm2_gain, norm2_bias, expand_bias,
                                       contract_bias)]
    forward = [attention_forward(units[n], zero, qkv_full, row_vector(qkv_bias), down_one, up_one,
                                 n, table_fwd, marks_fwd, win_code, info, plan) for n in split]
    units = [exchange(forward[n][0], plan, True) for n in split]
    ff = []
    for n in split:
        ff.append(feed_forward(units[n], flat_images, flat_cotangent, n, row_count, ff_src, whole,
                               expand_copies, contract_copies, vectors, adapter_src[n], picked,
                               adapter_copies, place, rows_code, plan, ff_block, ranks,
                               [v for f in ff[-1:] for v in (f[1], f[3])]))
    units = [exchange(ff[n][0], plan, False) for n in split]
    backward = []
    for n in split:
        backward.append(attention_backward(units[n], zero, qkv_full, forward[n][1],
                                           row_vector(qkv_bias), down_one, up_one, n, table_bwd,
                                           marks_bwd, win_code, info, plan, ranks, image_count,
                                           [b[1] for b in backward[-1:]]))
    units = [exchange(backward[n][0], plan, True) for n in split]
    early_sums = after(rows_sum(ff[-1][3]), backward[0][0][0]).reshape(image_count, RANK, -1)
    early = adapters_sum(early_sums, [FF_WIDTHS[k] // ranks for k in FF_KINDS], picked, groups)
    gain_one = after(gain_one, early[0])
    back = []
    for n in split:
        back.append(first_norm_back(units[n], flat_images, ff[n][2], n, row_count, gain_one,
                                    place.T, rows_code, plan, rows_block, back[-1:]))
    late_terms = after(backward[-1][1], back[0])
    late_sums = rows_sum(late_terms).reshape(image_count, RANK, -1)
    late = adapters_sum(late_sums, [D // ranks, 3 * D // ranks], picked, groups)
    return (ff[-1][1].reshape(images.shape), back[-1].reshape(images.shape), *late, *early)


def solution(mesh):
    whole = P()
    both = P("dp", "rows")
    adapter = P("dp", None, "rows")
    image = P("dp", "rows", None, None)
    placed = (image, whole, whole, both, whole, whole, whole, both, whole, whole, whole, both,
              whole, both, whole, P("dp", None), *([adapter] * 8), image)
    return jax.shard_map(
        per_device,
        mesh=mesh,
        in_specs=placed,
        out_specs=(image, image, *([adapter] * 8)),
        check_vma=False,
    )
```

```python
import itertools

import jax
import jax.numpy as jnp
import numpy as np
from jax import lax
from jax.experimental import pallas as pl
from jax.experimental.pallas import tpu as pltpu
from jax.sharding import PartitionSpec as P

HEAD_DIM = 64
WIN = 14
PITCH = 16
ADAPTERS = 8
RANK = 16
GRID = 5
D = 768
FF = 3072
HEADS = 12
PAIRS = HEADS // 2
TOK = WIN * PITCH
KEYS = 256
EPSILON = 1e-06
SQRT_HALF = 0.7071067811865476
INV_SQRT_TAU = 0.3989422804014327
SHIFT = 1024
SHORT = 8
CUT = SHORT * PITCH
BF = jnp.bfloat16
F32 = jnp.float32
VMEM_LIMIT = 60 * 1024 * 1024


def choose_owner(ranks, row_count, images):
    side_rows = ranks * row_count
    total = GRID * GRID * images
    weight = np.array(
        [0.77 if side_rows - (w // (GRID * images)) * WIN <= SHORT else 1.0 for w in range(total)]
    )

    def owner_of(cuts):
        return np.repeat(np.arange(ranks), np.diff([0] + list(cuts) + [total]))

    def cost_of(cuts):
        if min(np.diff([0] + list(cuts) + [total])) < 0:
            return 1e9
        owner = owner_of(cuts)
        load = np.bincount(owner, weights=weight, minlength=ranks).max()
        return 12.0 * load + color_edges(owner, ranks, row_count, images)[0]

    def filled(limit):
        cuts, load = [], 0.0
        for window in range(total):
            if load + weight[window] > limit + 1e-9:
                cuts.append(window)
                load = 0.0
            load += weight[window]
        return cuts + [total] * (ranks - 1 - len(cuts))

    limits = sorted({weight[a:b].sum() for a in range(total) for b in range(a + 1, total + 1)})
    least = next(limit for limit in limits if len(filled(limit)) == ranks - 1)
    reach = np.cumsum(weight) / weight.sum() * ranks
    even = [int(np.searchsorted(reach, r - 0.5)) for r in range(1, ranks)]
    found = (1e10, None)
    for cuts in (filled(least), even):
        best = cost_of(cuts)
        for _ in range(12):
            moved = False
            for place in range(ranks - 1):
                for width in (1, 2, 3):
                    for step in (-1, 1):
                        trial = list(cuts)
                        for extra in range(width):
                            if place + extra < ranks - 1:
                                trial[place + extra] += step
                        cost = cost_of(trial)
                        if cost < best - 1e-9:
                            best, cuts, moved = cost, trial, True
            if not moved:
                break
        if best < found[0] - 1e-9:
            found = (best, list(cuts))
    return owner_of(found[1])


def color_edges(owner, ranks, row_count, images):
    edges = {}
    local = [[] for _ in range(ranks)]
    for rank in range(ranks):
        for img in range(images):
            for k in range(row_count):
                row = rank * row_count + k
                for col in range(GRID):
                    window = (row // WIN) * images * GRID + img * GRID + col
                    unit = (img, k, col, window, row % WIN)
                    if owner[window] == rank:
                        local[rank].append(unit)
                    else:
                        edges.setdefault((rank, int(owner[window])), []).append(unit)
    colors = []
    for (src, dst), units in sorted(edges.items(), key=lambda e: (-len(e[1]), e[0])):
        for color in colors:
            if src not in color["src"] and dst not in color["dst"]:
                break
        else:
            color = {"src": set(), "dst": set(), "pairs": [], "units": []}
            colors.append(color)
        color["src"].add(src)
        color["dst"].add(dst)
        color["pairs"].append((src, dst))
        color["units"].append(units)
    sizes = [max(len(u) for u in c["units"]) for c in colors]
    cost = 0.4 * sum(sizes) + 3.0 * len(sizes)
    return cost, local, colors, sizes


def make_plan(ranks, row_count, images):
    total = GRID * GRID * images
    owner = choose_owner(ranks, row_count, images)
    _, local, colors, sizes = color_edges(owner, ranks, row_count, images)
    kinds = [ranks * row_count - w // (images * GRID) * WIN <= SHORT for w in range(total)]
    heights = [SHORT if short else WIN for short in kinds]
    most = int(np.bincount(owner, weights=heights, minlength=ranks).max())
    full_most = int(np.bincount(owner, weights=~np.array(kinds), minlength=ranks).max())
    short_most = int(np.bincount(owner, weights=np.array(kinds), minlength=ranks).max())
    skip = (len(colors) + 1) * SHIFT
    rows_code = np.full((ranks, images, row_count, GRID), skip, np.int32)
    win_code = np.full((ranks, most), skip, np.int32)
    first = np.searchsorted(owner, np.arange(ranks))

    def put(rank, unit, code, dst):
        img, k, col, window, place = unit
        rows_code[rank, img, k, col] = code
        win_code[dst, sum(heights[first[dst] : window]) + place] = code

    for rank in range(ranks):
        for number, unit in enumerate(local[rank]):
            put(rank, unit, number, rank)
    for which, color in enumerate(colors):
        for (src, dst), units in zip(color["pairs"], color["units"]):
            for number, unit in enumerate(units):
                put(src, unit, (which + 1) * SHIFT + number, dst)
    slot_info = np.zeros((ranks, 3), np.int32)
    for rank in range(ranks):
        mine = [kinds[w] for w in np.flatnonzero(owner == rank)]
        slot_info[rank] = (mine.count(False), mine.count(True),
                           sum(SHORT if short else WIN for short in mine))
    return {
        "rows": rows_code.reshape(ranks, -1),
        "wins": win_code,
        "info": slot_info,
        "units": most,
        "full": full_most,
        "short": short_most,
        "local": max(max(len(u) for u in local), 1),
        "sizes": sizes,
        "pairs": [c["pairs"] for c in colors],
    }


def place_matrix(side):
    out = np.zeros((GRID * PITCH, side), np.float32)
    for token in range(side):
        out[token // WIN * PITCH + token % WIN, token] = 1.0
    return out


def key_marks():
    fwd = np.zeros((2 * KEYS, 128), np.float32)
    bwd = np.zeros((2 * KEYS, 128), np.float32)
    for head in range(2):
        for key in range(KEYS):
            row = head * KEYS + key
            u, w = divmod(key, PITCH)
            if key >= TOK or w >= WIN:
                fwd[row, 14] = -1e30
                continue
            base = 64 * head
            for lane in (base + u, base + 32 + w):
                fwd[row, lane] = 1.0
            bwd[row, base + 13 - u] = 1.0
            bwd[row, base + 32 + 13 - w] = 1.0
    return fwd, bwd


def pair_tables(height_table, width_table):
    rev = jnp.pad(jnp.stack((height_table[::-1], width_table[::-1])), ((0, 0), (2, 3), (0, 0)))
    half = rev.reshape(64, HEAD_DIM).T
    zero = jnp.zeros_like(half)
    fwd = jnp.concatenate(
        (jnp.concatenate((half, zero), 1), jnp.concatenate((zero, half), 1)), 0
    )
    straight = jnp.pad(jnp.stack((height_table, width_table)), ((0, 0), (0, 5), (0, 0)))
    back = straight.reshape(64, HEAD_DIM)
    blank = jnp.zeros_like(back)
    bwd = jnp.concatenate(
        (jnp.concatenate((back, blank), 1), jnp.concatenate((blank, back), 1)), 0
    )
    return fwd, bwd


def nn(a, b):
    return lax.dot_general(a, b, (((1,), (0,)), ((), ())), preferred_element_type=F32)


def nt(a, b):
    return lax.dot_general(a, b, (((1,), (1,)), ((), ())), preferred_element_type=F32)


def tn(a, b):
    return lax.dot_general(a, b, (((0,), (0,)), ((), ())), preferred_element_type=F32)


def start_in(codes, count, bufs, dst, sem):
    def body(u, carry):
        code = codes[u]
        which = code // SHIFT
        index = code % SHIFT
        for number, buf in enumerate(bufs):
            @pl.when(which == number)
            def _():
                pltpu.make_async_copy(buf.at[index], dst.at[u], sem).start()
        return carry

    lax.fori_loop(0, count, body, 0)


def start_out(codes, first, count, src, bufs, spare, sem):
    def body(u, carry):
        code = codes[u]
        which = code // SHIFT
        index = code % SHIFT
        for number, buf in enumerate(bufs):
            @pl.when(which == number)
            def _():
                pltpu.make_async_copy(src.at[u], buf.at[index], sem).start()

        if spare is not None:
            @pl.when(which >= len(bufs))
            def _():
                pltpu.make_async_copy(src.at[u], bufs[0].at[spare + u], sem).start()
        return carry

    lax.fori_loop(first, first + count, body, 0)


def wait_all(whole, sem):
    pltpu.make_async_copy(whole, whole, sem).wait()


def norm_parts(values):
    average = jnp.mean(values, axis=-1, keepdims=True)
    centred = values - average
    variance = jnp.mean(centred * centred, axis=-1, keepdims=True)
    inverse = lax.rsqrt(variance + EPSILON)
    return centred * inverse, inverse


def norm_back(upstream, standard, inverse, gain):
    scaled = upstream * gain
    first_term = jnp.mean(scaled, axis=-1, keepdims=True)
    second_term = jnp.mean(scaled * standard, axis=-1, keepdims=True)
    return inverse * (scaled - first_term - standard * second_term)


def any_specs(count):
    return [pl.BlockSpec(memory_space=pl.ANY)] * count


def full_spec(shape):
    return pl.BlockSpec(shape, lambda *_: (0,) * len(shape))


def unit_shapes(plan):
    counts = [plan["local"] + plan["units"]] + plan["sizes"]
    return [jax.ShapeDtypeStruct((n, PITCH, D), BF) for n in counts]


def after(value, *others):
    return lax.optimization_barrier((value, *others))[0]


def exchange(bufs, plan, back):
    moved = [bufs[0]]
    for buf, pairs in zip(bufs[1:], plan["pairs"]):
        pairs = [(b, a) for a, b in pairs] if back else list(pairs)
        moved.append(lax.ppermute(buf, "rows", pairs))
    return moved


def cost(flops, moved, special=0):
    return pl.CostEstimate(flops=int(flops), bytes_accessed=int(moved), transcendentals=int(special))


def params():
    return pltpu.CompilerParams(vmem_limit_bytes=VMEM_LIMIT)


def rows_plan(images, row_count, rows_block, number):
    side = images.shape[1]
    steps = row_count // rows_block
    spec = pl.BlockSpec((rows_block, side, D), lambda i, *_: (number * steps + i, 0, 0))
    return side, steps, spec


def first_norm(images, number, row_count, gain, bias, place, codes, plan, rows_block):
    side, steps, rows_spec = rows_plan(images, row_count, rows_block, number)
    per_step = rows_block * GRID
    outs = unit_shapes(plan)

    def kernel(codes_ref, x_ref, g_ref, b_ref, p_ref, *rest):
        bufs, scratch, sems = rest[: len(outs)], rest[len(outs)], rest[len(outs) + 1]
        step = pl.program_id(0)
        values = x_ref[...].reshape(rows_block * side, D).astype(F32)
        standard, _ = norm_parts(values)
        normed = (standard * g_ref[...] + b_ref[...]).astype(BF)
        for r in range(rows_block):
            spread = nn(p_ref[...], normed[r * side : (r + 1) * side])
            scratch[pl.ds(step * per_step + r * GRID, GRID)] = spread.astype(BF).reshape(
                GRID, PITCH, D
            )
        start_out(codes_ref, step * per_step, per_step, scratch, bufs, None, sems.at[0])

        @pl.when(step == steps - 1)
        def _():
            wait_all(scratch, sems.at[0])

    return pl.pallas_call(
        kernel,
        out_shape=outs,
        grid_spec=pltpu.PrefetchScalarGridSpec(
            num_scalar_prefetch=1,
            grid=(steps,),
            in_specs=[rows_spec, full_spec((1, D)), full_spec((1, D)), full_spec(place.shape)],
            out_specs=any_specs(len(outs)),
            scratch_shapes=[
                pltpu.VMEM((row_count * GRID, PITCH, D), BF),
                pltpu.SemaphoreType.DMA((1,)),
            ],
        ),
        cost_estimate=cost(1e9, 8e6),
        compiler_params=params(),
        name="first_norm",
    )(codes, images, gain, bias, place)


def image_spec(shape, number):
    return pl.BlockSpec((1,) + shape[1:], lambda *_: (number,) + (0,) * (len(shape) - 1))


def saved_shapes(plan):
    rows = plan["units"] * PITCH
    return [
        jax.ShapeDtypeStruct((rows, D), BF),
        jax.ShapeDtypeStruct((rows, 3 * D), BF),
        jax.ShapeDtypeStruct((rows, RANK), BF),
        jax.ShapeDtypeStruct((PAIRS, rows, 2 * KEYS), BF),
        jax.ShapeDtypeStruct((rows, D), F32),
        jax.ShapeDtypeStruct((rows, D), BF),
    ]


def each_slot(info_ref, plan, body):
    n_full = info_ref[0]
    if plan["full"]:
        def full(slot, carry):
            body(pl.multiple_of(slot * TOK, 32), TOK, slot)
            return carry

        lax.fori_loop(0, n_full, full, 0)
    if plan["short"]:
        def short(slot, carry):
            body(pl.multiple_of(n_full * TOK + slot * CUT, 32), CUT, n_full + slot)
            return carry

        lax.fori_loop(0, info_ref[1], short, 0)


def key_value(mixed_ref, bias_low, at, rows, j):
    out = []
    for part in (1, 2):
        cols = slice(part * D + 128 * j, part * D + 128 * j + 128)
        own = mixed_ref[pl.ds(at, rows), cols]
        if rows < TOK:
            rest = jnp.broadcast_to(bias_low[:, cols], (TOK - rows, 128))
            own = jnp.concatenate((own, rest), 0)
        out.append(own)
    return out[0] * jnp.asarray(HEAD_DIM ** -0.5, BF), out[1]


def fill_heads(ref, value, low_half):
    nil = jnp.zeros_like(value)
    ref[0:TOK, 0:128] = jnp.where(low_half, value, nil)
    ref[KEYS : KEYS + TOK, 0:128] = jnp.where(low_half, nil, value)


def attention_forward(units, zero, weight, qkv_bias, down, up, number, table, marks, codes, info,
                      plan):
    outs = unit_shapes(plan)
    n_buf = len(outs)
    n_units = plan["units"]
    n_rows = n_units * PITCH
    n_slots = plan["full"] + plan["short"]

    def kernel(codes_ref, info_ref, *refs):
        in_bufs = refs[: n_buf + 1]
        w_src, bias_ref, down_ref, up_ref, table_ref, marks_ref = refs[n_buf + 1 : n_buf + 7]
        refs = refs[n_buf + 7 :]
        out_bufs = refs[:n_buf]
        win_out, mixed_out, inner_out, prob_out, inv_out, att_out = refs[n_buf : n_buf + 6]
        (x_in, x_out, w_vmem, keys, vals, mixed_ref, inner_ref, prob_ref, inv_ref, in_sems,
         out_sems, w_sems, save_sems, prob_sems) = refs[n_buf + 6 :]
        used = info_ref[2]
        fetches = []
        for part in range(3):
            rows = slice(part * D, (part + 1) * D)
            fetches.append(pltpu.make_async_copy(w_src.at[rows], w_vmem.at[rows], w_sems.at[part]))
            fetches[-1].start()
        start_in(codes_ref, n_units, in_bufs, x_in, in_sems.at[0])
        bias_low = bias_ref[...].astype(BF)
        lane = lax.broadcasted_iota(jnp.int32, (KEYS, 128), 1)
        for twin in range(2):
            keys[twin, :, 0:128] = jnp.zeros((2 * KEYS, 128), BF)
            keys[twin, :, 128:256] = marks_ref[...]
            vals[twin, :, 0:128] = jnp.zeros((2 * KEYS, 128), BF)
            vals[twin, 0:KEYS, 128:256] = (lane < 64).astype(BF)
            vals[twin, KEYS:, 128:256] = (lane >= 64).astype(BF)

        wait_all(x_in, in_sems.at[0])
        x = x_in[...].reshape(n_rows, D)
        saves = [pltpu.make_async_copy(x_in, win_out, save_sems.at[0])]
        inner = nt(x, down_ref[0]).astype(BF)
        inner_ref[...] = inner
        def part_columns(part, carry):
            rows = pl.ds(pl.multiple_of(part * D, D), D)
            pltpu.make_async_copy(w_src.at[rows], w_vmem.at[rows], w_sems.at[part]).wait()
            mixed = nt(x_in[...].reshape(n_rows, D), w_vmem[rows])
            mixed = mixed + bias_ref[:, rows] + nn(inner_ref[...], up_ref[0, :, rows])
            mixed_ref[:, rows] = mixed.astype(BF)
            return carry

        lax.fori_loop(0, 3, part_columns, 0)
        saves.append(pltpu.make_async_copy(mixed_ref, mixed_out, save_sems.at[1]))
        saves.append(pltpu.make_async_copy(inner_ref, inner_out, save_sems.at[2]))
        for save in saves:
            save.start()
        small = lax.broadcasted_iota(jnp.int32, (PITCH, 128), 1)
        low_half = lax.broadcasted_iota(jnp.int32, (TOK, 128), 1) < 64

        def attend(at, rows, slot):
            for j in range(PAIRS):
                twin = j % 2
                key, value = key_value(mixed_ref, bias_low, at, rows, j)
                fill_heads(keys.at[twin], key, low_half)
                fill_heads(vals.at[twin], value, low_half)
                cols = slice(128 * j, 128 * j + 128)
                q = mixed_ref[pl.ds(at, rows), cols]
                rel = nn(q, table_ref[...])
                pieces = []
                for x_at in range(rows // PITCH):
                    slab = rel[PITCH * x_at : PITCH * x_at + PITCH]
                    tall = pltpu.roll(slab, 113 + x_at, 1)
                    wide = pltpu.roll(slab, 113, 1, stride=1, stride_axis=0)
                    both = jnp.where(small % 64 < 32, tall, wide)
                    pieces.append(jnp.where(small == 14, 1.0, both).astype(BF))
                query = jnp.concatenate((q, jnp.concatenate(pieces, 0)), 1)
                scores = nt(query, keys[twin])
                probs = []
                for head in range(2):
                    part = scores[:, KEYS * head : KEYS * head + KEYS]
                    top = jnp.max(part, axis=-1, keepdims=True)
                    probs.append(jnp.exp(part - top).astype(BF))
                prob = jnp.concatenate(probs, 1)
                prob_ref[j, pl.ds(at, rows)] = prob
                summed = nn(prob, vals[twin])
                inverse = 1.0 / summed[:, 128:256]
                inv_ref[pl.ds(at, rows), cols] = inverse
                att = (summed[:, 0:128] * inverse).astype(BF)
                x_out[pl.ds(at // PITCH, rows // PITCH), :, cols] = att.reshape(
                    rows // PITCH, PITCH, 128
                )
            span = pl.ds(at, rows)
            pltpu.make_async_copy(prob_ref.at[:, span], prob_out.at[:, span],
                                  prob_sems.at[slot, 0]).start()
            pltpu.make_async_copy(inv_ref.at[span], inv_out.at[span], prob_sems.at[slot, 1]).start()
            start_out(codes_ref, at // PITCH, rows // PITCH, x_out, out_bufs, None, out_sems.at[0])

        each_slot(info_ref, plan, attend)
        start_out(codes_ref, used, n_units - used, x_out, out_bufs, plan["local"], out_sems.at[0])
        save = pltpu.make_async_copy(x_out, att_out, save_sems.at[3])
        save.start()

        def finish(at, rows, slot):
            span = pl.ds(at, rows)
            pltpu.make_async_copy(prob_ref.at[:, span], prob_out.at[:, span],
                                  prob_sems.at[slot, 0]).wait()
            pltpu.make_async_copy(inv_ref.at[span], inv_out.at[span], prob_sems.at[slot, 1]).wait()

        wait_all(x_out, out_sems.at[0])
        each_slot(info_ref, plan, finish)
        for one in saves + [save]:
            one.wait()

    saved = saved_shapes(plan)
    boxed = jax.ShapeDtypeStruct((n_units, PITCH, D), BF)
    results = pl.pallas_call(
        kernel,
        out_shape=outs + [boxed] + saved[1:5] + [boxed],
        grid_spec=pltpu.PrefetchScalarGridSpec(
            num_scalar_prefetch=2,
            grid=(1,),
            in_specs=any_specs(n_buf + 2)
            + [
                full_spec((1, 3 * D)),
                image_spec(down.shape, number),
                image_spec(up.shape, number),
                full_spec(table.shape),
                full_spec(marks.shape),
            ],
            out_specs=any_specs(n_buf + 6),
            scratch_shapes=[
                pltpu.VMEM((n_units, PITCH, D), BF),
                pltpu.VMEM((n_units, PITCH, D), BF),
                pltpu.VMEM((3 * D, D), BF),
                pltpu.VMEM((2, 2 * KEYS, 256), BF),
                pltpu.VMEM((2, 2 * KEYS, 256), BF),
                pltpu.VMEM((n_rows, 3 * D), BF),
                pltpu.VMEM((n_rows, RANK), BF),
                pltpu.VMEM((PAIRS, n_rows, 2 * KEYS), BF),
                pltpu.VMEM((n_rows, D), F32),
                pltpu.SemaphoreType.DMA((1,)),
                pltpu.SemaphoreType.DMA((1,)),
                pltpu.SemaphoreType.DMA((3,)),
                pltpu.SemaphoreType.DMA((4,)),
                pltpu.SemaphoreType.DMA((n_slots, 2)),
            ],
        ),
        cost_estimate=cost(10e9, 20e6, 4e6),
        compiler_params=params(),
        name="attention_forward",
    )(codes, info, *units, zero, weight, qkv_bias, down, up, table, marks)
    return results[:n_buf], results[n_buf:]


FF_KINDS = ("pd", "pu", "ed", "eu", "cd", "cu")
HALVES = (("eu", "pd", "pu", "ed", "cu"), ("cd",))
FF_WIDTHS = {"pd": D, "pu": D, "ed": D, "eu": FF, "cd": FF, "cu": D}


def stage_pieces(ranks):
    for h, kinds in enumerate(HALVES):
        at = 0
        for kind in kinds:
            wide = FF_WIDTHS[kind] // ranks
            yield h, at, wide, kind
            at += wide


def feed_forward(units, images, cotangent, number, row_count, weight_src, proj_copies,
                 expand_copies, contract_copies, vectors, adapter_src, adapter_index,
                 adapter_copies, place, codes, plan, rows_block, ranks, previous):
    side, steps, rows_spec = rows_plan(images, row_count, rows_block, number)
    per_step = rows_block * GRID
    tokens = rows_block * side
    outs = unit_shapes(plan)
    n_buf = len(outs)
    copies = [proj_copies, expand_copies, contract_copies]
    chunk = 512
    chunks = FF // chunk
    n_src = len(weight_src)
    stage_width = 2 * FF // ranks
    n_prev = len(previous)
    term_width = 3 * FF // ranks
    at_prev = 2 + n_buf + 2 + n_src + 5 + 4

    def kernel(codes_ref, pick_ref, *refs):
        in_bufs, refs = refs[:n_buf], refs[n_buf:]
        img_ref, cot_ref, refs = refs[0], refs[1], refs[2:]
        w_src, refs = refs[:n_src], refs[n_src:]
        (bp, g2, b2, be, bc), refs = refs[:5], refs[5:]
        a_src, place_ref, placet_ref, refs = refs[0:2], refs[2], refs[3], refs[4 + n_prev :]
        out_bufs, refs = refs[:n_buf], refs[n_buf:]
        block_ref, mid_ref, terms_ref, refs = refs[0], refs[1], refs[2], refs[3:]
        (pd, pu, ed, eu, cd, cu), refs = refs[:6], refs[6:]
        (d_pd, d_pu, d_ed, d_eu, d_cd, d_cu), refs = refs[:6], refs[6:]
        (u_in, u_out, wp, we, wc, stage_a, stage_b, acc_result, acc_second, in_sems, out_sems,
         w_sems, s_sems) = refs
        adapters = dict(zip(FF_KINDS, (pd, pu, ed, eu, cd, cu)))
        grads = dict(zip(FF_KINDS, (d_pd, d_pu, d_ed, d_eu, d_cd, d_cu)))
        step = pl.program_id(0)
        targets = [wp, we, wc]

        def weights(which):
            for src, dst in copies[which]:
                pltpu.make_async_copy(
                    w_src[which].at[src], targets[which].at[dst], w_sems.at[which]
                ).start()

        @pl.when(step == 0)
        def _():
            stages = (stage_a, stage_b)
            for half, src, dst in adapter_copies(pick_ref[number]):
                pltpu.make_async_copy(a_src[half].at[src], stages[half].at[dst],
                                      s_sems.at[half]).start()
            start_in(codes_ref, row_count * GRID, in_bufs, u_in, in_sems.at[0])
            for which in range(3):
                weights(which)
            for grad in grads.values():
                grad[...] = jnp.zeros_like(grad)
            wait_all(stage_a, s_sems.at[0])
            wait_all(stage_b, s_sems.at[1])
            for h, at, wide, kind in stage_pieces(ranks):
                for r in range(ranks):
                    adapters[kind][:, wide * r : wide * r + wide] = stages[h][
                        r, :, at : at + wide
                    ]
            wait_all(wp, w_sems.at[0])
            wait_all(u_in, in_sems.at[0])

        rows = []
        for r in range(rows_block):
            spread = u_in[pl.ds(step * per_step + r * GRID, GRID)].reshape(GRID * PITCH, D)
            rows.append(nn(placet_ref[...], spread).astype(BF))
        att = jnp.concatenate(rows, 0)
        cot = cot_ref[...].reshape(tokens, D)
        p_inner = nt(att, pd[...]).astype(BF)
        middle = (
            img_ref[...].reshape(tokens, D).astype(F32)
            + nt(att, wp[...])
            + bp[...]
            + nn(p_inner, pu[...])
        )
        standard, inverse = norm_parts(middle)
        second = (standard * g2[...] + b2[...]).astype(BF)
        e_inner = nt(second, ed[...]).astype(BF)
        c_mid = nt(cot, cu[...]).astype(BF)
        c_inner = jnp.zeros((tokens, RANK), F32)
        e_mid = jnp.zeros((tokens, RANK), F32)

        @pl.when(step == 0)
        def _():
            wait_all(we, w_sems.at[1])
            wait_all(wc, w_sems.at[2])

        acc_result[...] = middle + bc[...]
        acc_second[...] = jnp.zeros((tokens, D), F32)

        def one_chunk(n, carry):
            c_inner, e_mid = carry
            cols = pl.ds(pl.multiple_of(n * chunk, chunk), chunk)
            hidden = nn(second, we[:, cols]) + be[:, cols] + nn(e_inner, eu[:, cols])
            cdf = 0.5 * (1.0 + lax.erf(hidden * SQRT_HALF))
            slope = cdf + hidden * jnp.exp(-0.5 * hidden * hidden) * INV_SQRT_TAU
            active = (hidden * cdf).astype(BF)
            a_grad = nn(cot, wc[:, cols]) + nn(c_mid, cd[:, cols])
            h_grad = (a_grad * slope).astype(BF)
            acc_result[...] += nt(active, wc[:, cols])
            c_inner = c_inner + nt(active, cd[:, cols])
            acc_second[...] += nt(h_grad, we[:, cols])
            e_mid = e_mid + nt(h_grad, eu[:, cols])
            d_cd[:, cols] += tn(c_mid, active)
            d_eu[:, cols] += tn(e_inner, h_grad)
            return c_inner, e_mid

        c_inner, e_mid = lax.fori_loop(0, chunks, one_chunk, (c_inner, e_mid))
        result = acc_result[...]
        second_grad = acc_second[...]
        c_inner = c_inner.astype(BF)
        e_mid = e_mid.astype(BF)
        result = result + nn(c_inner, cu[...])
        block_ref[...] = result.astype(BF).reshape(rows_block, side, D)
        d_cu[...] += tn(c_inner, cot)
        d_ed[...] += tn(e_mid, second)
        second_grad = second_grad + nn(e_mid, ed[...])
        middle_grad = cot.astype(F32) + norm_back(second_grad, standard, inverse, g2[...])
        mid_ref[...] = middle_grad.reshape(rows_block, side, D)
        branch = middle_grad.astype(BF)
        p_mid = nt(branch, pu[...]).astype(BF)
        d_pu[...] += tn(p_inner, branch)
        d_pd[...] += tn(p_mid, att)
        att_grad = (nn(branch, wp[...]) + nn(p_mid, pd[...])).astype(BF)
        for r in range(rows_block):
            spread = nn(place_ref[...], att_grad[r * side : (r + 1) * side])
            u_out[pl.ds(step * per_step + r * GRID, GRID)] = spread.astype(BF).reshape(
                GRID, PITCH, D
            )
        start_out(codes_ref, step * per_step, per_step, u_out, out_bufs, None, out_sems.at[0])

        @pl.when(step == steps - 1)
        def _():
            at = 0
            for kind in FF_KINDS:
                wide = FF_WIDTHS[kind] // ranks
                for r in range(ranks):
                    terms_ref[r, :, at : at + wide] = grads[kind][
                        :, wide * r : wide * r + wide
                    ].astype(BF)
                at += wide
            if at < term_width:
                terms_ref[:, :, at:] = jnp.zeros((ranks, RANK, term_width - at), BF)
            wait_all(u_out, out_sems.at[0])

    results = pl.pallas_call(
        kernel,
        out_shape=outs
        + [
            jax.ShapeDtypeStruct(images.shape, BF),
            jax.ShapeDtypeStruct((row_count, side, D), F32),
            jax.ShapeDtypeStruct((ranks, images.shape[0] // row_count * RANK, term_width), BF),
        ],
        grid_spec=pltpu.PrefetchScalarGridSpec(
            num_scalar_prefetch=2,
            grid=(steps,),
            in_specs=any_specs(n_buf)
            + [rows_spec, rows_spec]
            + any_specs(n_src)
            + [full_spec(v.shape) for v in vectors]
            + any_specs(2)
            + [full_spec(place.shape), full_spec(place.shape[::-1])]
            + any_specs(n_prev),
            out_specs=any_specs(n_buf)
            + [
                rows_spec,
                pl.BlockSpec((rows_block, side, D), lambda i, *_: (i, 0, 0)),
                pl.BlockSpec((ranks, RANK, term_width), lambda *_: (0, number, 0)),
            ],
            scratch_shapes=[pltpu.VMEM((RANK, FF_WIDTHS[k]), BF) for k in FF_KINDS]
            + [pltpu.VMEM((RANK, FF_WIDTHS[k]), F32) for k in FF_KINDS]
            + [
                pltpu.VMEM((row_count * GRID, PITCH, D), BF),
                pltpu.VMEM((row_count * GRID, PITCH, D), BF),
                pltpu.VMEM((D, D), BF),
                pltpu.VMEM((D, FF), BF),
                pltpu.VMEM((D, FF), BF),
                pltpu.VMEM((ranks, RANK, stage_width), BF),
                pltpu.VMEM((ranks, RANK, FF // ranks), BF),
                pltpu.VMEM((tokens, D), F32),
                pltpu.VMEM((tokens, D), F32),
                pltpu.SemaphoreType.DMA((1,)),
                pltpu.SemaphoreType.DMA((1,)),
                pltpu.SemaphoreType.DMA((3,)),
                pltpu.SemaphoreType.DMA((2,)),
            ],
        ),
        input_output_aliases={at_prev: n_buf, at_prev + 1: n_buf + 2} if n_prev else {},
        cost_estimate=cost(18e9, 20e6, 4e6),
        compiler_params=params(),
        name="feed_forward",
    )(codes, adapter_index, *units, images, cotangent, *weight_src, *vectors, *adapter_src, place,
      place.T, *previous)
    return results[:n_buf], results[n_buf], results[n_buf + 1], results[n_buf + 2]


def attention_backward(units, zero, weight, saved, qkv_bias, down, up, number, table, marks, codes,
                       info, plan, ranks, image_count, previous):
    outs = unit_shapes(plan)
    n_buf = len(outs)
    n_units = plan["units"]
    n_rows = n_units * PITCH
    n_slots = plan["full"] + plan["short"]
    term_width = 4 * D // ranks

    def kernel(codes_ref, info_ref, *refs):
        in_bufs, refs = refs[: n_buf + 1], refs[n_buf + 1 :]
        w_src, refs = refs[0], refs[1:]
        (win_src, mixed_src, inner_src, prob_src, inv_src, att_src), refs = refs[:6], refs[6:]
        bias_ref, down_ref, up_ref, table_ref, marks_ref = refs[:5]
        refs = refs[5 + len(previous) :]
        out_bufs, refs = refs[:n_buf], refs[n_buf:]
        terms_ref, refs = refs[0], refs[1:]
        (g_in, x_out, w_vmem, keys, vals, grads, win_ref, mixed_ref, inner_ref, prob_ref, inv_ref,
         att_ref, in_sems, out_sems, load_sems, prob_sems) = refs
        used = info_ref[2]
        start_in(codes_ref, n_units, in_bufs, g_in, in_sems.at[0])
        loads = [
            pltpu.make_async_copy(src, dst, load_sems.at[n])
            for n, (src, dst) in enumerate(
                ((mixed_src, mixed_ref), (att_src, att_ref), (inner_src, inner_ref),
                 (win_src, win_ref), (w_src, w_vmem)))
        ]

        def slot_loads(at, rows, slot):
            span = pl.ds(at, rows)
            return (
                pltpu.make_async_copy(prob_src.at[:, span], prob_ref.at[:, span],
                                      prob_sems.at[slot, 0]),
                pltpu.make_async_copy(inv_src.at[span], inv_ref.at[span], prob_sems.at[slot, 1]),
            )

        def begin(at, rows, slot):
            for copy in slot_loads(at, rows, slot):
                copy.start()

        for load in loads[:2]:
            load.start()
        each_slot(info_ref, plan, begin)
        for load in loads[2:]:
            load.start()
        bias_low = bias_ref[...].astype(BF)
        for twin in range(2):
            keys[twin, :, 0:128] = jnp.zeros((2 * KEYS, 128), BF)
            keys[twin, :, 128:256] = marks_ref[...]
            vals[twin] = jnp.zeros((2 * KEYS, 128), BF)

        def clear(unit, carry):
            grads[pl.ds(pl.multiple_of(unit * PITCH, PITCH), PITCH)] = jnp.zeros((PITCH, 3 * D), BF)
            return carry

        lax.fori_loop(used, n_units, clear, 0)
        loads[0].wait()
        loads[1].wait()
        wait_all(g_in, in_sems.at[0])
        small = lax.broadcasted_iota(jnp.int32, (PITCH, 128), 1)
        low_half = lax.broadcasted_iota(jnp.int32, (TOK, 128), 1) < 64

        def attend(at, rows, slot):
            for copy in slot_loads(at, rows, slot):
                copy.wait()
            span = pl.ds(at, rows)
            half = low_half[:rows]
            for j in range(PAIRS):
                twin = j % 2
                cols = slice(128 * j, 128 * j + 128)
                key, value = key_value(mixed_ref, bias_low, at, rows, j)
                fill_heads(keys.at[twin], key, low_half)
                fill_heads(vals.at[twin], value, low_half)
                q = mixed_ref[span, cols]
                units_at = pl.ds(at // PITCH, rows // PITCH)
                grad = g_in[units_at, :, cols].reshape(rows, 128).astype(F32) * inv_ref[span, cols]
                grad_low = grad.astype(BF)
                weighed = grad * att_ref[units_at, :, cols].reshape(rows, 128).astype(F32)
                total = jnp.sum(weighed, axis=-1, keepdims=True)
                dot_a = jnp.sum(jnp.where(half, weighed, 0.0), axis=-1, keepdims=True)
                dots = (dot_a, total - dot_a)
                soft = nt(grad_low, vals[twin])
                pieces = []
                for head in range(2):
                    lanes = slice(KEYS * head, KEYS * head + KEYS)
                    prob = prob_ref[j, span, lanes].astype(F32)
                    pieces.append((prob * (soft[:, lanes] - dots[head])).astype(BF))
                both = nn(jnp.concatenate(pieces, 1), keys[twin])
                rel = both[:, 128:256]
                unrolled = []
                for x_at in range(rows // PITCH):
                    slab = rel[PITCH * x_at : PITCH * x_at + PITCH]
                    tall = pltpu.roll(slab, x_at, 1) if x_at else slab
                    wide = pltpu.roll(slab, 0, 1, stride=1, stride_axis=0)
                    unrolled.append(jnp.where(small % 64 < 32, tall, wide).astype(BF))
                q_grad = both[:, 0:128] + nn(jnp.concatenate(unrolled, 0), table_ref[...])
                grads[span, cols] = q_grad.astype(BF)
                nil = jnp.zeros_like(q)
                k_grad = jnp.zeros((KEYS, 128), F32)
                v_grad = jnp.zeros((KEYS, 128), F32)
                for head in range(2):
                    lanes = slice(KEYS * head, KEYS * head + KEYS)
                    mine = half if head == 0 else jnp.logical_not(half)
                    k_grad += tn(pieces[head], jnp.where(mine, q, nil))
                    v_grad += tn(prob_ref[j, span, lanes], jnp.where(mine, grad_low, nil))
                k_grad = k_grad[:rows] * HEAD_DIM ** -0.5
                v_grad = v_grad[:rows]
                grads[span, D + 128 * j : D + 128 * j + 128] = k_grad.astype(BF)
                grads[span, 2 * D + 128 * j : 2 * D + 128 * j + 128] = v_grad.astype(BF)

        each_slot(info_ref, plan, attend)
        for load in loads[2:]:
            load.wait()
        mixed_grad = grads[...]
        mid = nt(mixed_grad, up_ref[0]).astype(BF)

        def some_columns(piece, carry):
            cols = pl.ds(pl.multiple_of(piece * 256, 256), 256)
            normed = nn(grads[...], w_vmem[:, cols]) + nn(mid, down_ref[0, :, cols])
            x_out[:, :, cols] = normed.astype(BF).reshape(n_units, PITCH, 256)
            return carry

        lax.fori_loop(0, 3, some_columns, 0)
        start_out(codes_ref, 0, n_units, x_out, out_bufs, plan["local"], out_sems.at[0])
        d_up = tn(inner_ref[...], mixed_grad).astype(BF)
        d_down = tn(mid, win_ref[...].reshape(n_rows, D)).astype(BF)
        at = 0
        for value, wide in ((d_down, D // ranks), (d_up, 3 * D // ranks)):
            for r in range(ranks):
                terms_ref[r, :, at : at + wide] = value[:, wide * r : wide * r + wide]
            at += wide
        wait_all(x_out, out_sems.at[0])

    results = pl.pallas_call(
        kernel,
        out_shape=outs + [jax.ShapeDtypeStruct((ranks, image_count * RANK, term_width), BF)],
        grid_spec=pltpu.PrefetchScalarGridSpec(
            num_scalar_prefetch=2,
            grid=(1,),
            in_specs=any_specs(n_buf + 8)
            + [full_spec((1, 3 * D)), image_spec(down.shape, number), image_spec(up.shape, number),
               full_spec(table.shape), full_spec(marks.shape)] + any_specs(len(previous)),
            out_specs=any_specs(n_buf)
            + [pl.BlockSpec((ranks, RANK, term_width), lambda *_: (0, number, 0))],
            scratch_shapes=[
                pltpu.VMEM((n_units, PITCH, D), BF),
                pltpu.VMEM((n_units, PITCH, D), BF),
                pltpu.VMEM((3 * D, D), BF),
                pltpu.VMEM((2, 2 * KEYS, 256), BF),
                pltpu.VMEM((2, 2 * KEYS, 128), BF),
                pltpu.VMEM((n_rows, 3 * D), BF),
                pltpu.VMEM((n_units, PITCH, D), BF),
                pltpu.VMEM((n_rows, 3 * D), BF),
                pltpu.VMEM((n_rows, RANK), BF),
                pltpu.VMEM((PAIRS, n_rows, 2 * KEYS), BF),
                pltpu.VMEM((n_rows, D), F32),
                pltpu.VMEM((n_units, PITCH, D), BF),
                pltpu.SemaphoreType.DMA((1,)),
                pltpu.SemaphoreType.DMA((1,)),
                pltpu.SemaphoreType.DMA((5,)),
                pltpu.SemaphoreType.DMA((n_slots, 2)),
            ],
        ),
        input_output_aliases={2 + n_buf + 8 + 5: n_buf} if previous else {},
        cost_estimate=cost(12e9, 20e6, 4e6),
        compiler_params=params(),
        name="attention_backward",
    )(codes, info, *units, zero, weight, *saved, qkv_bias, down, up, table, marks, *previous)
    return results[:n_buf], results[n_buf]


def first_norm_back(units, images, middle_grad, number, row_count, gain, place_t, codes, plan,
                    rows_block, previous):
    side, steps, rows_spec = rows_plan(images, row_count, rows_block, number)
    per_step = rows_block * GRID
    n_buf = len(units)
    n_prev = len(previous)

    def kernel(codes_ref, *refs):
        in_bufs, refs = refs[:n_buf], refs[n_buf:]
        x_ref, m_ref, g_ref, p_ref, refs = refs[0], refs[1], refs[2], refs[3], refs[4 + n_prev :]
        out_ref, u_in, sems = refs
        step = pl.program_id(0)

        @pl.when(step == 0)
        def _():
            start_in(codes_ref, row_count * GRID, in_bufs, u_in, sems.at[0])

        values = x_ref[...].reshape(rows_block * side, D).astype(F32)
        standard, inverse = norm_parts(values)

        @pl.when(step == 0)
        def _():
            wait_all(u_in, sems.at[0])

        rows = []
        for r in range(rows_block):
            spread = u_in[pl.ds(step * per_step + r * GRID, GRID)].reshape(GRID * PITCH, D)
            rows.append(nn(p_ref[...], spread))
        upstream = jnp.concatenate(rows, 0)
        back = norm_back(upstream, standard, inverse, g_ref[...])
        out_ref[...] = m_ref[...] + back.reshape(rows_block, side, D)

    return pl.pallas_call(
        kernel,
        out_shape=jax.ShapeDtypeStruct(images.shape, F32),
        grid_spec=pltpu.PrefetchScalarGridSpec(
            num_scalar_prefetch=1,
            grid=(steps,),
            in_specs=any_specs(n_buf)
            + [
                rows_spec,
                pl.BlockSpec((rows_block, side, D), lambda i, *_: (i, 0, 0)),
                full_spec((1, D)),
                full_spec(place_t.shape),
            ]
            + any_specs(n_prev),
            out_specs=rows_spec,
            scratch_shapes=[
                pltpu.VMEM((row_count * GRID, PITCH, D), BF),
                pltpu.SemaphoreType.DMA((1,)),
            ],
        ),
        input_output_aliases={1 + n_buf + 4: 0} if n_prev else {},
        cost_estimate=cost(1e9, 8e6),
        compiler_params=params(),
        name="first_norm_back",
    )(codes, *units, images, middle_grad, gain, place_t, *previous)


KINDS = ("qd", "qu", "pd", "pu", "ed", "eu", "cd", "cu")
WIDTHS = {"qd": D, "qu": 3 * D, "pd": D, "pu": D, "ed": D, "eu": FF, "cd": FF, "cu": D}


def packed_form(groups, ranks):
    return groups == 4 and ranks == 8


def shift_z(value, step):
    return lax.ppermute(value, "rows", [(r, (r + 2 * step) % 8) for r in range(8)])


def flip_y(value):
    return lax.ppermute(value, "rows", [(r, r ^ 1) for r in range(8)])


def flip_x(value):
    return lax.ppermute(value, "dp", [(d, d ^ 2) for d in range(4)])


def flip_core(value):
    return lax.ppermute(value, "dp", [(d, d ^ 1) for d in range(4)])


NQ, NP = 144, 48
MOVES = ((0, 0, 0), (0, 0, 1), (0, 1, 0), (0, 1, 1), (1, 0, 0), (1, 0, 1), (1, 1, 0), (1, 1, 1),
         (0, 0, 2), (0, 0, 3), (1, 0, 2), (1, 0, 3), (0, 1, 2), (0, 1, 3), (1, 1, 2), (1, 1, 3))


def piece_table():
    table = np.zeros((4, 8, 32), np.int32)
    for d in range(4):
        for r in range(8):
            for number, (kx, ky, kz) in enumerate(MOVES):
                for kc in range(2):
                    source_d = (d ^ (2 * kx)) ^ kc
                    source_r = ((r // 2 - kz) % 4) * 2 + ((r % 2) ^ ky)
                    table[d, r, source_r * 4 + source_d] = 16 * kc + number
    return table


def pack(qkv, proj, expand, contract, adapters):
    core = (lax.axis_index("dp") % 2).reshape(1)
    rows = qkv.shape[0]
    ne, nc = expand.shape[0] // 2, contract.shape[0]
    n_ad = len(adapters)
    lists = KINDS

    def kernel(core_ref, q_ref, p_ref, e_ref, c_ref, *refs):
        ads = dict(zip(lists, refs[:n_ad]))
        second, own, other, extra = refs[n_ad:]

        def turned(value):
            wide = value.shape[1]
            eye = (
                lax.broadcasted_iota(jnp.int32, (wide, wide), 0)
                == lax.broadcasted_iota(jnp.int32, (wide, wide), 1)
            )
            return nt(eye.astype(F32).astype(BF), value).astype(BF)

        q_t = turned(q_ref[...])
        p_t = turned(p_ref[...])
        for half, chosen in ((0, 0), (1, 1)):
            @pl.when(core_ref[0] == chosen)
            def _():
                own[0:NQ] = q_t[half * NQ : half * NQ + NQ]
                own[NQ:] = p_t[half * NP : half * NP + NP]
                other[0:NQ] = q_t[(1 - half) * NQ : (1 - half) * NQ + NQ]
                other[NQ:] = p_t[(1 - half) * NP : (1 - half) * NP + NP]

        second[0:ne, 0 : expand.shape[1]] = e_ref[0:ne]
        second[0:ne, expand.shape[1] :] = e_ref[ne:]
        second[ne : ne + nc] = c_ref[...]
        base = ne + nc
        for i in range(2):
            rows_i = slice(base + i * RANK, base + i * RANK + RANK)
            at = 0
            for kind in HALVES[0]:
                wide = ads[kind].shape[2]
                second[rows_i, at : at + wide] = ads[kind][i]
                at += wide
            wide = ads["cd"].shape[2]
            second[base + 2 * RANK :, i * wide : i * wide + wide] = ads["cd"][i]
            at = ads["qu"].shape[2]
            extra[i * RANK : i * RANK + RANK, 0:at] = ads["qu"][i]
            extra[i * RANK : i * RANK + RANK, at:] = ads["qd"][i]

    shapes = [(ne + nc + 3 * RANK, D), (NQ + NP, rows), (NQ + NP, rows), (2 * RANK, 384)]
    return pl.pallas_call(
        kernel,
        out_shape=[jax.ShapeDtypeStruct(shape, BF) for shape in shapes],
        grid_spec=pltpu.PrefetchScalarGridSpec(
            num_scalar_prefetch=1,
            grid=(1,),
            in_specs=[full_spec(v.shape) for v in (qkv, proj, expand, contract) + adapters],
            out_specs=[full_spec(shape) for shape in shapes],
        ),
        cost_estimate=cost(1e8, 2e6),
        compiler_params=params(),
        name="pack",
    )(core, qkv, proj, expand, contract, *adapters)


def first_piece(own, other, extra):
    core = lax.axis_index("dp") % 2
    other = flip_core(other)
    joined = jnp.where(
        core == 0, jnp.concatenate((own, other), 1), jnp.concatenate((other, own), 1)
    )
    return jnp.concatenate((joined, extra), 0)


def gather_first(piece, norms):
    line = jnp.stack([piece] + [shift_z(piece, k) for k in (1, 2, 3)])
    line = after(line, *norms)
    left, right = line[:2], line[2:]
    left = jnp.concatenate((left, flip_y(left)))
    right = jnp.concatenate((right, flip_x(right)))
    left, right = lax.optimization_barrier((left, right))
    pieces = jnp.concatenate((left, flip_x(left), right, flip_y(right)))
    return (left, right), pieces, flip_core(pieces), line


def assemble(pieces, others, table, adapter_index, image_count):
    def kernel(table_ref, pick_ref, a_ref, b_ref, wq, wp, down_ref, up_ref, stage, w_sems, s_sems):
        def fetch(block, src_rows, dst, sem):
            code = table_ref[block]
            index = code % 16

            @pl.when(code < 16)
            def _():
                pltpu.make_async_copy(a_ref.at[index, src_rows], dst, sem).start()

            @pl.when(code >= 16)
            def _():
                pltpu.make_async_copy(b_ref.at[index, src_rows], dst, sem).start()

        for n in range(image_count):
            chosen = pick_ref[n]
            rows = pl.ds(pl.multiple_of(NQ + NP + RANK * (chosen % 2), 16), RANK)
            for r in range(8):
                fetch(r * 4 + chosen // 2, rows, stage.at[n, r], s_sems.at[0])
        for r in range(8):
            for d in range(4):
                x, c = divmod(d, 2)
                lanes = slice(384 * x, 384 * x + 384)
                top = 2 * NQ * r + NQ * c
                fetch(r * 4 + d, slice(0, NQ), wq.at[top : top + NQ, lanes], w_sems.at[0])
                top = 2 * NP * r + NP * c
                fetch(r * 4 + d, slice(NQ, NQ + NP), wp.at[top : top + NP, lanes], w_sems.at[1])
        wait_all(stage, s_sems.at[0])
        for n in range(image_count):
            for r in range(8):
                up_ref[n, :, 288 * r : 288 * r + 288] = stage[n, r, :, 0:288]
                down_ref[n, :, 96 * r : 96 * r + 96] = stage[n, r, :, 288:384]
        wait_all(wq, w_sems.at[0])
        wait_all(wp, w_sems.at[1])

    return pl.pallas_call(
        kernel,
        out_shape=[
            jax.ShapeDtypeStruct((3 * D, D), BF),
            jax.ShapeDtypeStruct((D, D), BF),
            jax.ShapeDtypeStruct((image_count, RANK, D), BF),
            jax.ShapeDtypeStruct((image_count, RANK, 3 * D), BF),
        ],
        grid_spec=pltpu.PrefetchScalarGridSpec(
            num_scalar_prefetch=2,
            grid=(1,),
            in_specs=any_specs(2),
            out_specs=[
                full_spec((3 * D, D)),
                full_spec((D, D)),
                full_spec((image_count, RANK, D)),
                full_spec((image_count, RANK, 3 * D)),
            ],
            scratch_shapes=[
                pltpu.VMEM((image_count, 8, RANK, 384), BF),
                pltpu.SemaphoreType.DMA((2,)),
                pltpu.SemaphoreType.DMA((1,)),
            ],
        ),
        cost_estimate=cost(1e6, 10e6),
        compiler_params=params(),
        name="assemble",
    )(table, adapter_index, pieces, others)


def second_copies(groups, ranks):
    ne, nc = FF // (groups * ranks), D // ranks
    wide = FF // ranks
    expand, contract = [], []
    for r in range(ranks):
        for d in range(groups):
            b = r * groups + d
            for h in range(2):
                top = d * 2 * ne + h * ne
                expand.append(
                    (
                        (b, slice(0, ne), slice(h * wide, h * wide + wide)),
                        (slice(top, top + ne), slice(r * wide, r * wide + wide)),
                    )
                )
            contract.append(
                ((b, slice(ne, ne + nc)), (slice(nc * r, nc * r + nc), slice(D * d, D * d + D)))
            )
    return expand, contract, ne + nc


def second_adapters(base, groups, ranks):
    per_group = ADAPTERS // groups
    wide = FF // ranks

    def copies(chosen):
        found = []
        for r in range(ranks):
            block = r * groups + chosen // per_group
            own = chosen % per_group
            rows = pl.ds(pl.multiple_of(base + own * RANK, RANK), RANK)
            found.append((0, (block, rows), (r,)))
            rows = slice(base + 2 * RANK, base + 3 * RANK)
            found.append((1, (block, rows, pl.ds(pl.multiple_of(own * wide, 128), wide)), (r,)))
        return found

    return copies


def plain_stage(chosen, ranks):
    images = chosen[0].shape[0]
    lists = dict(zip(FF_KINDS, chosen))
    halves = []
    for kinds in HALVES:
        parts = [lists[k].reshape(images, RANK, ranks, -1).transpose(0, 2, 1, 3) for k in kinds]
        halves.append(jnp.concatenate(parts, 3))
    return [[half[n] for half in halves] for n in range(images)]


def gather_plain(weights, adapters, adapter_index):
    full = []
    for m in weights:
        m = lax.all_gather(m, "dp", axis=0, tiled=True)
        full.append(lax.all_gather(m, "rows", axis=1, tiled=True))
    qkv, proj, expand, contract = full
    chosen = []
    for m in adapters:
        m = lax.all_gather(m, "dp", axis=0, tiled=True)
        m = jnp.take(m, adapter_index[:, 0], axis=0)
        chosen.append(lax.all_gather(m, "rows", axis=2, tiled=True))
    return [qkv.T, proj.T, expand, contract.T], chosen


def rows_sum(packed):
    moved = lax.all_to_all(packed, "rows", split_axis=0, concat_axis=0, tiled=True)
    return jnp.sum(moved.astype(F32), axis=0)


def adapters_sum(sums, widths, adapter_index, groups):
    per_group = ADAPTERS // groups
    local = sums
    hit = (adapter_index[None, :] == jnp.arange(ADAPTERS)[:, None]).astype(F32)
    spread = jnp.sum(hit[:, :, None, None] * local[None], axis=1).astype(BF)
    spread = spread.reshape(groups, per_group, RANK, -1)
    moved = lax.all_to_all(spread, "dp", split_axis=0, concat_axis=0, tiled=True)
    total = jnp.sum(moved.astype(F32), axis=0)
    outs = []
    at = 0
    for wide in widths:
        outs.append(total[:, :, at : at + wide])
        at += wide
    return outs


def per_device(
    images, norm1_gain, norm1_bias, qkv_weight, qkv_bias, height_table, width_table, proj_weight,
    proj_bias, norm2_gain, norm2_bias, expand_weight, expand_bias, contract_weight, contract_bias,
    adapter_index, qkv_down, qkv_up, proj_down, proj_up, expand_down, expand_up, contract_down,
    contract_up, cotangent,
):
    image_count, row_count, side, _ = images.shape
    ranks = lax.axis_size("rows")
    groups = lax.axis_size("dp")
    rank = lax.axis_index("rows")
    plan = make_plan(ranks, row_count, 1)
    packed = packed_form(groups, ranks)
    pieces_at = piece_table() if packed else np.zeros((groups, ranks, 1), np.int32)
    tables = [np.broadcast_to(plan[k][None], (groups,) + plan[k].shape)
              for k in ("rows", "wins", "info")] + [pieces_at]
    ends = np.cumsum([0] + [t.shape[2] for t in tables])
    mine = jnp.asarray(np.concatenate(tables, 2))[lax.axis_index("dp"), rank]
    rows_code, win_code, info, piece_code = [mine[a:b] for a, b in zip(ends[:-1], ends[1:])]
    rows_block = 4 if row_count % 4 == 0 else row_count
    ff_block = row_count
    place = jnp.asarray(place_matrix(side), BF)
    marks_fwd, marks_bwd = [jnp.asarray(m, BF) for m in key_marks()]
    table_fwd, table_bwd = pair_tables(height_table, width_table)
    zero = jnp.zeros((1, PITCH, D), BF)
    row_vector = lambda v: v.reshape(1, -1)
    picked = adapter_index[:, 0]
    flat_images = images.reshape(image_count * row_count, side, D)
    flat_cotangent = cotangent.reshape(image_count * row_count, side, D)

    adapters = (qkv_down, qkv_up, proj_down, proj_up, expand_down, expand_up, contract_down,
                contract_up)
    whole = [((slice(None),), (slice(None),))]
    gain_one, bias_one = row_vector(norm1_gain), row_vector(norm1_bias)
    split = range(image_count)
    if packed:
        second, own, other, extra = pack(qkv_weight, proj_weight, expand_weight,
                                         contract_weight.T, adapters)
        piece = first_piece(own, other, extra)
        gain_one = after(gain_one, piece)
    sent = [first_norm(flat_images, n, row_count, gain_one, bias_one, place, rows_code, plan,
                       rows_block) for n in split]
    if packed:
        ready, pieces, others, line = gather_first(piece, [v[0] for v in sent])
        second = lax.all_gather(after(second, line), ("rows", "dp"), axis=0, tiled=False)
        units = [exchange([after(v, *ready) for v in sent[n]], plan, False) for n in split]
        others = after(others, *units[0])
        qkv_full, proj_full, down_one, up_one = assemble(pieces, others, piece_code, picked,
                                                         image_count)
        expand_copies, contract_copies, base = second_copies(groups, ranks)
        adapter_copies = second_adapters(base, groups, ranks)
        ff_src = [proj_full, second, second]
        adapter_src = [[second, second]] * image_count
    else:
        units = [exchange(sent[n], plan, False) for n in split]
        weights = (qkv_weight, proj_weight, expand_weight, contract_weight)
        full, chosen = gather_plain(weights, adapters, adapter_index)
        expand_copies = contract_copies = whole
        qkv_full = full[0]
        down_one, up_one = chosen[:2]
        ff_src = full[1:]
        everything = (slice(None),)
        adapter_copies = lambda index: [(h, everything, everything) for h in range(2)]
        adapter_src = plain_stage(chosen[2:], ranks)
    vectors = [row_vector(v) for v in (proj_bias, norm2_gain, norm2_bias, expand_bias,
                                       contract_bias)]
    forward = [attention_forward(units[n], zero, qkv_full, row_vector(qkv_bias), down_one, up_one,
                                 n, table_fwd, marks_fwd, win_code, info, plan) for n in split]
    units = [exchange(forward[n][0], plan, True) for n in split]
    ff = []
    for n in split:
        ff.append(feed_forward(units[n], flat_images, flat_cotangent, n, row_count, ff_src, whole,
                               expand_copies, contract_copies, vectors, adapter_src[n], picked,
                               adapter_copies, place, rows_code, plan, ff_block, ranks,
                               [v for f in ff[-1:] for v in (f[1], f[3])]))
    units = [exchange(ff[n][0], plan, False) for n in split]
    backward = []
    for n in split:
        backward.append(attention_backward(units[n], zero, qkv_full, forward[n][1],
                                           row_vector(qkv_bias), down_one, up_one, n, table_bwd,
                                           marks_bwd, win_code, info, plan, ranks, image_count,
                                           [b[1] for b in backward[-1:]]))
    units = [exchange(backward[n][0], plan, True) for n in split]
    early_sums = after(rows_sum(ff[-1][3]), backward[0][0][0]).reshape(image_count, RANK, -1)
    early = adapters_sum(early_sums, [FF_WIDTHS[k] // ranks for k in FF_KINDS], picked, groups)
    gain_one = after(gain_one, early[0])
    back = []
    for n in split:
        back.append(first_norm_back(units[n], flat_images, ff[n][2], n, row_count, gain_one,
                                    place.T, rows_code, plan, rows_block, back[-1:]))
    late_terms = after(backward[-1][1], back[0])
    late_sums = rows_sum(late_terms).reshape(image_count, RANK, -1)
    late = adapters_sum(late_sums, [D // ranks, 3 * D // ranks], picked, groups)
    return (ff[-1][1].reshape(images.shape), back[-1].reshape(images.shape), *late, *early)


def solution(mesh):
    whole = P()
    both = P("dp", "rows")
    adapter = P("dp", None, "rows")
    image = P("dp", "rows", None, None)
    placed = (image, whole, whole, both, whole, whole, whole, both, whole, whole, whole, both,
              whole, both, whole, P("dp", None), *([adapter] * 8), image)
    return jax.shard_map(
        per_device,
        mesh=mesh,
        in_specs=placed,
        out_specs=(image, image, *([adapter] * 8)),
        check_vma=False,
    )
```
